32 devices in a mesh: slab: 4 (over x, core), view: 8 (over z, y).
Axes of the slice: x: 2, y: 2, z: 4, core: 2. Of those that a mesh axis runs over, the one named last changes fastest.
Arguments:
- volume: float32 [64, 4, 4096], P('slab'), may hold values from 0 to 2
- sinogram: float32 [16, 64, 4096], P('view', 'slab'), may hold values from -8 to 81928
- curvature: float32 [64, 4, 4096], P('slab'), may hold values from 0.003 to 3
- angles: int32 [16], P('view'), may hold values from 0 to 1151
- offsets: int32 [16, 4], P('view'), may hold values from 0 to 48, as said below
Outputs:
- updated: float32 [64, 4, 4096], P('slab')
The draws below stay inside these ranges and needn't reach their ends.
Inputs may be any that keep to these rules, and one draw needn't show every extreme that they name: `offsets`: in each view the band of slab k starts within 8 rows of ((k + s) mod the number of slabs) * 16, where s, fixed for the view, is 0 or half the number of slabs.
All inputs are finite; a program needn't handle non-finite values.
Results may differ from the reference program's by a relative error of at most 0.0003.
Values sent between devices are 32-bit elements; how exact they have to be, the bound alone decides.
No kernel may reach another device: no remote copies, remote signals or barrier semaphores. Data moves between devices by JAX's collectives and lax.ppermute only.
A program may use at most 64 MiB of HBM per device.

```python
import math
import jax
import jax.numpy as jnp
from jax import lax

SLAB_SLICES = 16
IMG_ROWS = 4
IMG_COLS = 4096
DET_COLS = 4096
ROTATION_VIEWS = 1152
SLICES = 64
DET_ROWS = 64
VIEWS = 16


def base_volume(key):
    return jax.random.uniform(jax.random.fold_in(key, 203), (SLICES, IMG_ROWS, IMG_COLS), jnp.float32, 0.0, 2.0)


def view_angles(key):
    return jax.random.randint(jax.random.fold_in(key, 201), (VIEWS,), 0, ROTATION_VIEWS, jnp.int32)


def band_offsets(key):
    slab_count = SLICES // SLAB_SLICES
    slab_ids = jnp.arange(slab_count, dtype=jnp.int32)
    home = SLAB_SLICES * slab_ids
    turned = SLAB_SLICES * ((slab_ids + slab_count // 2) % slab_count)
    jitter = jax.random.randint(jax.random.fold_in(key, 202), (VIEWS, slab_count), -(SLAB_SLICES // 2), SLAB_SLICES // 2 + 1, jnp.int32)
    placed = jnp.clip(home[None, :] + jitter, 0, DET_ROWS - SLAB_SLICES)
    return placed.at[0].set(turned).astype(jnp.int32)


def draw_volume(key, part):
    return base_volume(key)


def draw_angles(key, part):
    return view_angles(key)


def draw_offsets(key, part):
    return band_offsets(key)


def draw_sinogram(key, part):
    volume = base_volume(key)
    angles = view_angles(key)
    offsets = band_offsets(key)
    rough = jax.random.uniform(jax.random.fold_in(key, 204), (SLICES, IMG_ROWS * IMG_COLS), jnp.float32, -1.0, 1.0)
    truth = volume.reshape(SLICES, IMG_ROWS * IMG_COLS) * (1.0 + 0.2 * rough)
    depth = jnp.arange(SLICES, dtype=jnp.int32)
    across = jnp.arange(IMG_COLS, dtype=jnp.float32) - 0.5 * IMG_COLS + 0.5
    along = jnp.arange(IMG_ROWS, dtype=jnp.float32) - 0.5 * IMG_ROWS + 0.5

    def one_view(inputs):
        angle_index, offset_row = inputs
        angle_rad = angle_index.astype(jnp.float32) * (2.0 * math.pi / ROTATION_VIEWS)
        coord = 0.7 * (across[None, :] * jnp.cos(angle_rad) + along[:, None] * jnp.sin(angle_rad)) + 0.5 * DET_COLS - 0.5
        coord = coord.reshape(-1)
        lower = jnp.floor(coord)
        bin_index = lower.astype(jnp.int32)
        bin_frac = coord - lower
        summed = jnp.zeros((SLICES, DET_COLS), jnp.float32)
        summed = summed.at[:, bin_index].add(truth * (1.0 - bin_frac))
        summed = summed.at[:, bin_index + 1].add(truth * bin_frac)
        row_of = (offset_row[depth // SLAB_SLICES] + depth % SLAB_SLICES).astype(jnp.int32)
        return jnp.zeros((DET_ROWS, DET_COLS), jnp.float32).at[row_of].add(summed)
    clean = lax.map(one_view, (angles, offsets))
    noise_key = jax.random.fold_in(key, 205)
    noise = 1.5 * jnp.clip(jax.random.normal(noise_key, (VIEWS, DET_ROWS, DET_COLS), jnp.float32), -4.0, 4.0)
    return (clean + noise).astype(jnp.float32)


def draw_curvature(key, part):
    first_key = jax.random.fold_in(key, 0)
    base = jnp.exp(jax.random.uniform(first_key, (SLICES, IMG_ROWS * IMG_COLS), jnp.float32, math.log(0.3), math.log(3.0)))
    depth = jnp.arange(SLICES, dtype=jnp.float32) / SLICES
    place = jnp.arange(IMG_ROWS * IMG_COLS, dtype=jnp.float32) / (IMG_ROWS * IMG_COLS)
    ratio = 3.0
    trend = jnp.power(ratio, -depth)[:, None] * jnp.power(ratio, -place)[None, :]
    return (base * trend).reshape(SLICES, IMG_ROWS, IMG_COLS).astype(jnp.float32)


def setup_inputs(seed: int = 0) -> dict:
    streams_of = jax.random.split(jax.random.key(seed), 6)
    return {
        "volume": draw_volume(jax.random.fold_in(streams_of[5], 71), 0),
        "sinogram": draw_sinogram(jax.random.fold_in(streams_of[5], 71), 0),
        "curvature": draw_curvature(jax.random.fold_in(streams_of[5], 71), 0),
        "angles": draw_angles(jax.random.fold_in(streams_of[5], 71), 0),
        "offsets": draw_offsets(jax.random.fold_in(streams_of[5], 71), 0),
    }


huber_delta = 0.5
tv_weight = 4.0
step_limit = 1.0
detector_scale = 0.7
epsilon = 1e-06

def geometry(angle_index, rows_n, cols_n, bins_n):
    angle_rad = angle_index.astype(jnp.float32) * (2.0 * math.pi / ROTATION_VIEWS)
    across = jnp.arange(cols_n, dtype=jnp.float32) - 0.5 * cols_n + 0.5
    along = jnp.arange(rows_n, dtype=jnp.float32) - 0.5 * rows_n + 0.5
    coord = detector_scale * (across[None, :] * jnp.cos(angle_rad) + along[:, None] * jnp.sin(angle_rad)) + 0.5 * bins_n - 0.5
    coord = coord.reshape(-1)
    lower = jnp.floor(coord)
    return (lower.astype(jnp.int32), coord - lower)

def project(slices_flat, bin_index, bin_frac, bins_n):
    summed = jnp.zeros((slices_flat.shape[0], bins_n), jnp.float32)
    summed = summed.at[:, bin_index].add(slices_flat * (1.0 - bin_frac))
    return summed.at[:, bin_index + 1].add(slices_flat * bin_frac)

def backproject(det_rows, bin_index, bin_frac):
    return det_rows[:, bin_index] * (1.0 - bin_frac) + det_rows[:, bin_index + 1] * bin_frac

def slope(diff):
    return jnp.clip(diff / huber_delta, -1.0, 1.0)

def tv_padded(padded):
    centre = padded[1:-1, 1:-1, 1:-1]
    result = slope(centre - padded[:-2, 1:-1, 1:-1]) - slope(padded[2:, 1:-1, 1:-1] - centre)
    result = result + slope(centre - padded[1:-1, :-2, 1:-1]) - slope(padded[1:-1, 2:, 1:-1] - centre)
    result = result + slope(centre - padded[1:-1, 1:-1, :-2]) - slope(padded[1:-1, 1:-1, 2:] - centre)
    return result

def reference(volume, sinogram, curvature, angles, offsets):
    slices_n, rows_n, cols_n = volume.shape
    bins_n = sinogram.shape[2]
    flattened = volume.reshape(slices_n, rows_n * cols_n)
    depth = jnp.arange(slices_n, dtype=jnp.int32)

    def add_view(carry, inputs):
        angle_index, offset_row, measured = inputs
        bin_index, bin_frac = geometry(angle_index, rows_n, cols_n, bins_n)
        projected = project(flattened, bin_index, bin_frac, bins_n)
        row_of = (offset_row[depth // SLAB_SLICES] + depth % SLAB_SLICES).astype(jnp.int32)
        detector = jnp.zeros((DET_ROWS, bins_n), jnp.float32).at[row_of].add(projected)
        residual = detector - measured
        return (carry + backproject(residual[row_of], bin_index, bin_frac), None)
    start_grad = jnp.zeros((slices_n, rows_n * cols_n), jnp.float32)
    data_grad, _ = lax.scan(add_view, start_grad, (angles, offsets, sinogram))
    tv_grad = tv_padded(jnp.pad(volume, 1)).reshape(slices_n, rows_n * cols_n)
    direction = (data_grad + tv_weight * tv_grad) / curvature.reshape(slices_n, rows_n * cols_n)
    rms_value = jnp.sqrt(jnp.mean(direction * direction) + epsilon)
    factor = jnp.minimum(1.0, step_limit / rms_value)
    return (flattened - factor * direction).reshape(slices_n, rows_n, cols_n)
```

```python
import math
import jax
import jax.numpy as jnp
from jax import lax
from jax.experimental import pallas as pl
from jax.experimental.pallas import tpu as pltpu
from jax.sharding import PartitionSpec as P

ROTATION_VIEWS = 1152


huber_delta = 0.5
tv_weight = 4.0
step_limit = 1.0
epsilon = 1e-06
scale = 0.7
LANES = 128
GROUP = 8


def coordinate(across, along, cos, sin, bins_n):
    return scale * (across * cos + along * sin) + 0.5 * bins_n - 0.5


def window_of(start, cos, sin, along, cols_n, bins_n, base):
    first = coordinate(start - 0.5 * cols_n + 0.5, along, cos, sin, bins_n)
    last = coordinate(start + (LANES - 1.0) - 0.5 * cols_n + 0.5, along, cos, sin, bins_n)
    return jnp.minimum(first, last).astype(jnp.int32) - (base + 1)


def project_kernel(cols_n, rows_n, bins_n, base, blocks_n, views_n, trig_ref, vol_ref, out_ref, rows_ref, acc_ref, sem):
    copies = [pltpu.make_async_copy(vol_ref.at[:, i, :], rows_ref.at[i], sem.at[i]) for i in range(rows_n)]
    for c in copies:
        c.start()
    acc_ref[...] = jnp.zeros_like(acc_ref)
    lane8 = lax.broadcasted_iota(jnp.int32, (8, LANES), 1)
    lane = lax.broadcasted_iota(jnp.int32, (16, LANES), 1)
    sub = lax.broadcasted_iota(jnp.int32, (LANES, LANES), 0).astype(jnp.float32).astype(jnp.bfloat16)
    zero = jnp.zeros((LANES, LANES), jnp.bfloat16)

    def tall(x):
        return jnp.concatenate([jnp.concatenate([x, x], 0).astype(jnp.bfloat16)] * (LANES // 16), 0)

    for row in range(rows_n):
        copies[row].wait()
        along = row - 0.5 * rows_n + 0.5

        def step(g, _):
            outs = []
            for u in range(GROUP):
                block = g * GROUP + u
                start = (block * LANES).astype(jnp.float32)
                vals = rows_ref[row, :, pl.ds(pl.multiple_of(block * LANES, LANES), LANES)]
                high = vals.astype(jnp.bfloat16)
                rest = vals - high.astype(jnp.float32)
                mid = rest.astype(jnp.bfloat16)
                low = (rest - mid.astype(jnp.float32)).astype(jnp.bfloat16)
                terms = jnp.concatenate([high, mid, low], 0)
                mats = []
                wins = []
                for v in range(views_n):
                    cos = trig_ref[v]
                    sin = trig_ref[views_n + v]
                    across = (lane8 + block * LANES).astype(jnp.float32) - 0.5 * cols_n + 0.5
                    coord = coordinate(across, along, cos, sin, bins_n)
                    lower = jnp.floor(coord)
                    frac = coord - lower
                    rel = lower - float(base)
                    bm = rel - LANES * jnp.floor(rel * (1.0 / LANES))
                    bn = jnp.where(bm == LANES - 1.0, 0.0, bm + 1.0)
                    fh = jnp.floor(frac * 128.0) * (1.0 / 128.0)
                    fl = frac - fh
                    here = sub == tall(bm)
                    next_ = sub == tall(bn)
                    wh = jnp.where(here, tall(1.0 - fh), jnp.where(next_, tall(fh), zero))
                    wl = jnp.where(here, tall(-fl), jnp.where(next_, tall(fl), zero))
                    mats.append(jnp.concatenate([wh, wl], 1))
                    wins.append(window_of(start, cos, sin, along, cols_n, bins_n, base))
                weights = jnp.concatenate(mats, 0)
                both = jnp.concatenate([terms, terms], 1)
                prod = lax.dot_general(both, weights, (((1,), (1,)), ((), ())), preferred_element_type=jnp.float32)
                outs.append((prod[0:16] + prod[16:32] + prod[32:48], wins))
            for summed, wins in outs:
                for v in range(views_n):
                    first = wins[v]
                    k = first >> 7
                    own = lane >= (first & (LANES - 1))
                    part = summed[:, v * LANES:(v + 1) * LANES]
                    acc_ref[v, k] += jnp.where(own, part, 0.0)
                    acc_ref[v, k + 1] += jnp.where(own, 0.0, part)
            return 0

        lax.fori_loop(0, cols_n // LANES // GROUP, step, 0)
    out_ref[...] = acc_ref[:, :blocks_n]


def project(trig, volume, bins_n, base, blocks_n, views_n):
    slices_n, rows_n, cols_n = volume.shape
    body = lambda *refs: project_kernel(cols_n, rows_n, bins_n, base, blocks_n, views_n, *refs)
    return pl.pallas_call(
        body,
        out_shape=jax.ShapeDtypeStruct((views_n, blocks_n, slices_n, LANES), jnp.float32),
        in_specs=[pl.BlockSpec(memory_space=pltpu.SMEM), pl.BlockSpec(memory_space=pl.ANY)],
        out_specs=pl.BlockSpec(memory_space=pltpu.VMEM),
        scratch_shapes=[
            pltpu.VMEM((rows_n, slices_n, cols_n), jnp.float32),
            pltpu.VMEM((views_n, blocks_n + 1, slices_n, LANES), jnp.float32),
            pltpu.SemaphoreType.DMA((rows_n,)),
        ],
        name="project",
    )(trig, volume)


def backproject_kernel(cols_n, rows_n, bins_n, base, views_n, width, per_n, trig_ref, starts_ref, res_ref, out_ref):
    lane16 = lax.broadcasted_iota(jnp.int32, (16, LANES), 1)
    pixel0 = starts_ref[views_n]

    def row_step(row, _):
        along = row.astype(jnp.float32) - 0.5 * rows_n + 0.5

        def step(u, _):
            column = pixel0 + u * LANES
            start = column.astype(jnp.float32)
            across = (lane16 + column).astype(jnp.float32) - 0.5 * cols_n + 0.5
            total = jnp.zeros((16, LANES), jnp.float32)
            for v in range(views_n):
                cos = trig_ref[v]
                sin = trig_ref[views_n + v]
                coord = coordinate(across, along, cos, sin, bins_n)
                lower = jnp.floor(coord)
                frac = coord - lower
                offset = starts_ref[v]
                rel = lower.astype(jnp.int32) - (base + offset)
                here = rel & (LANES - 1)
                next_ = (rel + 1) & (LANES - 1)
                first = window_of(start, cos, sin, along, cols_n, bins_n, base) - offset
                k = first >> 7
                left = res_ref[v, k]
                right = res_ref[v, jnp.minimum(k + 1, width - 1)]
                band = jnp.where(lane16 >= (first & (LANES - 1)), left, right)
                a = jnp.take_along_axis(band, here, axis=1, mode="promise_in_bounds")
                b = jnp.take_along_axis(band, next_, axis=1, mode="promise_in_bounds")
                total = total + (a * (1.0 - frac) + b * frac)
            out_ref[row, :, pl.ds(pl.multiple_of(u * LANES, LANES), LANES)] = total
            return 0

        lax.fori_loop(0, per_n // LANES, step, 0)
        return 0

    lax.fori_loop(0, rows_n, row_step, 0)


def backproject(trig, starts, res, rows_n, cols_n, bins_n, base, per_n):
    views_n, width, slices_n, _ = res.shape
    body = lambda *refs: backproject_kernel(cols_n, rows_n, bins_n, base, views_n, width, per_n, *refs)
    return pl.pallas_call(
        body,
        out_shape=jax.ShapeDtypeStruct((rows_n, slices_n, per_n), jnp.float32),
        in_specs=[pl.BlockSpec(memory_space=pltpu.SMEM), pl.BlockSpec(memory_space=pltpu.SMEM), pl.BlockSpec(memory_space=pltpu.VMEM)],
        out_specs=pl.BlockSpec(memory_space=pltpu.VMEM),
        name="backproject",
    )(trig, starts, res)


def padded_2(cells, sides, width):
    for axis, dim in sides:
        count = lax.axis_size(axis)
        ends = count - 1
        head = lax.slice_in_dim(cells, 0, width, axis=dim)
        tail = lax.slice_in_dim(cells, cells.shape[dim] - width, cells.shape[dim], axis=dim)
        cells = jnp.concatenate(
            [
                lax.ppermute(tail, axis, [(i, (i + 1) % count) for i in range(ends)]),
                cells,
                lax.ppermute(head, axis, [((i + 1) % count, i) for i in range(ends)]),
            ],
            axis=dim,
        )
    return cells


def slope(diff):
    return jnp.clip(diff / huber_delta, -1.0, 1.0)


def tv_padded(padded):
    centre = padded[1:-1, 1:-1, 1:-1]
    result = slope(centre - padded[:-2, 1:-1, 1:-1]) - slope(padded[2:, 1:-1, 1:-1] - centre)
    result = (
        result + slope(centre - padded[1:-1, :-2, 1:-1]) - slope(padded[1:-1, 2:, 1:-1] - centre)
    )
    result = (
        result + slope(centre - padded[1:-1, 1:-1, :-2]) - slope(padded[1:-1, 1:-1, 2:] - centre)
    )
    return result


def extent(rows_n, cols_n, bins_n):
    reach = scale * math.hypot(0.5 * (cols_n - 1), 0.5 * (rows_n - 1))
    centre = 0.5 * bins_n - 0.5
    base = (int(centre - reach) - 3) // 8 * 8
    blocks = -(-(int(centre + reach) + 3 - base) // LANES)
    return base, blocks


def local(volume, sinogram, curvature, angles, offsets):
    slices_n, rows_n, cols_n = volume.shape
    views_n = angles.shape[0]
    bins_n = sinogram.shape[2]
    base, blocks = extent(rows_n, cols_n, bins_n)
    pixels_n = rows_n * cols_n
    slab_count = lax.axis_size("slab")
    all_rows = sinogram.shape[1] * slab_count
    slab_pos = lax.axis_index("slab")
    angle_rad = angles.astype(jnp.float32) * (2.0 * math.pi / ROTATION_VIEWS)
    trig = jnp.concatenate([jnp.cos(angle_rad), jnp.sin(angle_rad)])
    proj = project(trig, volume, bins_n, base, blocks, views_n)
    stacked = []
    bands = []
    for v in range(views_n):
        start = lax.dynamic_index_in_dim(offsets[v], slab_pos, 0, keepdims=False)
        flat = proj[v].transpose(1, 0, 2).reshape(slices_n, blocks * LANES)
        stacked.append(
            lax.dynamic_update_slice(
                jnp.zeros((all_rows, blocks * LANES), jnp.float32), flat, (start, jnp.int32(0))
            )
        )
        bands.append(start)
    own = lax.psum_scatter(jnp.stack(stacked), "slab", scatter_dimension=1, tiled=True)
    measured = sinogram[:, :, base : base + blocks * LANES]
    residual = lax.all_gather(own - measured, "slab", axis=1, tiled=True)
    windows = jnp.stack(
        [
            lax.dynamic_slice(
                residual[v], (bands[v], jnp.int32(0)), (slices_n, blocks * LANES)
            )
            .reshape(slices_n, blocks, LANES)
            .transpose(1, 0, 2)
            for v in range(views_n)
        ]
    )
    starts = jnp.zeros((views_n + 1,), jnp.int32)
    data_local = backproject(trig, starts, windows, rows_n, cols_n, bins_n, base, cols_n)
    extended = padded_2(volume, (("slab", 0),), 1)
    padded = jnp.pad(extended, ((0, 0), (1, 1), (1, 1)))
    tv_grad = tv_padded(padded)
    data_grad = lax.psum(data_local, "view").transpose(1, 0, 2)
    direction = (data_grad + tv_weight * tv_grad) / curvature
    squares = lax.psum(jnp.sum(direction * direction), "slab")
    voxel_count = slices_n * slab_count * pixels_n
    factor = jnp.minimum(1.0, step_limit / jnp.sqrt(squares / voxel_count + epsilon))
    return volume - factor * direction


def solution(mesh):
    in_specs = (
        P("slab", None, None),
        P("view", "slab", None),
        P("slab", None, None),
        P("view"),
        P("view", None),
    )
    out_specs = P("slab", None, None)
    return jax.shard_map(local, mesh=mesh, in_specs=in_specs, out_specs=out_specs, check_vma=False)
```

```python
import math
import jax
import jax.numpy as jnp
from jax import lax
from jax.experimental import pallas as pl
from jax.experimental.pallas import tpu as pltpu
from jax.sharding import PartitionSpec as P

ROTATION_VIEWS = 1152


huber_delta = 0.5
tv_weight = 4.0
step_limit = 1.0
epsilon = 1e-06
scale = 0.7
LANES = 128
GROUP = 8


def coordinate(across, along, cos, sin, bins_n):
    return scale * (across * cos + along * sin) + 0.5 * bins_n - 0.5


def window_of(start, cos, sin, along, cols_n, bins_n, base):
    first = coordinate(start - 0.5 * cols_n + 0.5, along, cos, sin, bins_n)
    last = coordinate(start + (LANES - 1.0) - 0.5 * cols_n + 0.5, along, cos, sin, bins_n)
    return jnp.minimum(first, last).astype(jnp.int32) - (base + 1)


def project_kernel(cols_n, rows_n, bins_n, base, blocks_n, views_n, trig_ref, vol_ref, out_ref, rows_ref, acc_ref, sem):
    copies = [pltpu.make_async_copy(vol_ref.at[:, i, :], rows_ref.at[i], sem.at[i]) for i in range(rows_n)]
    for c in copies:
        c.start()
    acc_ref[...] = jnp.zeros_like(acc_ref)
    lane8 = lax.broadcasted_iota(jnp.int32, (8, LANES), 1)
    lane = lax.broadcasted_iota(jnp.int32, (16, LANES), 1)
    sub = lax.broadcasted_iota(jnp.int32, (LANES, LANES), 0).astype(jnp.float32).astype(jnp.bfloat16)
    zero = jnp.zeros((LANES, LANES), jnp.bfloat16)

    def tall(x):
        return jnp.concatenate([jnp.concatenate([x, x], 0).astype(jnp.bfloat16)] * (LANES // 16), 0)

    for row in range(rows_n):
        copies[row].wait()
        along = row - 0.5 * rows_n + 0.5

        def step(g, _):
            outs = []
            for u in range(GROUP):
                block = g * GROUP + u
                start = (block * LANES).astype(jnp.float32)
                vals = rows_ref[row, :, pl.ds(pl.multiple_of(block * LANES, LANES), LANES)]
                high = vals.astype(jnp.bfloat16)
                rest = vals - high.astype(jnp.float32)
                mid = rest.astype(jnp.bfloat16)
                low = (rest - mid.astype(jnp.float32)).astype(jnp.bfloat16)
                terms = jnp.concatenate([high, mid, low], 0)
                mats = []
                wins = []
                for v in range(views_n):
                    cos = trig_ref[v]
                    sin = trig_ref[views_n + v]
                    across = (lane8 + block * LANES).astype(jnp.float32) - 0.5 * cols_n + 0.5
                    coord = coordinate(across, along, cos, sin, bins_n)
                    lower = jnp.floor(coord)
                    frac = coord - lower
                    rel = lower - float(base)
                    bm = rel - LANES * jnp.floor(rel * (1.0 / LANES))
                    bn = jnp.where(bm == LANES - 1.0, 0.0, bm + 1.0)
                    fh = jnp.floor(frac * 128.0) * (1.0 / 128.0)
                    fl = frac - fh
                    here = sub == tall(bm)
                    next_ = sub == tall(bn)
                    wh = jnp.where(here, tall(1.0 - fh), jnp.where(next_, tall(fh), zero))
                    wl = jnp.where(here, tall(-fl), jnp.where(next_, tall(fl), zero))
                    mats.append(jnp.concatenate([wh, wl], 1))
                    wins.append(window_of(start, cos, sin, along, cols_n, bins_n, base))
                weights = jnp.concatenate(mats, 0)
                both = jnp.concatenate([terms, terms], 1)
                prod = lax.dot_general(both, weights, (((1,), (1,)), ((), ())), preferred_element_type=jnp.float32)
                outs.append((prod[0:16] + prod[16:32] + prod[32:48], wins))
            for summed, wins in outs:
                for v in range(views_n):
                    first = wins[v]
                    k = first >> 7
                    own = lane >= (first & (LANES - 1))
                    part = summed[:, v * LANES:(v + 1) * LANES]
                    acc_ref[v, k] += jnp.where(own, part, 0.0)
                    acc_ref[v, k + 1] += jnp.where(own, 0.0, part)
            return 0

        lax.fori_loop(0, cols_n // LANES // GROUP, step, 0)
    out_ref[...] = acc_ref[:, :blocks_n]


def project(trig, volume, bins_n, base, blocks_n, views_n):
    slices_n, rows_n, cols_n = volume.shape
    body = lambda *refs: project_kernel(cols_n, rows_n, bins_n, base, blocks_n, views_n, *refs)
    return pl.pallas_call(
        body,
        out_shape=jax.ShapeDtypeStruct((views_n, blocks_n, slices_n, LANES), jnp.float32),
        in_specs=[pl.BlockSpec(memory_space=pltpu.SMEM), pl.BlockSpec(memory_space=pl.ANY)],
        out_specs=pl.BlockSpec(memory_space=pltpu.VMEM),
        scratch_shapes=[
            pltpu.VMEM((rows_n, slices_n, cols_n), jnp.float32),
            pltpu.VMEM((views_n, blocks_n + 1, slices_n, LANES), jnp.float32),
            pltpu.SemaphoreType.DMA((rows_n,)),
        ],
        name="project",
    )(trig, volume)


def backproject_kernel(cols_n, rows_n, bins_n, base, views_n, width, per_n, trig_ref, starts_ref, res_ref, out_ref):
    lane16 = lax.broadcasted_iota(jnp.int32, (16, LANES), 1)
    pixel0 = starts_ref[views_n]

    def row_step(row, _):
        along = row.astype(jnp.float32) - 0.5 * rows_n + 0.5

        def step(u, _):
            column = pixel0 + u * LANES
            start = column.astype(jnp.float32)
            across = (lane16 + column).astype(jnp.float32) - 0.5 * cols_n + 0.5
            total = jnp.zeros((16, LANES), jnp.float32)
            for v in range(views_n):
                cos = trig_ref[v]
                sin = trig_ref[views_n + v]
                coord = coordinate(across, along, cos, sin, bins_n)
                lower = jnp.floor(coord)
                frac = coord - lower
                offset = starts_ref[v]
                rel = lower.astype(jnp.int32) - (base + offset)
                here = rel & (LANES - 1)
                next_ = (rel + 1) & (LANES - 1)
                first = window_of(start, cos, sin, along, cols_n, bins_n, base) - offset
                k = first >> 7
                left = res_ref[v, k]
                right = res_ref[v, jnp.minimum(k + 1, width - 1)]
                band = jnp.where(lane16 >= (first & (LANES - 1)), left, right)
                a = jnp.take_along_axis(band, here, axis=1, mode="promise_in_bounds")
                b = jnp.take_along_axis(band, next_, axis=1, mode="promise_in_bounds")
                total = total + (a * (1.0 - frac) + b * frac)
            out_ref[row, :, pl.ds(pl.multiple_of(u * LANES, LANES), LANES)] = total
            return 0

        lax.fori_loop(0, per_n // LANES, step, 0)
        return 0

    lax.fori_loop(0, rows_n, row_step, 0)


def backproject(trig, starts, res, rows_n, cols_n, bins_n, base, per_n):
    views_n, width, slices_n, _ = res.shape
    body = lambda *refs: backproject_kernel(cols_n, rows_n, bins_n, base, views_n, width, per_n, *refs)
    return pl.pallas_call(
        body,
        out_shape=jax.ShapeDtypeStruct((rows_n, slices_n, per_n), jnp.float32),
        in_specs=[pl.BlockSpec(memory_space=pltpu.SMEM), pl.BlockSpec(memory_space=pltpu.SMEM), pl.BlockSpec(memory_space=pltpu.VMEM)],
        out_specs=pl.BlockSpec(memory_space=pltpu.VMEM),
        name="backproject",
    )(trig, starts, res)


def padded_2(cells, sides, width):
    for axis, dim in sides:
        count = lax.axis_size(axis)
        ends = count - 1
        head = lax.slice_in_dim(cells, 0, width, axis=dim)
        tail = lax.slice_in_dim(cells, cells.shape[dim] - width, cells.shape[dim], axis=dim)
        cells = jnp.concatenate(
            [
                lax.ppermute(tail, axis, [(i, (i + 1) % count) for i in range(ends)]),
                cells,
                lax.ppermute(head, axis, [((i + 1) % count, i) for i in range(ends)]),
            ],
            axis=dim,
        )
    return cells


def slope(diff):
    return jnp.clip(diff / huber_delta, -1.0, 1.0)


def tv_padded(padded):
    centre = padded[1:-1, 1:-1, 1:-1]
    result = slope(centre - padded[:-2, 1:-1, 1:-1]) - slope(padded[2:, 1:-1, 1:-1] - centre)
    result = (
        result + slope(centre - padded[1:-1, :-2, 1:-1]) - slope(padded[1:-1, 2:, 1:-1] - centre)
    )
    result = (
        result + slope(centre - padded[1:-1, 1:-1, :-2]) - slope(padded[1:-1, 1:-1, 2:] - centre)
    )
    return result


def extent(rows_n, cols_n, bins_n):
    reach = scale * math.hypot(0.5 * (cols_n - 1), 0.5 * (rows_n - 1))
    centre = 0.5 * bins_n - 0.5
    base = (int(centre - reach) - 3) // 8 * 8
    blocks = -(-(int(centre + reach) + 3 - base) // LANES)
    return base, blocks


def local_any(volume, sinogram, curvature, angles, offsets):
    slices_n, rows_n, cols_n = volume.shape
    views_n = angles.shape[0]
    bins_n = sinogram.shape[2]
    base, blocks = extent(rows_n, cols_n, bins_n)
    pixels_n = rows_n * cols_n
    slab_count = lax.axis_size("slab")
    all_rows = sinogram.shape[1] * slab_count
    slab_pos = lax.axis_index("slab")
    angle_rad = angles.astype(jnp.float32) * (2.0 * math.pi / ROTATION_VIEWS)
    trig = jnp.concatenate([jnp.cos(angle_rad), jnp.sin(angle_rad)])
    proj = project(trig, volume, bins_n, base, blocks, views_n)
    stacked = []
    bands = []
    for v in range(views_n):
        start = lax.dynamic_index_in_dim(offsets[v], slab_pos, 0, keepdims=False)
        flat = proj[v].transpose(1, 0, 2).reshape(slices_n, blocks * LANES)
        stacked.append(
            lax.dynamic_update_slice(
                jnp.zeros((all_rows, blocks * LANES), jnp.float32), flat, (start, jnp.int32(0))
            )
        )
        bands.append(start)
    own = lax.psum_scatter(jnp.stack(stacked), "slab", scatter_dimension=1, tiled=True)
    measured = sinogram[:, :, base : base + blocks * LANES]
    residual = lax.all_gather(own - measured, "slab", axis=1, tiled=True)
    windows = jnp.stack(
        [
            lax.dynamic_slice(
                residual[v], (bands[v], jnp.int32(0)), (slices_n, blocks * LANES)
            )
            .reshape(slices_n, blocks, LANES)
            .transpose(1, 0, 2)
            for v in range(views_n)
        ]
    )
    starts = jnp.zeros((views_n + 1,), jnp.int32)
    data_local = backproject(trig, starts, windows, rows_n, cols_n, bins_n, base, cols_n)
    extended = padded_2(volume, (("slab", 0),), 1)
    padded = jnp.pad(extended, ((0, 0), (1, 1), (1, 1)))
    tv_grad = tv_padded(padded)
    data_grad = lax.psum(data_local, "view").transpose(1, 0, 2)
    direction = (data_grad + tv_weight * tv_grad) / curvature
    squares = lax.psum(jnp.sum(direction * direction), "slab")
    voxel_count = slices_n * slab_count * pixels_n
    factor = jnp.minimum(1.0, step_limit / jnp.sqrt(squares / voxel_count + epsilon))
    return volume - factor * direction


WINDOW = 3
COS_LANE = LANES - 2
SIN_LANE = LANES - 1


def window_start(part, per_n, cos, sin, rows_n, cols_n, bins_n, base, blocks):
    low = None
    for row in (0, rows_n - 1):
        along = row - 0.5 * rows_n + 0.5
        for edge in (0.0, per_n - 1.0):
            across = (part * per_n).astype(jnp.float32) + edge - 0.5 * cols_n + 0.5
            t = coordinate(across, along, cos, sin, bins_n)
            low = t if low is None else jnp.minimum(low, t)
    first = low.astype(jnp.int32) - (base + 1)
    return jnp.clip(first, 0, (blocks - WINDOW) * LANES)


def residual_kernel(dims, parts_n, ints_ref, trig_ref, proj_ref, near_ref, far_c_ref, far_o_ref, own_ref, pair_ref, cross_c_ref, cross_o_ref, *rest):
    rows_n, cols_n, bins_n, base, blocks = dims
    outs = rest[:parts_n]
    near_pad, far_pad, sino, res = rest[parts_n:]
    views_n, _, band, _ = proj_ref.shape
    slab, core, part = ints_ref[0], ints_ref[1], ints_ref[2]
    for pad in (near_pad, far_pad):
        pad[:, :, 0:band] = jnp.zeros((views_n, blocks, band, LANES), jnp.float32)
        pad[:, :, 2 * band:] = jnp.zeros((views_n, blocks, band, LANES), jnp.float32)
    near_pad[:, :, band:2 * band] = near_ref[...]
    far_pad[core, :, band:2 * band] = far_c_ref[...]
    far_pad[1 - core, :, band:2 * band] = far_o_ref[...]

    def rows_of(k):
        return pl.ds(pl.multiple_of(k * band, band), band)

    sino[:, :, rows_of(slab)] = own_ref[...]
    sino[:, :, rows_of(slab ^ 1)] = pair_ref[...]
    sino[core, :, rows_of(slab ^ 2)] = cross_c_ref[0]
    sino[core, :, rows_of(slab ^ 3)] = cross_c_ref[1]
    sino[1 - core, :, rows_of(slab ^ 3)] = cross_o_ref[0]
    sino[1 - core, :, rows_of(slab ^ 2)] = cross_o_ref[1]
    for v in range(views_n):
        start, near, far = ints_ref[3 + 3 * v], ints_ref[4 + 3 * v], ints_ref[5 + 3 * v]
        res[v, 0:blocks] = (
            (proj_ref[v] + near_pad[v, :, pl.ds(near, band), :])
            + far_pad[v, :, pl.ds(far, band), :]
        ) - sino[v, :, pl.ds(start, band), :]
        res[v, blocks] = jnp.zeros((band, LANES), jnp.float32)
    lane = lax.broadcasted_iota(jnp.int32, (band, LANES), 1)
    per_n = cols_n // parts_n
    for r in range(parts_n):
        for v in range(views_n):
            cos, sin = trig_ref[v], trig_ref[views_n + v]
            first = window_start(part ^ r, per_n, cos, sin, rows_n, cols_n, bins_n, base, blocks)
            k = first >> 7
            shift = first & (LANES - 1)
            turned = [pltpu.roll(res[v, k + m], (LANES - shift) & (LANES - 1), 1) for m in range(WINDOW + 1)]
            for m in range(WINDOW):
                value = jnp.where(lane < LANES - shift, turned[m], turned[m + 1])
                if m == WINDOW - 1:
                    value = jnp.where(lane == COS_LANE, cos, jnp.where(lane == SIN_LANE, sin, value))
                outs[r][v, m] = value


def residual_windows(dims, parts_n, ints, trig, arrays):
    views_n, blocks, band, _ = arrays[0].shape
    body = lambda *refs: residual_kernel(dims, parts_n, *refs)
    vmem = pl.BlockSpec(memory_space=pltpu.VMEM)
    smem = pl.BlockSpec(memory_space=pltpu.SMEM)
    return pl.pallas_call(
        body,
        out_shape=[jax.ShapeDtypeStruct((views_n, WINDOW, band, LANES), jnp.float32)] * parts_n,
        in_specs=[smem, smem] + [vmem] * len(arrays),
        out_specs=[vmem] * parts_n,
        scratch_shapes=[
            pltpu.VMEM((views_n, blocks, 3 * band, LANES), jnp.float32),
            pltpu.VMEM((views_n, blocks, 3 * band, LANES), jnp.float32),
            pltpu.VMEM((views_n, blocks, 4 * band, LANES), jnp.float32),
            pltpu.VMEM((views_n, blocks + 1, band, LANES), jnp.float32),
        ],
        name="residual_windows",
    )(ints, trig, *arrays)


def gather_kernel(dims, parts_n, views_n, ints_ref, *rest):
    rows_n, cols_n, bins_n, base, blocks = dims
    pieces = rest[:parts_n]
    out_ref, trig_ref, starts_ref = rest[parts_n:]
    per_n = cols_n // parts_n
    part = ints_ref[2]
    lane8 = lax.broadcasted_iota(jnp.int32, (8, LANES), 1)
    lane = lax.broadcasted_iota(jnp.int32, (16, LANES), 1)
    total_n = parts_n * views_n
    for n in range(total_n):
        tagged = pieces[n // views_n][n % views_n, WINDOW - 1, 0:8, :]
        cos = jnp.max(jnp.where(lane8 == COS_LANE, tagged, -2.0))
        sin = jnp.max(jnp.where(lane8 == SIN_LANE, tagged, -2.0))
        trig_ref[n] = cos
        trig_ref[total_n + n] = sin
        starts_ref[n] = window_start(part, per_n, cos, sin, rows_n, cols_n, bins_n, base, blocks)

    def step(index, _):
        row = index // (per_n // LANES)
        u = index - row * (per_n // LANES)
        along = row.astype(jnp.float32) - 0.5 * rows_n + 0.5
        column = part * per_n + u * LANES
        start = column.astype(jnp.float32)
        across = (lane + column).astype(jnp.float32) - 0.5 * cols_n + 0.5
        total = jnp.zeros((16, LANES), jnp.float32)
        for n in range(total_n):
            cos = trig_ref[n]
            sin = trig_ref[total_n + n]
            offset = starts_ref[n]
            coord = coordinate(across, along, cos, sin, bins_n)
            lower = jnp.floor(coord)
            frac = coord - lower
            rel = lower.astype(jnp.int32) - (base + offset)
            here = rel & (LANES - 1)
            next_ = (rel + 1) & (LANES - 1)
            first = jnp.maximum(window_of(start, cos, sin, along, cols_n, bins_n, base) - offset, 0)
            k = jnp.minimum(first >> 7, WINDOW - 1)
            windows = pieces[n // views_n]
            left = windows[n % views_n, k]
            right = windows[n % views_n, jnp.minimum(k + 1, WINDOW - 1)]
            held = jnp.where(lane >= (first & (LANES - 1)), left, right)
            a = jnp.take_along_axis(held, here, axis=1, mode="promise_in_bounds")
            b = jnp.take_along_axis(held, next_, axis=1, mode="promise_in_bounds")
            total = total + (a * (1.0 - frac) + b * frac)
        out_ref[row, :, pl.ds(pl.multiple_of(u * LANES, LANES), LANES)] = total
        return 0

    lax.fori_loop(0, rows_n * (per_n // LANES), step, 0)


def gather_views(dims, parts_n, ints, pieces):
    views_n, _, slices_n, _ = pieces[0].shape
    rows_n, cols_n = dims[:2]
    body = lambda *refs: gather_kernel(dims, parts_n, views_n, *refs)
    vmem = pl.BlockSpec(memory_space=pltpu.VMEM)
    return pl.pallas_call(
        body,
        out_shape=jax.ShapeDtypeStruct((rows_n, slices_n, cols_n // parts_n), jnp.float32),
        in_specs=[pl.BlockSpec(memory_space=pltpu.SMEM)] + [vmem] * parts_n,
        out_specs=vmem,
        scratch_shapes=[
            pltpu.SMEM((2 * parts_n * views_n,), jnp.float32),
            pltpu.SMEM((parts_n * views_n,), jnp.int32),
        ],
        name="gather_views",
    )(ints, *pieces)


def finish_kernel(parts_n, order_ref, factor_ref, vol_ref, *rest):
    pieces = rest[:parts_n]
    out_ref = rest[parts_n]
    factor = factor_ref[0]
    per_n = pieces[0].shape[2]
    for r in range(parts_n):
        cols = pl.ds(pl.multiple_of(order_ref[r] * per_n, per_n), per_n)
        out_ref[:, :, cols] = vol_ref[:, :, cols] - factor * pieces[r][...]


def finish(order, factor, volume, pieces):
    parts_n = len(pieces)
    vmem = pl.BlockSpec(memory_space=pltpu.VMEM)
    smem = pl.BlockSpec(memory_space=pltpu.SMEM)
    return pl.pallas_call(
        lambda *refs: finish_kernel(parts_n, *refs),
        out_shape=jax.ShapeDtypeStruct(volume.shape, volume.dtype),
        in_specs=[smem, smem] + [vmem] * (parts_n + 1),
        out_specs=vmem,
        name="finish",
    )(order, factor, volume, *pieces)


def swapped(x, axis, bit):
    return lax.ppermute(x, axis, [(i, i ^ bit) for i in range(lax.axis_size(axis))])


def gathered(piece):
    part = lax.axis_index("view")
    depth = part // 2
    end = (depth == 0) | (depth == 3)

    def along(x, pairs):
        return lax.ppermute(x, "view", [(2 * a + y, 2 * b + y) for a, b in pairs for y in (0, 1)])

    across = [swapped(piece, "view", 1)]
    second = along(piece, [(0, 1), (1, 0), (2, 3), (3, 2)])
    middle = along(piece, [(1, 2), (2, 1)])
    across.append(swapped(second, "view", 1))
    onward = along(middle, [(1, 0), (2, 3)])
    middle_last = along(second, [(1, 2), (2, 1)])
    third = jnp.where(end, onward, middle)
    across.append(swapped(third, "view", 1))
    last = jnp.where(end, along(middle_last, [(1, 0), (2, 3)]), middle_last)
    across.append(swapped(last, "view", 1))
    upper = depth // 2
    depths = [depth, depth ^ 1, 2 - upper, 3 - 3 * upper]
    order = jnp.stack([2 * d + part % 2 for d in depths] + [2 * d + 1 - part % 2 for d in depths])
    return order.astype(jnp.int32), [piece, second, third, last] + across


def local_split(volume, sinogram, curvature, angles, offsets):
    slices_n, rows_n, cols_n = volume.shape
    views_n = angles.shape[0]
    bins_n = sinogram.shape[2]
    base, blocks = extent(rows_n, cols_n, bins_n)
    dims = (rows_n, cols_n, bins_n, base, blocks)
    slab_count = lax.axis_size("slab")
    parts_n = lax.axis_size("view")
    slab = lax.axis_index("slab")
    core = slab % 2
    part = lax.axis_index("view")
    per_n = cols_n // parts_n

    measured = sinogram[:, :, base : base + blocks * LANES]
    measured = measured.reshape(views_n, slices_n, blocks, LANES).transpose(0, 2, 1, 3)
    pair_rows = swapped(measured, "slab", 1)
    chip_rows = jnp.stack(
        [
            lax.dynamic_index_in_dim(measured, core, 0, keepdims=False),
            lax.dynamic_index_in_dim(pair_rows, core, 0, keepdims=False),
        ]
    )
    cross_rows = swapped(chip_rows, "slab", 2)
    cross_other = swapped(cross_rows, "slab", 1)

    angle_rad = angles.astype(jnp.float32) * (2.0 * math.pi / ROTATION_VIEWS)
    trig = jnp.concatenate([jnp.cos(angle_rad), jnp.sin(angle_rad)])
    proj = project(trig, volume, bins_n, base, blocks, views_n)
    near = swapped(proj, "slab", 1)
    turned = offsets[:, 0] > slices_n
    chip = slab // 2
    edge_core = jnp.where(turned, chip, 1 - chip)
    sends_own = lax.dynamic_index_in_dim(edge_core, core, 0, keepdims=False) == core
    edge = jnp.where(
        sends_own,
        lax.dynamic_index_in_dim(proj, core, 0, keepdims=False),
        lax.dynamic_index_in_dim(near, core, 0, keepdims=False),
    )
    far = swapped(edge, "slab", 2)
    far_other = swapped(far, "slab", 1)

    def of(k):
        return lax.dynamic_index_in_dim(offsets, k, 1, keepdims=False)

    far_slab = 2 * (1 - chip) + jnp.where(turned, 1 - chip, chip)
    start = of(slab)
    far_start = jnp.take_along_axis(offsets, far_slab[:, None], axis=1)[:, 0]

    def shift(other):
        return slices_n + jnp.clip(start - other, -slices_n, slices_n)

    table = jnp.stack([start, shift(of(slab ^ 1)), shift(far_start)], axis=1).reshape(-1)
    ints = jnp.concatenate([jnp.stack([slab, core, part]).astype(jnp.int32), table])
    windows = residual_windows(
        dims, parts_n, ints, trig,
        [proj, near, far, far_other, measured, pair_rows, cross_rows, cross_other],
    )
    pieces = [windows[0]] + [swapped(windows[r], "view", r) for r in range(1, parts_n)]
    data_grad = gather_views(dims, parts_n, ints, pieces).transpose(1, 0, 2)

    wide = jnp.pad(volume, ((0, 0), (0, 0), (1, 1)))
    block = lax.dynamic_slice_in_dim(wide, part * per_n, per_n + 2, axis=2)
    padded = jnp.pad(padded_2(block, (("slab", 0),), 1), ((0, 0), (1, 1), (0, 0)))
    tv_grad = tv_padded(padded)
    curv = lax.dynamic_slice_in_dim(curvature, part * per_n, per_n, axis=2)
    direction = (data_grad + tv_weight * tv_grad) / curv
    squares = jnp.sum(direction * direction).reshape(1, 1)
    for axis in ("slab", "view"):
        bit = 1
        while bit < lax.axis_size(axis):
            squares = squares + swapped(squares, axis, bit)
            bit *= 2
    order, parts = gathered(direction)
    voxel_count = slices_n * slab_count * rows_n * cols_n
    factor = jnp.minimum(1.0, step_limit / jnp.sqrt(squares / voxel_count + epsilon))
    return finish(order, factor.reshape(1), volume, parts)


def local(volume, sinogram, curvature, angles, offsets):
    shape = (lax.axis_size("slab"), lax.axis_size("view"), angles.shape[0])
    if shape == (4, 8, 2):
        return local_split(volume, sinogram, curvature, angles, offsets)
    return local_any(volume, sinogram, curvature, angles, offsets)


def solution(mesh):
    in_specs = (
        P("slab", None, None),
        P("view", "slab", None),
        P("slab", None, None),
        P("view"),
        P("view", None),
    )
    out_specs = P("slab", None, None)
    return jax.shard_map(local, mesh=mesh, in_specs=in_specs, out_specs=out_specs, check_vma=False)
```

```python
import math
import jax
import jax.numpy as jnp
from jax import lax
from jax.experimental import pallas as pl
from jax.experimental.pallas import tpu as pltpu
from jax.sharding import PartitionSpec as P

ROTATION_VIEWS = 1152


huber_delta = 0.5
tv_weight = 4.0
step_limit = 1.0
epsilon = 1e-06
scale = 0.7
LANES = 128
GROUP = 8


def coordinate(across, along, cos, sin, bins_n):
    return scale * (across * cos + along * sin) + 0.5 * bins_n - 0.5


def window_of(start, cos, sin, along, cols_n, bins_n, base):
    first = coordinate(start - 0.5 * cols_n + 0.5, along, cos, sin, bins_n)
    last = coordinate(start + (LANES - 1.0) - 0.5 * cols_n + 0.5, along, cos, sin, bins_n)
    return jnp.minimum(first, last).astype(jnp.int32) - (base + 1)


def project_kernel(cols_n, rows_n, bins_n, base, blocks_n, views_n, trig_ref, vol_ref, out_ref, rows_ref, acc_ref, sem):
    copies = [pltpu.make_async_copy(vol_ref.at[:, i, :], rows_ref.at[i], sem.at[i]) for i in range(rows_n)]
    for c in copies:
        c.start()
    acc_ref[...] = jnp.zeros_like(acc_ref)
    lane8 = lax.broadcasted_iota(jnp.int32, (8, LANES), 1)
    lane = lax.broadcasted_iota(jnp.int32, (16, LANES), 1)
    sub = lax.broadcasted_iota(jnp.int32, (LANES, LANES), 0).astype(jnp.float32).astype(jnp.bfloat16)
    zero = jnp.zeros((LANES, LANES), jnp.bfloat16)

    def tall(x):
        return jnp.concatenate([jnp.concatenate([x, x], 0).astype(jnp.bfloat16)] * (LANES // 16), 0)

    for row in range(rows_n):
        copies[row].wait()
        along = row - 0.5 * rows_n + 0.5

        def step(g, _):
            outs = []
            for u in range(GROUP):
                block = g * GROUP + u
                start = (block * LANES).astype(jnp.float32)
                vals = rows_ref[row, :, pl.ds(pl.multiple_of(block * LANES, LANES), LANES)]
                high = vals.astype(jnp.bfloat16)
                rest = vals - high.astype(jnp.float32)
                mid = rest.astype(jnp.bfloat16)
                low = (rest - mid.astype(jnp.float32)).astype(jnp.bfloat16)
                terms = jnp.concatenate([high, mid, low], 0)
                mats = []
                wins = []
                for v in range(views_n):
                    cos = trig_ref[v]
                    sin = trig_ref[views_n + v]
                    across = (lane8 + block * LANES).astype(jnp.float32) - 0.5 * cols_n + 0.5
                    coord = coordinate(across, along, cos, sin, bins_n)
                    lower = jnp.floor(coord)
                    frac = coord - lower
                    rel = lower - float(base)
                    bm = rel - LANES * jnp.floor(rel * (1.0 / LANES))
                    bn = jnp.where(bm == LANES - 1.0, 0.0, bm + 1.0)
                    fh = jnp.floor(frac * 128.0) * (1.0 / 128.0)
                    fl = frac - fh
                    here = sub == tall(bm)
                    next_ = sub == tall(bn)
                    wh = jnp.where(here, tall(1.0 - fh), jnp.where(next_, tall(fh), zero))
                    wl = jnp.where(here, tall(-fl), jnp.where(next_, tall(fl), zero))
                    mats.append(jnp.concatenate([wh, wl], 1))
                    wins.append(window_of(start, cos, sin, along, cols_n, bins_n, base))
                weights = jnp.concatenate(mats, 0)
                both = jnp.concatenate([terms, terms], 1)
                prod = lax.dot_general(both, weights, (((1,), (1,)), ((), ())), preferred_element_type=jnp.float32)
                outs.append((prod[0:16] + prod[16:32] + prod[32:48], wins))
            for summed, wins in outs:
                for v in range(views_n):
                    first = wins[v]
                    k = first >> 7
                    own = lane >= (first & (LANES - 1))
                    part = summed[:, v * LANES:(v + 1) * LANES]
                    acc_ref[v, k] += jnp.where(own, part, 0.0)
                    acc_ref[v, k + 1] += jnp.where(own, 0.0, part)
            return 0

        lax.fori_loop(0, cols_n // LANES // GROUP, step, 0)
    out_ref[...] = acc_ref[:, :blocks_n]


def project(trig, volume, bins_n, base, blocks_n, views_n):
    slices_n, rows_n, cols_n = volume.shape
    body = lambda *refs: project_kernel(cols_n, rows_n, bins_n, base, blocks_n, views_n, *refs)
    return pl.pallas_call(
        body,
        out_shape=jax.ShapeDtypeStruct((views_n, blocks_n, slices_n, LANES), jnp.float32),
        in_specs=[pl.BlockSpec(memory_space=pltpu.SMEM), pl.BlockSpec(memory_space=pl.ANY)],
        out_specs=pl.BlockSpec(memory_space=pltpu.VMEM),
        scratch_shapes=[
            pltpu.VMEM((rows_n, slices_n, cols_n), jnp.float32),
            pltpu.VMEM((views_n, blocks_n + 1, slices_n, LANES), jnp.float32),
            pltpu.SemaphoreType.DMA((rows_n,)),
        ],
        name="project",
    )(trig, volume)


def backproject_kernel(cols_n, rows_n, bins_n, base, views_n, width, per_n, trig_ref, starts_ref, res_ref, out_ref):
    lane16 = lax.broadcasted_iota(jnp.int32, (16, LANES), 1)
    pixel0 = starts_ref[views_n]

    def row_step(row, _):
        along = row.astype(jnp.float32) - 0.5 * rows_n + 0.5

        def step(u, _):
            column = pixel0 + u * LANES
            start = column.astype(jnp.float32)
            across = (lane16 + column).astype(jnp.float32) - 0.5 * cols_n + 0.5
            total = jnp.zeros((16, LANES), jnp.float32)
            for v in range(views_n):
                cos = trig_ref[v]
                sin = trig_ref[views_n + v]
                coord = coordinate(across, along, cos, sin, bins_n)
                lower = jnp.floor(coord)
                frac = coord - lower
                offset = starts_ref[v]
                rel = lower.astype(jnp.int32) - (base + offset)
                here = rel & (LANES - 1)
                next_ = (rel + 1) & (LANES - 1)
                first = window_of(start, cos, sin, along, cols_n, bins_n, base) - offset
                k = first >> 7
                left = res_ref[v, k]
                right = res_ref[v, jnp.minimum(k + 1, width - 1)]
                band = jnp.where(lane16 >= (first & (LANES - 1)), left, right)
                a = jnp.take_along_axis(band, here, axis=1, mode="promise_in_bounds")
                b = jnp.take_along_axis(band, next_, axis=1, mode="promise_in_bounds")
                total = total + (a * (1.0 - frac) + b * frac)
            out_ref[row, :, pl.ds(pl.multiple_of(u * LANES, LANES), LANES)] = total
            return 0

        lax.fori_loop(0, per_n // LANES, step, 0)
        return 0

    lax.fori_loop(0, rows_n, row_step, 0)


def backproject(trig, starts, res, rows_n, cols_n, bins_n, base, per_n):
    views_n, width, slices_n, _ = res.shape
    body = lambda *refs: backproject_kernel(cols_n, rows_n, bins_n, base, views_n, width, per_n, *refs)
    return pl.pallas_call(
        body,
        out_shape=jax.ShapeDtypeStruct((rows_n, slices_n, per_n), jnp.float32),
        in_specs=[pl.BlockSpec(memory_space=pltpu.SMEM), pl.BlockSpec(memory_space=pltpu.SMEM), pl.BlockSpec(memory_space=pltpu.VMEM)],
        out_specs=pl.BlockSpec(memory_space=pltpu.VMEM),
        name="backproject",
    )(trig, starts, res)


def padded_2(cells, sides, width):
    for axis, dim in sides:
        count = lax.axis_size(axis)
        ends = count - 1
        head = lax.slice_in_dim(cells, 0, width, axis=dim)
        tail = lax.slice_in_dim(cells, cells.shape[dim] - width, cells.shape[dim], axis=dim)
        cells = jnp.concatenate(
            [
                lax.ppermute(tail, axis, [(i, (i + 1) % count) for i in range(ends)]),
                cells,
                lax.ppermute(head, axis, [((i + 1) % count, i) for i in range(ends)]),
            ],
            axis=dim,
        )
    return cells


def slope(diff):
    return jnp.clip(diff / huber_delta, -1.0, 1.0)


def tv_padded(padded):
    centre = padded[1:-1, 1:-1, 1:-1]
    result = slope(centre - padded[:-2, 1:-1, 1:-1]) - slope(padded[2:, 1:-1, 1:-1] - centre)
    result = (
        result + slope(centre - padded[1:-1, :-2, 1:-1]) - slope(padded[1:-1, 2:, 1:-1] - centre)
    )
    result = (
        result + slope(centre - padded[1:-1, 1:-1, :-2]) - slope(padded[1:-1, 1:-1, 2:] - centre)
    )
    return result


def extent(rows_n, cols_n, bins_n):
    reach = scale * math.hypot(0.5 * (cols_n - 1), 0.5 * (rows_n - 1))
    centre = 0.5 * bins_n - 0.5
    base = (int(centre - reach) - 3) // 8 * 8
    blocks = -(-(int(centre + reach) + 3 - base) // LANES)
    return base, blocks


def local_any(volume, sinogram, curvature, angles, offsets):
    slices_n, rows_n, cols_n = volume.shape
    views_n = angles.shape[0]
    bins_n = sinogram.shape[2]
    base, blocks = extent(rows_n, cols_n, bins_n)
    pixels_n = rows_n * cols_n
    slab_count = lax.axis_size("slab")
    all_rows = sinogram.shape[1] * slab_count
    slab_pos = lax.axis_index("slab")
    angle_rad = angles.astype(jnp.float32) * (2.0 * math.pi / ROTATION_VIEWS)
    trig = jnp.concatenate([jnp.cos(angle_rad), jnp.sin(angle_rad)])
    proj = project(trig, volume, bins_n, base, blocks, views_n)
    stacked = []
    bands = []
    for v in range(views_n):
        start = lax.dynamic_index_in_dim(offsets[v], slab_pos, 0, keepdims=False)
        flat = proj[v].transpose(1, 0, 2).reshape(slices_n, blocks * LANES)
        stacked.append(
            lax.dynamic_update_slice(
                jnp.zeros((all_rows, blocks * LANES), jnp.float32), flat, (start, jnp.int32(0))
            )
        )
        bands.append(start)
    own = lax.psum_scatter(jnp.stack(stacked), "slab", scatter_dimension=1, tiled=True)
    measured = sinogram[:, :, base : base + blocks * LANES]
    residual = lax.all_gather(own - measured, "slab", axis=1, tiled=True)
    windows = jnp.stack(
        [
            lax.dynamic_slice(
                residual[v], (bands[v], jnp.int32(0)), (slices_n, blocks * LANES)
            )
            .reshape(slices_n, blocks, LANES)
            .transpose(1, 0, 2)
            for v in range(views_n)
        ]
    )
    starts = jnp.zeros((views_n + 1,), jnp.int32)
    data_local = backproject(trig, starts, windows, rows_n, cols_n, bins_n, base, cols_n)
    extended = padded_2(volume, (("slab", 0),), 1)
    padded = jnp.pad(extended, ((0, 0), (1, 1), (1, 1)))
    tv_grad = tv_padded(padded)
    data_grad = lax.psum(data_local, "view").transpose(1, 0, 2)
    direction = (data_grad + tv_weight * tv_grad) / curvature
    squares = lax.psum(jnp.sum(direction * direction), "slab")
    voxel_count = slices_n * slab_count * pixels_n
    factor = jnp.minimum(1.0, step_limit / jnp.sqrt(squares / voxel_count + epsilon))
    return volume - factor * direction


WINDOW = 3
COS_LANE = LANES - 2
SIN_LANE = LANES - 1


def window_start(part, per_n, cos, sin, rows_n, cols_n, bins_n, base, blocks):
    low = None
    for row in (0, rows_n - 1):
        along = row - 0.5 * rows_n + 0.5
        for edge in (0.0, per_n - 1.0):
            across = (part * per_n).astype(jnp.float32) + edge - 0.5 * cols_n + 0.5
            t = coordinate(across, along, cos, sin, bins_n)
            low = t if low is None else jnp.minimum(low, t)
    first = low.astype(jnp.int32) - (base + 1)
    return jnp.clip(first, 0, (blocks - WINDOW) * LANES)


def residual_kernel(dims, parts_n, ints_ref, trig_ref, *rest):
    rows_n, cols_n, bins_n, base, blocks = dims
    projs, sinos, outs = rest[:4], rest[4:8], rest[8 : 8 + parts_n]
    pads = rest[8 + parts_n : 11 + parts_n]
    sino, res = rest[11 + parts_n :]
    views_n, _, band, _ = projs[0].shape
    slab, part = ints_ref[0], ints_ref[1]
    for other in range(1, 4):
        pad = pads[other - 1]
        pad[:, :, 0:band] = jnp.zeros((views_n, blocks, band, LANES), jnp.float32)
        pad[:, :, 2 * band :] = jnp.zeros((views_n, blocks, band, LANES), jnp.float32)
        pad[:, :, band : 2 * band] = projs[other][...]
    for other in range(4):
        rows = pl.ds(pl.multiple_of((slab ^ other) * band, band), band)
        sino[:, :, rows] = sinos[other][:, 0:blocks]
    for v in range(views_n):
        value = projs[0][v]
        for other in range(1, 4):
            value = value + pads[other - 1][v, :, pl.ds(ints_ref[2 + 4 * v + other], band), :]
        res[v, 0:blocks] = value - sino[v, :, pl.ds(ints_ref[2 + 4 * v], band), :]
        res[v, blocks] = jnp.zeros((band, LANES), jnp.float32)
    lane = lax.broadcasted_iota(jnp.int32, (band, LANES), 1)
    per_n = cols_n // parts_n
    for r in range(parts_n):
        for v in range(views_n):
            cos, sin = trig_ref[v], trig_ref[views_n + v]
            first = window_start(part ^ r, per_n, cos, sin, rows_n, cols_n, bins_n, base, blocks)
            k = first >> 7
            shift = first & (LANES - 1)
            turned = [pltpu.roll(res[v, k + m], (LANES - shift) & (LANES - 1), 1) for m in range(WINDOW + 1)]
            for m in range(WINDOW):
                value = jnp.where(lane < LANES - shift, turned[m], turned[m + 1])
                if m == WINDOW - 1:
                    value = jnp.where(lane == COS_LANE, cos, jnp.where(lane == SIN_LANE, sin, value))
                outs[r][v, m] = value


def residual_windows(dims, parts_n, ints, trig, arrays):
    views_n, blocks, band, _ = arrays[0].shape
    body = lambda *refs: residual_kernel(dims, parts_n, *refs)
    vmem = pl.BlockSpec(memory_space=pltpu.VMEM)
    smem = pl.BlockSpec(memory_space=pltpu.SMEM)
    return pl.pallas_call(
        body,
        out_shape=[jax.ShapeDtypeStruct((views_n, WINDOW, band, LANES), jnp.float32)] * parts_n,
        in_specs=[smem, smem] + [vmem] * len(arrays),
        out_specs=[vmem] * parts_n,
        scratch_shapes=[
            pltpu.VMEM((views_n, blocks, 3 * band, LANES), jnp.float32),
            pltpu.VMEM((views_n, blocks, 3 * band, LANES), jnp.float32),
            pltpu.VMEM((views_n, blocks, 3 * band, LANES), jnp.float32),
            pltpu.VMEM((views_n, blocks, 4 * band, LANES), jnp.float32),
            pltpu.VMEM((views_n, blocks + 1, band, LANES), jnp.float32),
        ],
        name="residual_windows",
    )(ints, trig, *arrays)


def gather_kernel(dims, parts_n, views_n, ints_ref, *rest):
    rows_n, cols_n, bins_n, base, blocks = dims
    pieces = rest[:parts_n]
    out_ref, trig_ref, starts_ref = rest[parts_n:]
    per_n = cols_n // parts_n
    part = ints_ref[1]
    lane8 = lax.broadcasted_iota(jnp.int32, (8, LANES), 1)
    lane = lax.broadcasted_iota(jnp.int32, (16, LANES), 1)
    total_n = parts_n * views_n
    for n in range(total_n):
        tagged = pieces[n // views_n][n % views_n, WINDOW - 1, 0:8, :]
        cos = jnp.max(jnp.where(lane8 == COS_LANE, tagged, -2.0))
        sin = jnp.max(jnp.where(lane8 == SIN_LANE, tagged, -2.0))
        trig_ref[n] = cos
        trig_ref[total_n + n] = sin
        starts_ref[n] = window_start(part, per_n, cos, sin, rows_n, cols_n, bins_n, base, blocks)

    def step(index, _):
        row = index // (per_n // LANES)
        u = index - row * (per_n // LANES)
        along = row.astype(jnp.float32) - 0.5 * rows_n + 0.5
        column = part * per_n + u * LANES
        start = column.astype(jnp.float32)
        across = (lane + column).astype(jnp.float32) - 0.5 * cols_n + 0.5
        total = jnp.zeros((16, LANES), jnp.float32)
        for n in range(total_n):
            cos = trig_ref[n]
            sin = trig_ref[total_n + n]
            offset = starts_ref[n]
            coord = coordinate(across, along, cos, sin, bins_n)
            lower = jnp.floor(coord)
            frac = coord - lower
            rel = lower.astype(jnp.int32) - (base + offset)
            here = rel & (LANES - 1)
            next_ = (rel + 1) & (LANES - 1)
            first = jnp.maximum(window_of(start, cos, sin, along, cols_n, bins_n, base) - offset, 0)
            k = jnp.minimum(first >> 7, WINDOW - 1)
            windows = pieces[n // views_n]
            left = windows[n % views_n, k]
            right = windows[n % views_n, jnp.minimum(k + 1, WINDOW - 1)]
            held = jnp.where(lane >= (first & (LANES - 1)), left, right)
            a = jnp.take_along_axis(held, here, axis=1, mode="promise_in_bounds")
            b = jnp.take_along_axis(held, next_, axis=1, mode="promise_in_bounds")
            total = total + (a * (1.0 - frac) + b * frac)
        out_ref[row, :, pl.ds(pl.multiple_of(u * LANES, LANES), LANES)] = total
        return 0

    lax.fori_loop(0, rows_n * (per_n // LANES), step, 0)


def gather_views(dims, parts_n, ints, pieces):
    views_n, _, slices_n, _ = pieces[0].shape
    rows_n, cols_n = dims[:2]
    body = lambda *refs: gather_kernel(dims, parts_n, views_n, *refs)
    vmem = pl.BlockSpec(memory_space=pltpu.VMEM)
    return pl.pallas_call(
        body,
        out_shape=jax.ShapeDtypeStruct((rows_n, slices_n, cols_n // parts_n), jnp.float32),
        in_specs=[pl.BlockSpec(memory_space=pltpu.SMEM)] + [vmem] * parts_n,
        out_specs=vmem,
        scratch_shapes=[
            pltpu.SMEM((2 * parts_n * views_n,), jnp.float32),
            pltpu.SMEM((parts_n * views_n,), jnp.int32),
        ],
        name="gather_views",
    )(ints, *pieces)


def finish_kernel(parts_n, order_ref, factor_ref, vol_ref, *rest):
    pieces = rest[:parts_n]
    out_ref = rest[parts_n]
    factor = factor_ref[0]
    per_n = pieces[0].shape[2]
    for r in range(parts_n):
        cols = pl.ds(pl.multiple_of(order_ref[r] * per_n, per_n), per_n)
        out_ref[:, :, cols] = vol_ref[:, :, cols] - factor * pieces[r][...]


def finish(order, factor, volume, pieces):
    parts_n = len(pieces)
    vmem = pl.BlockSpec(memory_space=pltpu.VMEM)
    smem = pl.BlockSpec(memory_space=pltpu.SMEM)
    return pl.pallas_call(
        lambda *refs: finish_kernel(parts_n, *refs),
        out_shape=jax.ShapeDtypeStruct(volume.shape, volume.dtype),
        in_specs=[smem, smem] + [vmem] * (parts_n + 1),
        out_specs=vmem,
        name="finish",
    )(order, factor, volume, *pieces)


def swapped(x, axis, bit):
    return lax.ppermute(x, axis, [(i, i ^ bit) for i in range(lax.axis_size(axis))])


def gathered(piece, squares):
    part = lax.axis_index("view")
    depth = part // 2
    end = (depth == 0) | (depth == 3)

    def along(x, pairs):
        return lax.ppermute(x, "view", [(2 * a + y, 2 * b + y) for a, b in pairs for y in (0, 1)])

    first = swapped(piece, "view", 1)
    second = along(piece, [(0, 1), (1, 0), (2, 3), (3, 2)])
    middle = along(piece, [(1, 2), (2, 1)])
    squares = squares + swapped(squares, "slab", 1) + (swapped(squares, "slab", 2) + swapped(squares, "slab", 3))
    first, second, middle, squares = lax.optimization_barrier((first, second, middle, squares))
    across = [first, swapped(second, "view", 1)]
    onward = along(middle, [(1, 0), (2, 3)])
    middle_last = along(second, [(1, 2), (2, 1)])
    squares = squares + swapped(squares, "view", 1) + (swapped(squares, "view", 2) + swapped(squares, "view", 3))
    onward, middle_last, squares = lax.optimization_barrier((onward, middle_last, squares))
    third = jnp.where(end, onward, middle)
    across.append(swapped(third, "view", 1))
    last = along(middle_last, [(1, 0), (2, 3)])
    squares = squares + swapped(squares, "view", 4)
    last, squares = lax.optimization_barrier((last, squares))
    last = jnp.where(end, last, middle_last)
    across.append(swapped(last, "view", 1))
    upper = depth // 2
    depths = [depth, depth ^ 1, 2 - upper, 3 - 3 * upper]
    order = jnp.stack([2 * d + part % 2 for d in depths] + [2 * d + 1 - part % 2 for d in depths])
    return order.astype(jnp.int32), [piece, second, third, last] + across, squares


def local_split(volume, sinogram, curvature, angles, offsets):
    slices_n, rows_n, cols_n = volume.shape
    views_n = angles.shape[0]
    bins_n = sinogram.shape[2]
    base, blocks = extent(rows_n, cols_n, bins_n)
    dims = (rows_n, cols_n, bins_n, base, blocks)
    slab_count = lax.axis_size("slab")
    parts_n = lax.axis_size("view")
    slab = lax.axis_index("slab")
    part = lax.axis_index("view")
    per_n = cols_n // parts_n

    angle_rad = angles.astype(jnp.float32) * (2.0 * math.pi / ROTATION_VIEWS)
    trig = jnp.concatenate([jnp.cos(angle_rad), jnp.sin(angle_rad)])

    def outer(at):
        face = lax.dynamic_slice(volume, (at, 0, part * per_n), (1, rows_n, per_n))
        return face.reshape(1, 1, slices_n, LANES)

    measured = sinogram[:, :, base : base + blocks * LANES]
    measured = measured.reshape(views_n, slices_n, blocks, LANES).transpose(0, 2, 1, 3)
    faces = jnp.concatenate([outer(0), outer(slices_n - 1)], axis=0)
    measured = jnp.concatenate([measured, faces], axis=1)
    cross_rows = swapped(measured, "slab", 2)
    pair_rows = swapped(measured, "slab", 1)
    trig, measured = lax.optimization_barrier((trig, measured))
    proj = project(trig, volume, bins_n, base, blocks, views_n)
    cross_pair_rows = swapped(cross_rows, "slab", 1)
    cross = swapped(proj, "slab", 2)
    near = swapped(proj, "slab", 1)
    cross_pair = swapped(cross, "slab", 1)

    def of(k):
        return lax.dynamic_index_in_dim(offsets, k, 1, keepdims=False)

    start = of(slab)
    shifts = [slices_n + jnp.clip(start - of(slab ^ k), -slices_n, slices_n) for k in (1, 2, 3)]
    table = jnp.stack([start] + shifts, axis=1).reshape(-1)
    ints = jnp.concatenate([jnp.stack([slab, part]).astype(jnp.int32), table])
    windows = residual_windows(
        dims,
        parts_n,
        ints,
        trig,
        [proj, near, cross, cross_pair, measured, pair_rows, cross_rows, cross_pair_rows],
    )
    pieces = [windows[0]] + [swapped(windows[r], "view", r) for r in range(1, parts_n)]
    data_grad = gather_views(dims, parts_n, ints, pieces).transpose(1, 0, 2)

    def face_of(rows, which):
        return rows[which, blocks].reshape(1, rows_n, per_n)

    odd = slab % 2 == 1
    below = jnp.where(odd, face_of(pair_rows, 1), jnp.where(slab == 0, 0.0, face_of(cross_pair_rows, 1)))
    above = jnp.where(odd, jnp.where(slab == slab_count - 1, 0.0, face_of(cross_pair_rows, 0)), face_of(pair_rows, 0))
    wide = jnp.pad(volume, ((0, 0), (0, 0), (1, 1)))
    block = lax.dynamic_slice_in_dim(wide, part * per_n, per_n + 2, axis=2)
    sides = ((0, 0), (0, 0), (1, 1))
    block = jnp.concatenate([jnp.pad(below, sides), block, jnp.pad(above, sides)], axis=0)
    tv_grad = tv_padded(jnp.pad(block, ((0, 0), (1, 1), (0, 0))))
    curv = lax.dynamic_slice_in_dim(curvature, part * per_n, per_n, axis=2)
    direction = (data_grad + tv_weight * tv_grad) / curv
    order, parts, squares = gathered(direction, jnp.sum(direction * direction).reshape(1, 1))
    voxel_count = slices_n * slab_count * rows_n * cols_n
    factor = jnp.minimum(1.0, step_limit / jnp.sqrt(squares / voxel_count + epsilon))
    return finish(order, factor.reshape(1), volume, parts)


def local(volume, sinogram, curvature, angles, offsets):
    shape = (lax.axis_size("slab"), lax.axis_size("view"), angles.shape[0])
    if shape == (4, 8, 2):
        return local_split(volume, sinogram, curvature, angles, offsets)
    return local_any(volume, sinogram, curvature, angles, offsets)


def solution(mesh):
    in_specs = (
        P("slab", None, None),
        P("view", "slab", None),
        P("slab", None, None),
        P("view"),
        P("view", None),
    )
    out_specs = P("slab", None, None)
    return jax.shard_map(local, mesh=mesh, in_specs=in_specs, out_specs=out_specs, check_vma=False)
```

```python
import math
import jax
import jax.numpy as jnp
from jax import lax
from jax.experimental import pallas as pl
from jax.experimental.pallas import tpu as pltpu
from jax.sharding import PartitionSpec as P

ROTATION_VIEWS = 1152


huber_delta = 0.5
tv_weight = 4.0
step_limit = 1.0
epsilon = 1e-06
scale = 0.7
LANES = 128
GROUP = 32


def coordinate(across, along, cos, sin, bins_n):
    return scale * (across * cos + along * sin) + 0.5 * bins_n - 0.5


def window_of(start, cos, sin, along, cols_n, bins_n, base):
    first = coordinate(start - 0.5 * cols_n + 0.5, along, cos, sin, bins_n)
    last = coordinate(start + (LANES - 1.0) - 0.5 * cols_n + 0.5, along, cos, sin, bins_n)
    return jnp.minimum(first, last).astype(jnp.int32) - (base + 1)


def project_kernel(cols_n, rows_n, bins_n, base, blocks_n, views_n, trig_ref, vol_ref, out_ref, rows_ref, acc_ref, sem):
    copies = [pltpu.make_async_copy(vol_ref.at[:, i, :], rows_ref.at[i], sem.at[i]) for i in range(rows_n)]
    for c in copies:
        c.start()
    acc_ref[...] = jnp.zeros_like(acc_ref)
    lane8 = lax.broadcasted_iota(jnp.int32, (8, LANES), 1)
    lane = lax.broadcasted_iota(jnp.int32, (16, LANES), 1)
    sub = lax.broadcasted_iota(jnp.int32, (LANES, LANES), 0).astype(jnp.float32).astype(jnp.bfloat16)
    zero = jnp.zeros((LANES, LANES), jnp.bfloat16)

    def tall(x):
        return jnp.concatenate([jnp.concatenate([x, x], 0).astype(jnp.bfloat16)] * (LANES // 16), 0)

    for row in range(rows_n):
        copies[row].wait()
        along = row - 0.5 * rows_n + 0.5

        def step(g, _):
            outs = []
            for u in range(GROUP):
                block = g * GROUP + u
                start = (block * LANES).astype(jnp.float32)
                vals = rows_ref[row, :, pl.ds(pl.multiple_of(block * LANES, LANES), LANES)]
                high = vals.astype(jnp.bfloat16)
                rest = vals - high.astype(jnp.float32)
                mid = rest.astype(jnp.bfloat16)
                low = (rest - mid.astype(jnp.float32)).astype(jnp.bfloat16)
                terms = jnp.concatenate([high, mid, low], 0)
                mats = []
                wins = []
                for v in range(views_n):
                    cos = trig_ref[v]
                    sin = trig_ref[views_n + v]
                    across = (lane8 + block * LANES).astype(jnp.float32) - 0.5 * cols_n + 0.5
                    coord = coordinate(across, along, cos, sin, bins_n)
                    lower = jnp.floor(coord)
                    frac = coord - lower
                    rel = lower - float(base)
                    bm = rel - LANES * jnp.floor(rel * (1.0 / LANES))
                    bn = jnp.where(bm == LANES - 1.0, 0.0, bm + 1.0)
                    fh = jnp.floor(frac * 128.0) * (1.0 / 128.0)
                    fl = frac - fh
                    here = sub == tall(bm)
                    next_ = sub == tall(bn)
                    wh = jnp.where(here, tall(1.0 - fh), jnp.where(next_, tall(fh), zero))
                    wl = jnp.where(here, tall(-fl), jnp.where(next_, tall(fl), zero))
                    mats.append(jnp.concatenate([wh, wl], 1))
                    wins.append(window_of(start, cos, sin, along, cols_n, bins_n, base))
                weights = jnp.concatenate(mats, 0)
                both = jnp.concatenate([terms, terms], 1)
                prod = lax.dot_general(both, weights, (((1,), (1,)), ((), ())), preferred_element_type=jnp.float32)
                outs.append((prod[0:16] + prod[16:32] + prod[32:48], wins))
            for summed, wins in outs:
                for v in range(views_n):
                    first = wins[v]
                    k = first >> 7
                    own = lane >= (first & (LANES - 1))
                    part = summed[:, v * LANES:(v + 1) * LANES]
                    acc_ref[v, k] += jnp.where(own, part, 0.0)
                    acc_ref[v, k + 1] += jnp.where(own, 0.0, part)
            return 0

        lax.fori_loop(0, cols_n // LANES // GROUP, step, 0)
    out_ref[...] = acc_ref[:, :blocks_n]


def project(trig, volume, bins_n, base, blocks_n, views_n):
    slices_n, rows_n, cols_n = volume.shape
    body = lambda *refs: project_kernel(cols_n, rows_n, bins_n, base, blocks_n, views_n, *refs)
    return pl.pallas_call(
        body,
        out_shape=jax.ShapeDtypeStruct((views_n, blocks_n, slices_n, LANES), jnp.float32),
        in_specs=[pl.BlockSpec(memory_space=pltpu.SMEM), pl.BlockSpec(memory_space=pl.ANY)],
        out_specs=pl.BlockSpec(memory_space=pltpu.VMEM),
        scratch_shapes=[
            pltpu.VMEM((rows_n, slices_n, cols_n), jnp.float32),
            pltpu.VMEM((views_n, blocks_n + 1, slices_n, LANES), jnp.float32),
            pltpu.SemaphoreType.DMA((rows_n,)),
        ],
        name="project",
    )(trig, volume)


def backproject_kernel(cols_n, rows_n, bins_n, base, views_n, width, per_n, trig_ref, starts_ref, res_ref, out_ref):
    lane16 = lax.broadcasted_iota(jnp.int32, (16, LANES), 1)
    pixel0 = starts_ref[views_n]

    def row_step(row, _):
        along = row.astype(jnp.float32) - 0.5 * rows_n + 0.5

        def step(u, _):
            column = pixel0 + u * LANES
            start = column.astype(jnp.float32)
            across = (lane16 + column).astype(jnp.float32) - 0.5 * cols_n + 0.5
            total = jnp.zeros((16, LANES), jnp.float32)
            for v in range(views_n):
                cos = trig_ref[v]
                sin = trig_ref[views_n + v]
                coord = coordinate(across, along, cos, sin, bins_n)
                lower = jnp.floor(coord)
                frac = coord - lower
                offset = starts_ref[v]
                rel = lower.astype(jnp.int32) - (base + offset)
                here = rel & (LANES - 1)
                next_ = (rel + 1) & (LANES - 1)
                first = window_of(start, cos, sin, along, cols_n, bins_n, base) - offset
                k = first >> 7
                left = res_ref[v, k]
                right = res_ref[v, jnp.minimum(k + 1, width - 1)]
                band = jnp.where(lane16 >= (first & (LANES - 1)), left, right)
                a = jnp.take_along_axis(band, here, axis=1, mode="promise_in_bounds")
                b = jnp.take_along_axis(band, next_, axis=1, mode="promise_in_bounds")
                total = total + (a * (1.0 - frac) + b * frac)
            out_ref[row, :, pl.ds(pl.multiple_of(u * LANES, LANES), LANES)] = total
            return 0

        lax.fori_loop(0, per_n // LANES, step, 0)
        return 0

    lax.fori_loop(0, rows_n, row_step, 0)


def backproject(trig, starts, res, rows_n, cols_n, bins_n, base, per_n):
    views_n, width, slices_n, _ = res.shape
    body = lambda *refs: backproject_kernel(cols_n, rows_n, bins_n, base, views_n, width, per_n, *refs)
    return pl.pallas_call(
        body,
        out_shape=jax.ShapeDtypeStruct((rows_n, slices_n, per_n), jnp.float32),
        in_specs=[pl.BlockSpec(memory_space=pltpu.SMEM), pl.BlockSpec(memory_space=pltpu.SMEM), pl.BlockSpec(memory_space=pltpu.VMEM)],
        out_specs=pl.BlockSpec(memory_space=pltpu.VMEM),
        name="backproject",
    )(trig, starts, res)


def padded_2(cells, sides, width):
    for axis, dim in sides:
        count = lax.axis_size(axis)
        ends = count - 1
        head = lax.slice_in_dim(cells, 0, width, axis=dim)
        tail = lax.slice_in_dim(cells, cells.shape[dim] - width, cells.shape[dim], axis=dim)
        cells = jnp.concatenate(
            [
                lax.ppermute(tail, axis, [(i, (i + 1) % count) for i in range(ends)]),
                cells,
                lax.ppermute(head, axis, [((i + 1) % count, i) for i in range(ends)]),
            ],
            axis=dim,
        )
    return cells


def slope(diff):
    return jnp.clip(diff / huber_delta, -1.0, 1.0)


def tv_padded(padded):
    centre = padded[1:-1, 1:-1, 1:-1]
    result = slope(centre - padded[:-2, 1:-1, 1:-1]) - slope(padded[2:, 1:-1, 1:-1] - centre)
    result = (
        result + slope(centre - padded[1:-1, :-2, 1:-1]) - slope(padded[1:-1, 2:, 1:-1] - centre)
    )
    result = (
        result + slope(centre - padded[1:-1, 1:-1, :-2]) - slope(padded[1:-1, 1:-1, 2:] - centre)
    )
    return result


def extent(rows_n, cols_n, bins_n):
    reach = scale * math.hypot(0.5 * (cols_n - 1), 0.5 * (rows_n - 1))
    centre = 0.5 * bins_n - 0.5
    base = (int(centre - reach) - 3) // 8 * 8
    blocks = -(-(int(centre + reach) + 3 - base) // LANES)
    return base, blocks


def local_any(volume, sinogram, curvature, angles, offsets):
    slices_n, rows_n, cols_n = volume.shape
    views_n = angles.shape[0]
    bins_n = sinogram.shape[2]
    base, blocks = extent(rows_n, cols_n, bins_n)
    pixels_n = rows_n * cols_n
    slab_count = lax.axis_size("slab")
    all_rows = sinogram.shape[1] * slab_count
    slab_pos = lax.axis_index("slab")
    angle_rad = angles.astype(jnp.float32) * (2.0 * math.pi / ROTATION_VIEWS)
    trig = jnp.concatenate([jnp.cos(angle_rad), jnp.sin(angle_rad)])
    proj = project(trig, volume, bins_n, base, blocks, views_n)
    stacked = []
    bands = []
    for v in range(views_n):
        start = lax.dynamic_index_in_dim(offsets[v], slab_pos, 0, keepdims=False)
        flat = proj[v].transpose(1, 0, 2).reshape(slices_n, blocks * LANES)
        stacked.append(
            lax.dynamic_update_slice(
                jnp.zeros((all_rows, blocks * LANES), jnp.float32), flat, (start, jnp.int32(0))
            )
        )
        bands.append(start)
    own = lax.psum_scatter(jnp.stack(stacked), "slab", scatter_dimension=1, tiled=True)
    measured = sinogram[:, :, base : base + blocks * LANES]
    residual = lax.all_gather(own - measured, "slab", axis=1, tiled=True)
    windows = jnp.stack(
        [
            lax.dynamic_slice(
                residual[v], (bands[v], jnp.int32(0)), (slices_n, blocks * LANES)
            )
            .reshape(slices_n, blocks, LANES)
            .transpose(1, 0, 2)
            for v in range(views_n)
        ]
    )
    starts = jnp.zeros((views_n + 1,), jnp.int32)
    data_local = backproject(trig, starts, windows, rows_n, cols_n, bins_n, base, cols_n)
    extended = padded_2(volume, (("slab", 0),), 1)
    padded = jnp.pad(extended, ((0, 0), (1, 1), (1, 1)))
    tv_grad = tv_padded(padded)
    data_grad = lax.psum(data_local, "view").transpose(1, 0, 2)
    direction = (data_grad + tv_weight * tv_grad) / curvature
    squares = lax.psum(jnp.sum(direction * direction), "slab")
    voxel_count = slices_n * slab_count * pixels_n
    factor = jnp.minimum(1.0, step_limit / jnp.sqrt(squares / voxel_count + epsilon))
    return volume - factor * direction


WINDOW = 3
COS_LANE = LANES - 2
SIN_LANE = LANES - 1


def window_start(part, per_n, cos, sin, rows_n, cols_n, bins_n, base, blocks):
    low = None
    for row in (0, rows_n - 1):
        along = row - 0.5 * rows_n + 0.5
        for edge in (0.0, per_n - 1.0):
            across = (part * per_n).astype(jnp.float32) + edge - 0.5 * cols_n + 0.5
            t = coordinate(across, along, cos, sin, bins_n)
            low = t if low is None else jnp.minimum(low, t)
    first = low.astype(jnp.int32) - (base + 1)
    return jnp.clip(first, 0, (blocks - WINDOW) * LANES)


def residual_kernel(dims, parts_n, ints_ref, trig_ref, *rest):
    rows_n, cols_n, bins_n, base, blocks = dims
    projs, sinos, outs = rest[:4], rest[4:8], rest[8 : 8 + parts_n]
    pads = rest[8 + parts_n : 11 + parts_n]
    sino, res = rest[11 + parts_n :]
    views_n, _, band, _ = projs[0].shape
    slab, part = ints_ref[0], ints_ref[1]
    for other in range(1, 4):
        pad = pads[other - 1]
        pad[:, :, 0:band] = jnp.zeros((views_n, blocks, band, LANES), jnp.float32)
        pad[:, :, 2 * band :] = jnp.zeros((views_n, blocks, band, LANES), jnp.float32)
        pad[:, :, band : 2 * band] = projs[other][...]
    for other in range(4):
        rows = pl.ds(pl.multiple_of((slab ^ other) * band, band), band)
        sino[:, :, rows] = sinos[other][:, 0:blocks]
    for v in range(views_n):
        value = projs[0][v]
        for other in range(1, 4):
            value = value + pads[other - 1][v, :, pl.ds(ints_ref[2 + 4 * v + other], band), :]
        res[v, 0:blocks] = value - sino[v, :, pl.ds(ints_ref[2 + 4 * v], band), :]
        res[v, blocks] = jnp.zeros((band, LANES), jnp.float32)
    lane = lax.broadcasted_iota(jnp.int32, (band, LANES), 1)
    per_n = cols_n // parts_n
    for r in range(parts_n):
        for v in range(views_n):
            cos, sin = trig_ref[v], trig_ref[views_n + v]
            first = window_start(part ^ r, per_n, cos, sin, rows_n, cols_n, bins_n, base, blocks)
            k = first >> 7
            shift = first & (LANES - 1)
            turned = [pltpu.roll(res[v, k + m], (LANES - shift) & (LANES - 1), 1) for m in range(WINDOW + 1)]
            for m in range(WINDOW):
                value = jnp.where(lane < LANES - shift, turned[m], turned[m + 1])
                if m == WINDOW - 1:
                    value = jnp.where(lane == COS_LANE, cos, jnp.where(lane == SIN_LANE, sin, value))
                outs[r][v, m] = value


def residual_windows(dims, parts_n, ints, trig, arrays):
    views_n, blocks, band, _ = arrays[0].shape
    body = lambda *refs: residual_kernel(dims, parts_n, *refs)
    vmem = pl.BlockSpec(memory_space=pltpu.VMEM)
    smem = pl.BlockSpec(memory_space=pltpu.SMEM)
    return pl.pallas_call(
        body,
        out_shape=[jax.ShapeDtypeStruct((views_n, WINDOW, band, LANES), jnp.float32)] * parts_n,
        in_specs=[smem, smem] + [vmem] * len(arrays),
        out_specs=[vmem] * parts_n,
        scratch_shapes=[
            pltpu.VMEM((views_n, blocks, 3 * band, LANES), jnp.float32),
            pltpu.VMEM((views_n, blocks, 3 * band, LANES), jnp.float32),
            pltpu.VMEM((views_n, blocks, 3 * band, LANES), jnp.float32),
            pltpu.VMEM((views_n, blocks, 4 * band, LANES), jnp.float32),
            pltpu.VMEM((views_n, blocks + 1, band, LANES), jnp.float32),
        ],
        name="residual_windows",
    )(ints, trig, *arrays)


def gather_kernel(dims, parts_n, views_n, ints_ref, tv_ref, curv_ref, *rest):
    rows_n, cols_n, bins_n, base, blocks = dims
    pieces = rest[:parts_n]
    out_ref, rows_ref, trig_ref, starts_ref = rest[parts_n:]
    per_n = cols_n // parts_n
    part = ints_ref[1]
    lane8 = lax.broadcasted_iota(jnp.int32, (8, LANES), 1)
    lane = lax.broadcasted_iota(jnp.int32, (16, LANES), 1)
    total_n = parts_n * views_n
    for n in range(total_n):
        tagged = pieces[n // views_n][n % views_n, WINDOW - 1, 0:8, :]
        cos = jnp.max(jnp.where(lane8 == COS_LANE, tagged, -2.0))
        sin = jnp.max(jnp.where(lane8 == SIN_LANE, tagged, -2.0))
        trig_ref[n] = cos
        trig_ref[total_n + n] = sin
        starts_ref[n] = window_start(part, per_n, cos, sin, rows_n, cols_n, bins_n, base, blocks)

    def step(index, squares):
        row = index // (per_n // LANES)
        u = index - row * (per_n // LANES)
        along = row.astype(jnp.float32) - 0.5 * rows_n + 0.5
        column = part * per_n + u * LANES
        start = column.astype(jnp.float32)
        across = (lane + column).astype(jnp.float32) - 0.5 * cols_n + 0.5
        total = jnp.zeros((16, LANES), jnp.float32)
        for n in range(total_n):
            cos = trig_ref[n]
            sin = trig_ref[total_n + n]
            offset = starts_ref[n]
            coord = coordinate(across, along, cos, sin, bins_n)
            lower = jnp.floor(coord)
            frac = coord - lower
            rel = lower.astype(jnp.int32) - (base + offset)
            here = rel & (LANES - 1)
            next_ = (rel + 1) & (LANES - 1)
            first = jnp.maximum(window_of(start, cos, sin, along, cols_n, bins_n, base) - offset, 0)
            k = jnp.minimum(first >> 7, WINDOW - 1)
            windows = pieces[n // views_n]
            left = windows[n % views_n, k]
            right = windows[n % views_n, jnp.minimum(k + 1, WINDOW - 1)]
            held = jnp.where(lane >= (first & (LANES - 1)), left, right)
            a = jnp.take_along_axis(held, here, axis=1, mode="promise_in_bounds")
            b = jnp.take_along_axis(held, next_, axis=1, mode="promise_in_bounds")
            total = total + (a * (1.0 - frac) + b * frac)
        cols = pl.ds(pl.multiple_of(u * LANES, LANES), LANES)
        total = (total + tv_ref[row, :, cols]) / curv_ref[row, :, cols]
        rows_ref[row, :, cols] = total
        return squares + total * total

    squares = lax.fori_loop(0, rows_n * (per_n // LANES), step, jnp.zeros((16, LANES), jnp.float32))
    for row in range(rows_n):
        out_ref[0:16, row, :] = rows_ref[row]
    out_ref[16] = jnp.full((rows_n, per_n), jnp.sum(squares), jnp.float32)


def gather_views(dims, parts_n, ints, tv, curv, pieces):
    views_n, _, slices_n, _ = pieces[0].shape
    rows_n, cols_n = dims[:2]
    body = lambda *refs: gather_kernel(dims, parts_n, views_n, *refs)
    vmem = pl.BlockSpec(memory_space=pltpu.VMEM)
    return pl.pallas_call(
        body,
        out_shape=jax.ShapeDtypeStruct((slices_n + 1, rows_n, cols_n // parts_n), jnp.float32),
        in_specs=[pl.BlockSpec(memory_space=pltpu.SMEM)] + [vmem] * (parts_n + 2),
        out_specs=vmem,
        scratch_shapes=[
            pltpu.VMEM((rows_n, slices_n, cols_n // parts_n), jnp.float32),
            pltpu.SMEM((2 * parts_n * views_n,), jnp.float32),
            pltpu.SMEM((parts_n * views_n,), jnp.int32),
        ],
        name="gather_views",
    )(ints, tv, curv, *pieces)


def finish_kernel(parts_n, order_ref, factor_ref, vol_ref, *rest):
    pieces = rest[:parts_n]
    out_ref = rest[parts_n]
    factor = factor_ref[0]
    slices_n, _, per_n = pieces[0].shape
    for r in range(parts_n):
        cols = pl.ds(pl.multiple_of(order_ref[r] * per_n, per_n), per_n)
        out_ref[:, :, cols] = vol_ref[:, :, cols] - factor * pieces[r][0 : slices_n - 1]


def finish(order, factor, volume, pieces):
    parts_n = len(pieces)
    vmem = pl.BlockSpec(memory_space=pltpu.VMEM)
    smem = pl.BlockSpec(memory_space=pltpu.SMEM)
    return pl.pallas_call(
        lambda *refs: finish_kernel(parts_n, *refs),
        out_shape=jax.ShapeDtypeStruct(volume.shape, volume.dtype),
        in_specs=[smem, smem] + [vmem] * (parts_n + 1),
        out_specs=vmem,
        name="finish",
    )(order, factor, volume, *pieces)


def swapped(x, axis, bit):
    return lax.ppermute(x, axis, [(i, i ^ bit) for i in range(lax.axis_size(axis))])


def gathered(piece):
    part = lax.axis_index("view")
    depth = part // 2
    end = (depth == 0) | (depth == 3)

    def along(x, pairs):
        return lax.ppermute(x, "view", [(2 * a + y, 2 * b + y) for a, b in pairs for y in (0, 1)])

    first = swapped(piece, "view", 1)
    second = along(piece, [(0, 1), (1, 0), (2, 3), (3, 2)])
    middle = along(piece, [(1, 2), (2, 1)])
    across = [first, swapped(second, "view", 1)]
    onward = along(middle, [(1, 0), (2, 3)])
    middle_last = along(second, [(1, 2), (2, 1)])
    third = jnp.where(end, onward, middle)
    across.append(swapped(third, "view", 1))
    last = jnp.where(end, along(middle_last, [(1, 0), (2, 3)]), middle_last)
    across.append(swapped(last, "view", 1))
    upper = depth // 2
    depths = [depth, depth ^ 1, 2 - upper, 3 - 3 * upper]
    order = jnp.stack([2 * d + part % 2 for d in depths] + [2 * d + 1 - part % 2 for d in depths])
    return order.astype(jnp.int32), [piece, second, third, last] + across


def local_split(volume, sinogram, curvature, angles, offsets):
    slices_n, rows_n, cols_n = volume.shape
    views_n = angles.shape[0]
    bins_n = sinogram.shape[2]
    base, blocks = extent(rows_n, cols_n, bins_n)
    dims = (rows_n, cols_n, bins_n, base, blocks)
    slab_count = lax.axis_size("slab")
    parts_n = lax.axis_size("view")
    slab = lax.axis_index("slab")
    part = lax.axis_index("view")
    per_n = cols_n // parts_n

    angle_rad = angles.astype(jnp.float32) * (2.0 * math.pi / ROTATION_VIEWS)
    trig = jnp.concatenate([jnp.cos(angle_rad), jnp.sin(angle_rad)])

    def outer(at):
        face = lax.dynamic_slice(volume, (at, 0, part * per_n), (1, rows_n, per_n))
        return face.reshape(1, 1, slices_n, LANES)

    measured = sinogram[:, :, base : base + blocks * LANES]
    measured = measured.reshape(views_n, slices_n, blocks, LANES).transpose(0, 2, 1, 3)
    faces = jnp.concatenate([outer(0), outer(slices_n - 1)], axis=0)
    measured = jnp.concatenate([measured, faces], axis=1)
    cross_rows = swapped(measured, "slab", 2)
    pair_rows = swapped(measured, "slab", 1)
    trig, measured = lax.optimization_barrier((trig, measured))
    proj = project(trig, volume, bins_n, base, blocks, views_n)
    cross_pair_rows = swapped(cross_rows, "slab", 1)
    cross = swapped(proj, "slab", 2)
    near = swapped(proj, "slab", 1)
    cross_pair = swapped(cross, "slab", 1)

    def of(k):
        return lax.dynamic_index_in_dim(offsets, k, 1, keepdims=False)

    start = of(slab)
    shifts = [slices_n + jnp.clip(start - of(slab ^ k), -slices_n, slices_n) for k in (1, 2, 3)]
    table = jnp.stack([start] + shifts, axis=1).reshape(-1)
    ints = jnp.concatenate([jnp.stack([slab, part]).astype(jnp.int32), table])
    windows = residual_windows(
        dims,
        parts_n,
        ints,
        trig,
        [proj, near, cross, cross_pair, measured, pair_rows, cross_rows, cross_pair_rows],
    )
    pieces = [windows[0]] + [swapped(windows[r], "view", r) for r in range(1, parts_n)]
    def face_of(rows, which):
        return rows[which, blocks].reshape(1, rows_n, per_n)

    odd = slab % 2 == 1
    below = jnp.where(odd, face_of(pair_rows, 1), jnp.where(slab == 0, 0.0, face_of(cross_pair_rows, 1)))
    above = jnp.where(odd, jnp.where(slab == slab_count - 1, 0.0, face_of(cross_pair_rows, 0)), face_of(pair_rows, 0))
    wide = jnp.pad(volume, ((0, 0), (0, 0), (1, 1)))
    block = lax.dynamic_slice_in_dim(wide, part * per_n, per_n + 2, axis=2)
    sides = ((0, 0), (0, 0), (1, 1))
    block = jnp.concatenate([jnp.pad(below, sides), block, jnp.pad(above, sides)], axis=0)
    tv_grad = tv_padded(jnp.pad(block, ((0, 0), (1, 1), (0, 0))))
    curv = lax.dynamic_slice_in_dim(curvature, part * per_n, per_n, axis=2)
    tv = (tv_weight * tv_grad).transpose(1, 0, 2)
    order, parts = gathered(gather_views(dims, parts_n, ints, tv, curv.transpose(1, 0, 2), pieces))
    sums = [p[slices_n, 0, 0] for p in parts]
    while len(sums) > 1:
        sums = [a + b for a, b in zip(sums[0::2], sums[1::2])]
    squares = sums[0].reshape(1, 1)
    squares = squares + swapped(squares, "slab", 1) + (swapped(squares, "slab", 2) + swapped(squares, "slab", 3))
    voxel_count = slices_n * slab_count * rows_n * cols_n
    factor = jnp.minimum(1.0, step_limit / jnp.sqrt(squares / voxel_count + epsilon))
    return finish(order, factor.reshape(1), volume, parts)


def local(volume, sinogram, curvature, angles, offsets):
    shape = (lax.axis_size("slab"), lax.axis_size("view"), angles.shape[0])
    if shape == (4, 8, 2):
        return local_split(volume, sinogram, curvature, angles, offsets)
    return local_any(volume, sinogram, curvature, angles, offsets)


def solution(mesh):
    in_specs = (
        P("slab", None, None),
        P("view", "slab", None),
        P("slab", None, None),
        P("view"),
        P("view", None),
    )
    out_specs = P("slab", None, None)
    return jax.shard_map(local, mesh=mesh, in_specs=in_specs, out_specs=out_specs, check_vma=False)
```

```python
import math
import jax
import jax.numpy as jnp
from jax import lax
from jax.experimental import pallas as pl
from jax.experimental.pallas import tpu as pltpu
from jax.sharding import PartitionSpec as P

ROTATION_VIEWS = 1152


huber_delta = 0.5
tv_weight = 4.0
step_limit = 1.0
epsilon = 1e-06
scale = 0.7
LANES = 128
GROUP = 32


def coordinate(across, along, cos, sin, bins_n):
    return scale * (across * cos + along * sin) + 0.5 * bins_n - 0.5


def window_of(start, cos, sin, along, cols_n, bins_n, base):
    first = coordinate(start - 0.5 * cols_n + 0.5, along, cos, sin, bins_n)
    last = coordinate(start + (LANES - 1.0) - 0.5 * cols_n + 0.5, along, cos, sin, bins_n)
    return jnp.minimum(first, last).astype(jnp.int32) - (base + 1)


def project_kernel(cols_n, rows_n, bins_n, base, blocks_n, views_n, trig_ref, vol_ref, out_ref, rows_ref, acc_ref, sem):
    copies = [pltpu.make_async_copy(vol_ref.at[:, i, :], rows_ref.at[i], sem.at[i]) for i in range(rows_n)]
    for c in copies:
        c.start()
    acc_ref[...] = jnp.zeros_like(acc_ref)
    lane8 = lax.broadcasted_iota(jnp.int32, (8, LANES), 1)
    lane = lax.broadcasted_iota(jnp.int32, (16, LANES), 1)
    sub = lax.broadcasted_iota(jnp.int32, (LANES, LANES), 0).astype(jnp.float32).astype(jnp.bfloat16)
    zero = jnp.zeros((LANES, LANES), jnp.bfloat16)

    def tall(x):
        return jnp.concatenate([jnp.concatenate([x, x], 0).astype(jnp.bfloat16)] * (LANES // 16), 0)

    for row in range(rows_n):
        copies[row].wait()
        along = row - 0.5 * rows_n + 0.5

        def step(g, _):
            outs = []
            for u in range(GROUP):
                block = g * GROUP + u
                start = (block * LANES).astype(jnp.float32)
                vals = rows_ref[row, :, pl.ds(pl.multiple_of(block * LANES, LANES), LANES)]
                high = vals.astype(jnp.bfloat16)
                rest = vals - high.astype(jnp.float32)
                mid = rest.astype(jnp.bfloat16)
                low = (rest - mid.astype(jnp.float32)).astype(jnp.bfloat16)
                terms = jnp.concatenate([high, mid, low], 0)
                mats = []
                wins = []
                for v in range(views_n):
                    cos = trig_ref[v]
                    sin = trig_ref[views_n + v]
                    across = (lane8 + block * LANES).astype(jnp.float32) - 0.5 * cols_n + 0.5
                    coord = coordinate(across, along, cos, sin, bins_n)
                    lower = jnp.floor(coord)
                    frac = coord - lower
                    rel = lower - float(base)
                    bm = rel - LANES * jnp.floor(rel * (1.0 / LANES))
                    bn = jnp.where(bm == LANES - 1.0, 0.0, bm + 1.0)
                    fh = jnp.floor(frac * 128.0) * (1.0 / 128.0)
                    fl = frac - fh
                    here = sub == tall(bm)
                    next_ = sub == tall(bn)
                    wh = jnp.where(here, tall(1.0 - fh), jnp.where(next_, tall(fh), zero))
                    wl = jnp.where(here, tall(-fl), jnp.where(next_, tall(fl), zero))
                    mats.append(jnp.concatenate([wh, wl], 1))
                    wins.append(window_of(start, cos, sin, along, cols_n, bins_n, base))
                weights = jnp.concatenate(mats, 0)
                both = jnp.concatenate([terms, terms], 1)
                prod = lax.dot_general(both, weights, (((1,), (1,)), ((), ())), preferred_element_type=jnp.float32)
                outs.append((prod[0:16] + prod[16:32] + prod[32:48], wins))
            for summed, wins in outs:
                for v in range(views_n):
                    first = wins[v]
                    k = first >> 7
                    own = lane >= (first & (LANES - 1))
                    part = summed[:, v * LANES:(v + 1) * LANES]
                    acc_ref[v, k] += jnp.where(own, part, 0.0)
                    acc_ref[v, k + 1] += jnp.where(own, 0.0, part)
            return 0

        lax.fori_loop(0, cols_n // LANES // GROUP, step, 0)
    out_ref[...] = acc_ref[:, :blocks_n]


def project(trig, volume, bins_n, base, blocks_n, views_n):
    slices_n, rows_n, cols_n = volume.shape
    body = lambda *refs: project_kernel(cols_n, rows_n, bins_n, base, blocks_n, views_n, *refs)
    return pl.pallas_call(
        body,
        out_shape=jax.ShapeDtypeStruct((views_n, blocks_n, slices_n, LANES), jnp.float32),
        in_specs=[pl.BlockSpec(memory_space=pltpu.SMEM), pl.BlockSpec(memory_space=pl.ANY)],
        out_specs=pl.BlockSpec(memory_space=pltpu.VMEM),
        scratch_shapes=[
            pltpu.VMEM((rows_n, slices_n, cols_n), jnp.float32),
            pltpu.VMEM((views_n, blocks_n + 1, slices_n, LANES), jnp.float32),
            pltpu.SemaphoreType.DMA((rows_n,)),
        ],
        name="project",
    )(trig, volume)


def backproject_kernel(cols_n, rows_n, bins_n, base, views_n, width, per_n, trig_ref, starts_ref, res_ref, out_ref):
    lane16 = lax.broadcasted_iota(jnp.int32, (16, LANES), 1)
    pixel0 = starts_ref[views_n]

    def row_step(row, _):
        along = row.astype(jnp.float32) - 0.5 * rows_n + 0.5

        def step(u, _):
            column = pixel0 + u * LANES
            start = column.astype(jnp.float32)
            across = (lane16 + column).astype(jnp.float32) - 0.5 * cols_n + 0.5
            total = jnp.zeros((16, LANES), jnp.float32)
            for v in range(views_n):
                cos = trig_ref[v]
                sin = trig_ref[views_n + v]
                coord = coordinate(across, along, cos, sin, bins_n)
                lower = jnp.floor(coord)
                frac = coord - lower
                offset = starts_ref[v]
                rel = lower.astype(jnp.int32) - (base + offset)
                here = rel & (LANES - 1)
                next_ = (rel + 1) & (LANES - 1)
                first = window_of(start, cos, sin, along, cols_n, bins_n, base) - offset
                k = first >> 7
                left = res_ref[v, k]
                right = res_ref[v, jnp.minimum(k + 1, width - 1)]
                band = jnp.where(lane16 >= (first & (LANES - 1)), left, right)
                a = jnp.take_along_axis(band, here, axis=1, mode="promise_in_bounds")
                b = jnp.take_along_axis(band, next_, axis=1, mode="promise_in_bounds")
                total = total + (a * (1.0 - frac) + b * frac)
            out_ref[row, :, pl.ds(pl.multiple_of(u * LANES, LANES), LANES)] = total
            return 0

        lax.fori_loop(0, per_n // LANES, step, 0)
        return 0

    lax.fori_loop(0, rows_n, row_step, 0)


def backproject(trig, starts, res, rows_n, cols_n, bins_n, base, per_n):
    views_n, width, slices_n, _ = res.shape
    body = lambda *refs: backproject_kernel(cols_n, rows_n, bins_n, base, views_n, width, per_n, *refs)
    return pl.pallas_call(
        body,
        out_shape=jax.ShapeDtypeStruct((rows_n, slices_n, per_n), jnp.float32),
        in_specs=[pl.BlockSpec(memory_space=pltpu.SMEM), pl.BlockSpec(memory_space=pltpu.SMEM), pl.BlockSpec(memory_space=pltpu.VMEM)],
        out_specs=pl.BlockSpec(memory_space=pltpu.VMEM),
        name="backproject",
    )(trig, starts, res)


def padded_2(cells, sides, width):
    for axis, dim in sides:
        count = lax.axis_size(axis)
        ends = count - 1
        head = lax.slice_in_dim(cells, 0, width, axis=dim)
        tail = lax.slice_in_dim(cells, cells.shape[dim] - width, cells.shape[dim], axis=dim)
        cells = jnp.concatenate(
            [
                lax.ppermute(tail, axis, [(i, (i + 1) % count) for i in range(ends)]),
                cells,
                lax.ppermute(head, axis, [((i + 1) % count, i) for i in range(ends)]),
            ],
            axis=dim,
        )
    return cells


def slope(diff):
    return jnp.clip(diff / huber_delta, -1.0, 1.0)


def tv_padded(padded):
    centre = padded[1:-1, 1:-1, 1:-1]
    result = slope(centre - padded[:-2, 1:-1, 1:-1]) - slope(padded[2:, 1:-1, 1:-1] - centre)
    result = (
        result + slope(centre - padded[1:-1, :-2, 1:-1]) - slope(padded[1:-1, 2:, 1:-1] - centre)
    )
    result = (
        result + slope(centre - padded[1:-1, 1:-1, :-2]) - slope(padded[1:-1, 1:-1, 2:] - centre)
    )
    return result


def extent(rows_n, cols_n, bins_n):
    reach = scale * math.hypot(0.5 * (cols_n - 1), 0.5 * (rows_n - 1))
    centre = 0.5 * bins_n - 0.5
    base = (int(centre - reach) - 3) // 8 * 8
    blocks = -(-(int(centre + reach) + 3 - base) // LANES)
    return base, blocks


def local_any(volume, sinogram, curvature, angles, offsets):
    slices_n, rows_n, cols_n = volume.shape
    views_n = angles.shape[0]
    bins_n = sinogram.shape[2]
    base, blocks = extent(rows_n, cols_n, bins_n)
    pixels_n = rows_n * cols_n
    slab_count = lax.axis_size("slab")
    all_rows = sinogram.shape[1] * slab_count
    slab_pos = lax.axis_index("slab")
    angle_rad = angles.astype(jnp.float32) * (2.0 * math.pi / ROTATION_VIEWS)
    trig = jnp.concatenate([jnp.cos(angle_rad), jnp.sin(angle_rad)])
    proj = project(trig, volume, bins_n, base, blocks, views_n)
    stacked = []
    bands = []
    for v in range(views_n):
        start = lax.dynamic_index_in_dim(offsets[v], slab_pos, 0, keepdims=False)
        flat = proj[v].transpose(1, 0, 2).reshape(slices_n, blocks * LANES)
        stacked.append(
            lax.dynamic_update_slice(
                jnp.zeros((all_rows, blocks * LANES), jnp.float32), flat, (start, jnp.int32(0))
            )
        )
        bands.append(start)
    own = lax.psum_scatter(jnp.stack(stacked), "slab", scatter_dimension=1, tiled=True)
    measured = sinogram[:, :, base : base + blocks * LANES]
    residual = lax.all_gather(own - measured, "slab", axis=1, tiled=True)
    windows = jnp.stack(
        [
            lax.dynamic_slice(
                residual[v], (bands[v], jnp.int32(0)), (slices_n, blocks * LANES)
            )
            .reshape(slices_n, blocks, LANES)
            .transpose(1, 0, 2)
            for v in range(views_n)
        ]
    )
    starts = jnp.zeros((views_n + 1,), jnp.int32)
    data_local = backproject(trig, starts, windows, rows_n, cols_n, bins_n, base, cols_n)
    extended = padded_2(volume, (("slab", 0),), 1)
    padded = jnp.pad(extended, ((0, 0), (1, 1), (1, 1)))
    tv_grad = tv_padded(padded)
    data_grad = lax.psum(data_local, "view").transpose(1, 0, 2)
    direction = (data_grad + tv_weight * tv_grad) / curvature
    squares = lax.psum(jnp.sum(direction * direction), "slab")
    voxel_count = slices_n * slab_count * pixels_n
    factor = jnp.minimum(1.0, step_limit / jnp.sqrt(squares / voxel_count + epsilon))
    return volume - factor * direction


WINDOW = 3
COS_LANE = LANES - 2
SIN_LANE = LANES - 1


def window_start(part, per_n, cos, sin, rows_n, cols_n, bins_n, base, blocks):
    low = None
    for row in (0, rows_n - 1):
        along = row - 0.5 * rows_n + 0.5
        for edge in (0.0, per_n - 1.0):
            across = (part * per_n).astype(jnp.float32) + edge - 0.5 * cols_n + 0.5
            t = coordinate(across, along, cos, sin, bins_n)
            low = t if low is None else jnp.minimum(low, t)
    first = low.astype(jnp.int32) - (base + 1)
    return jnp.clip(first, 0, (blocks - WINDOW) * LANES)


def residual_kernel(dims, parts_n, ints_ref, trig_ref, *rest):
    rows_n, cols_n, bins_n, base, blocks = dims
    projs, sinos, outs = rest[:4], rest[4:8], rest[8 : 8 + parts_n]
    pads = rest[8 + parts_n : 11 + parts_n]
    sino, res = rest[11 + parts_n :]
    views_n, _, band, _ = projs[0].shape
    slab, part = ints_ref[0], ints_ref[1]
    for other in range(1, 4):
        pad = pads[other - 1]
        pad[:, :, 0:band] = jnp.zeros((views_n, blocks, band, LANES), jnp.float32)
        pad[:, :, 2 * band :] = jnp.zeros((views_n, blocks, band, LANES), jnp.float32)
        pad[:, :, band : 2 * band] = projs[other][...]
    for other in range(4):
        rows = pl.ds(pl.multiple_of((slab ^ other) * band, band), band)
        sino[:, :, rows] = sinos[other][:, 0:blocks]
    for v in range(views_n):
        value = projs[0][v]
        for other in range(1, 4):
            value = value + pads[other - 1][v, :, pl.ds(ints_ref[2 + 4 * v + other], band), :]
        res[v, 0:blocks] = value - sino[v, :, pl.ds(ints_ref[2 + 4 * v], band), :]
        res[v, blocks] = jnp.zeros((band, LANES), jnp.float32)
    lane = lax.broadcasted_iota(jnp.int32, (band, LANES), 1)
    per_n = cols_n // parts_n
    for r in range(parts_n):
        for v in range(views_n):
            cos, sin = trig_ref[v], trig_ref[views_n + v]
            first = window_start(part ^ r, per_n, cos, sin, rows_n, cols_n, bins_n, base, blocks)
            k = first >> 7
            shift = first & (LANES - 1)
            turned = [pltpu.roll(res[v, k + m], (LANES - shift) & (LANES - 1), 1) for m in range(WINDOW + 1)]
            for m in range(WINDOW):
                value = jnp.where(lane < LANES - shift, turned[m], turned[m + 1])
                if m == WINDOW - 1:
                    value = jnp.where(lane == COS_LANE, cos, jnp.where(lane == SIN_LANE, sin, value))
                outs[r][v, m] = value


def residual_windows(dims, parts_n, ints, trig, arrays):
    views_n, blocks, band, _ = arrays[0].shape
    body = lambda *refs: residual_kernel(dims, parts_n, *refs)
    vmem = pl.BlockSpec(memory_space=pltpu.VMEM)
    smem = pl.BlockSpec(memory_space=pltpu.SMEM)
    return pl.pallas_call(
        body,
        out_shape=[jax.ShapeDtypeStruct((views_n, WINDOW, band, LANES), jnp.float32)] * parts_n,
        in_specs=[smem, smem] + [vmem] * len(arrays),
        out_specs=[vmem] * parts_n,
        scratch_shapes=[
            pltpu.VMEM((views_n, blocks, 3 * band, LANES), jnp.float32),
            pltpu.VMEM((views_n, blocks, 3 * band, LANES), jnp.float32),
            pltpu.VMEM((views_n, blocks, 3 * band, LANES), jnp.float32),
            pltpu.VMEM((views_n, blocks, 4 * band, LANES), jnp.float32),
            pltpu.VMEM((views_n, blocks + 1, band, LANES), jnp.float32),
        ],
        name="residual_windows",
    )(ints, trig, *arrays)


def gather_kernel(dims, parts_n, views_n, ints_ref, tv_ref, curv_ref, *rest):
    rows_n, cols_n, bins_n, base, blocks = dims
    pieces = rest[:parts_n]
    out_ref, rows_ref, trig_ref, starts_ref = rest[parts_n:]
    per_n = cols_n // parts_n
    part = ints_ref[1]
    lane8 = lax.broadcasted_iota(jnp.int32, (8, LANES), 1)
    lane = lax.broadcasted_iota(jnp.int32, (16, LANES), 1)
    total_n = parts_n * views_n
    for n in range(total_n):
        tagged = pieces[n // views_n][n % views_n, WINDOW - 1, 0:8, :]
        cos = jnp.max(jnp.where(lane8 == COS_LANE, tagged, -2.0))
        sin = jnp.max(jnp.where(lane8 == SIN_LANE, tagged, -2.0))
        trig_ref[n] = cos
        trig_ref[total_n + n] = sin
        starts_ref[n] = window_start(part, per_n, cos, sin, rows_n, cols_n, bins_n, base, blocks)

    def step(index, squares):
        row = index // (per_n // LANES)
        u = index - row * (per_n // LANES)
        along = row.astype(jnp.float32) - 0.5 * rows_n + 0.5
        column = part * per_n + u * LANES
        start = column.astype(jnp.float32)
        across = (lane + column).astype(jnp.float32) - 0.5 * cols_n + 0.5
        total = jnp.zeros((16, LANES), jnp.float32)
        for n in range(total_n):
            cos = trig_ref[n]
            sin = trig_ref[total_n + n]
            offset = starts_ref[n]
            coord = coordinate(across, along, cos, sin, bins_n)
            lower = jnp.floor(coord)
            frac = coord - lower
            rel = lower.astype(jnp.int32) - (base + offset)
            here = rel & (LANES - 1)
            next_ = (rel + 1) & (LANES - 1)
            first = jnp.maximum(window_of(start, cos, sin, along, cols_n, bins_n, base) - offset, 0)
            k = jnp.minimum(first >> 7, WINDOW - 1)
            windows = pieces[n // views_n]
            left = windows[n % views_n, k]
            right = windows[n % views_n, jnp.minimum(k + 1, WINDOW - 1)]
            held = jnp.where(lane >= (first & (LANES - 1)), left, right)
            a = jnp.take_along_axis(held, here, axis=1, mode="promise_in_bounds")
            b = jnp.take_along_axis(held, next_, axis=1, mode="promise_in_bounds")
            total = total + (a * (1.0 - frac) + b * frac)
        cols = pl.ds(pl.multiple_of(u * LANES, LANES), LANES)
        total = (total + tv_ref[row, :, cols]) / curv_ref[row, :, cols]
        rows_ref[row, :, cols] = total
        return squares + total * total

    squares = lax.fori_loop(0, rows_n * (per_n // LANES), step, jnp.zeros((16, LANES), jnp.float32))
    for row in range(rows_n):
        out_ref[0:16, row, :] = rows_ref[row]
    out_ref[16] = jnp.full((rows_n, per_n), jnp.sum(squares), jnp.float32)


def gather_views(dims, parts_n, ints, tv, curv, pieces):
    views_n, _, slices_n, _ = pieces[0].shape
    rows_n, cols_n = dims[:2]
    body = lambda *refs: gather_kernel(dims, parts_n, views_n, *refs)
    vmem = pl.BlockSpec(memory_space=pltpu.VMEM)
    return pl.pallas_call(
        body,
        out_shape=jax.ShapeDtypeStruct((slices_n + 1, rows_n, cols_n // parts_n), jnp.float32),
        in_specs=[pl.BlockSpec(memory_space=pltpu.SMEM)] + [vmem] * (parts_n + 2),
        out_specs=vmem,
        scratch_shapes=[
            pltpu.VMEM((rows_n, slices_n, cols_n // parts_n), jnp.float32),
            pltpu.SMEM((2 * parts_n * views_n,), jnp.float32),
            pltpu.SMEM((parts_n * views_n,), jnp.int32),
        ],
        name="gather_views",
    )(ints, tv, curv, *pieces)


def total_kernel(*refs):
    sums = [ref[0, 0:1, :] for ref in refs[:-1]]
    while len(sums) > 1:
        sums = [a + b for a, b in zip(sums[0::2], sums[1::2])]
    refs[-1][...] = sums[0]


def total(pieces):
    slices_n, rows_n, _ = pieces[0].shape
    last = pl.BlockSpec((1, rows_n, LANES), lambda i: (slices_n - 1, 0, 0))
    return pl.pallas_call(
        total_kernel,
        grid=(1,),
        out_shape=jax.ShapeDtypeStruct((1, LANES), jnp.float32),
        in_specs=[last] * len(pieces),
        out_specs=pl.BlockSpec((1, LANES), lambda i: (0, 0)),
        name="total",
    )(*pieces)


def finish_kernel(parts_n, voxel_count, ints_ref, *rest):
    sums, vol_ref, pieces = rest[:4], rest[4], rest[5 : 5 + parts_n]
    out_ref = rest[5 + parts_n]
    squares = sums[0][...] + sums[1][...] + (sums[2][...] + sums[3][...])
    rms = jnp.sqrt(squares / float(voxel_count) + epsilon)
    factor = jnp.max(jnp.minimum(1.0, step_limit / rms))
    slices_n, _, per_n = pieces[0].shape
    part = ints_ref[1]
    depth = part >> 1
    upper = depth >> 1
    side = part & 1
    depths = [depth, depth ^ 1, 2 - upper, 3 - 3 * upper]
    order = [2 * d + side for d in depths] + [2 * d + 1 - side for d in depths]
    for r in range(parts_n):
        cols = pl.ds(pl.multiple_of(order[r] * per_n, per_n), per_n)
        out_ref[:, :, cols] = vol_ref[:, :, cols] - factor * pieces[r][0 : slices_n - 1]


def finish(voxel_count, ints, sums, volume, pieces):
    parts_n = len(pieces)
    vmem = pl.BlockSpec(memory_space=pltpu.VMEM)
    smem = pl.BlockSpec(memory_space=pltpu.SMEM)
    return pl.pallas_call(
        lambda *refs: finish_kernel(parts_n, voxel_count, *refs),
        out_shape=jax.ShapeDtypeStruct(volume.shape, volume.dtype),
        in_specs=[smem] + [vmem] * (parts_n + 5),
        out_specs=vmem,
        name="finish",
    )(ints, *sums, volume, *pieces)


def swapped(x, axis, bit):
    return lax.ppermute(x, axis, [(i, i ^ bit) for i in range(lax.axis_size(axis))])


def gathered(piece):
    part = lax.axis_index("view")
    depth = part // 2
    end = (depth == 0) | (depth == 3)

    def along(x, pairs):
        return lax.ppermute(x, "view", [(2 * a + y, 2 * b + y) for a, b in pairs for y in (0, 1)])

    first = swapped(piece, "view", 1)
    second = along(piece, [(0, 1), (1, 0), (2, 3), (3, 2)])
    middle = along(piece, [(1, 2), (2, 1)])
    across = [first, swapped(second, "view", 1)]
    onward = along(middle, [(1, 0), (2, 3)])
    middle_last = along(second, [(1, 2), (2, 1)])
    third = jnp.where(end, onward, middle)
    across.append(swapped(third, "view", 1))
    last = jnp.where(end, along(middle_last, [(1, 0), (2, 3)]), middle_last)
    across.append(swapped(last, "view", 1))
    return [piece, second, third, last] + across


def local_split(volume, sinogram, curvature, angles, offsets):
    slices_n, rows_n, cols_n = volume.shape
    views_n = angles.shape[0]
    bins_n = sinogram.shape[2]
    base, blocks = extent(rows_n, cols_n, bins_n)
    dims = (rows_n, cols_n, bins_n, base, blocks)
    slab_count = lax.axis_size("slab")
    parts_n = lax.axis_size("view")
    slab = lax.axis_index("slab")
    part = lax.axis_index("view")
    per_n = cols_n // parts_n

    angle_rad = angles.astype(jnp.float32) * (2.0 * math.pi / ROTATION_VIEWS)
    trig = jnp.concatenate([jnp.cos(angle_rad), jnp.sin(angle_rad)])

    def outer(at):
        face = lax.dynamic_slice(volume, (at, 0, part * per_n), (1, rows_n, per_n))
        return face.reshape(1, 1, slices_n, LANES)

    measured = sinogram[:, :, base : base + blocks * LANES]
    measured = measured.reshape(views_n, slices_n, blocks, LANES).transpose(0, 2, 1, 3)
    faces = jnp.concatenate([outer(0), outer(slices_n - 1)], axis=0)
    measured = jnp.concatenate([measured, faces], axis=1)
    cross_rows = swapped(measured, "slab", 2)
    pair_rows = swapped(measured, "slab", 1)
    trig, measured = lax.optimization_barrier((trig, measured))
    proj = project(trig, volume, bins_n, base, blocks, views_n)
    cross_pair_rows = swapped(cross_rows, "slab", 1)
    cross = swapped(proj, "slab", 2)
    near = swapped(proj, "slab", 1)
    cross_pair = swapped(cross, "slab", 1)

    def of(k):
        return lax.dynamic_index_in_dim(offsets, k, 1, keepdims=False)

    start = of(slab)
    shifts = [slices_n + jnp.clip(start - of(slab ^ k), -slices_n, slices_n) for k in (1, 2, 3)]
    table = jnp.stack([start] + shifts, axis=1).reshape(-1)
    ints = jnp.concatenate([jnp.stack([slab, part]).astype(jnp.int32), table])
    windows = residual_windows(
        dims,
        parts_n,
        ints,
        trig,
        [proj, near, cross, cross_pair, measured, pair_rows, cross_rows, cross_pair_rows],
    )
    pieces = [windows[0]] + [swapped(windows[r], "view", r) for r in range(1, parts_n)]
    def face_of(rows, which):
        return rows[which, blocks].reshape(1, rows_n, per_n)

    odd = slab % 2 == 1
    below = jnp.where(odd, face_of(pair_rows, 1), jnp.where(slab == 0, 0.0, face_of(cross_pair_rows, 1)))
    above = jnp.where(odd, jnp.where(slab == slab_count - 1, 0.0, face_of(cross_pair_rows, 0)), face_of(pair_rows, 0))
    wide = jnp.pad(volume, ((0, 0), (0, 0), (1, 1)))
    block = lax.dynamic_slice_in_dim(wide, part * per_n, per_n + 2, axis=2)
    sides = ((0, 0), (0, 0), (1, 1))
    block = jnp.concatenate([jnp.pad(below, sides), block, jnp.pad(above, sides)], axis=0)
    tv_grad = tv_padded(jnp.pad(block, ((0, 0), (1, 1), (0, 0))))
    curv = lax.dynamic_slice_in_dim(curvature, part * per_n, per_n, axis=2)
    tv = (tv_weight * tv_grad).transpose(1, 0, 2)
    parts = gathered(gather_views(dims, parts_n, ints, tv, curv.transpose(1, 0, 2), pieces))
    squares = total(parts)
    sums = [squares] + [swapped(squares, "slab", k) for k in (1, 2, 3)]
    voxel_count = slices_n * slab_count * rows_n * cols_n
    return finish(voxel_count, ints, sums, volume, parts)


def local(volume, sinogram, curvature, angles, offsets):
    shape = (lax.axis_size("slab"), lax.axis_size("view"), angles.shape[0])
    if shape == (4, 8, 2):
        return local_split(volume, sinogram, curvature, angles, offsets)
    return local_any(volume, sinogram, curvature, angles, offsets)


def solution(mesh):
    in_specs = (
        P("slab", None, None),
        P("view", "slab", None),
        P("slab", None, None),
        P("view"),
        P("view", None),
    )
    out_specs = P("slab", None, None)
    return jax.shard_map(local, mesh=mesh, in_specs=in_specs, out_specs=out_specs, check_vma=False)
```

```python
import math
import jax
import jax.numpy as jnp
from jax import lax
from jax.experimental import pallas as pl
from jax.experimental.pallas import tpu as pltpu
from jax.sharding import PartitionSpec as P

ROTATION_VIEWS = 1152


huber_delta = 0.5
tv_weight = 4.0
step_limit = 1.0
epsilon = 1e-06
scale = 0.7
LANES = 128
GROUP = 32


def coordinate(across, along, cos, sin, bins_n):
    return scale * (across * cos + along * sin) + 0.5 * bins_n - 0.5


def window_of(start, cos, sin, along, cols_n, bins_n, base):
    first = coordinate(start - 0.5 * cols_n + 0.5, along, cos, sin, bins_n)
    last = coordinate(start + (LANES - 1.0) - 0.5 * cols_n + 0.5, along, cos, sin, bins_n)
    return jnp.minimum(first, last).astype(jnp.int32) - (base + 1)


def project_kernel(cols_n, rows_n, bins_n, base, blocks_n, views_n, trig_ref, vol_ref, out_ref, rows_ref, acc_ref, sem):
    copies = [pltpu.make_async_copy(vol_ref.at[:, i, :], rows_ref.at[i], sem.at[i]) for i in range(rows_n)]
    for c in copies:
        c.start()
    acc_ref[...] = jnp.zeros_like(acc_ref)
    lane8 = lax.broadcasted_iota(jnp.int32, (8, LANES), 1)
    lane = lax.broadcasted_iota(jnp.int32, (16, LANES), 1)
    sub = lax.broadcasted_iota(jnp.int32, (LANES, LANES), 0).astype(jnp.float32).astype(jnp.bfloat16)
    zero = jnp.zeros((LANES, LANES), jnp.bfloat16)

    def tall(x):
        return jnp.concatenate([jnp.concatenate([x, x], 0).astype(jnp.bfloat16)] * (LANES // 16), 0)

    for row in range(rows_n):
        copies[row].wait()
        along = row - 0.5 * rows_n + 0.5

        def step(g, _):
            outs = []
            for u in range(GROUP):
                block = g * GROUP + u
                start = (block * LANES).astype(jnp.float32)
                vals = rows_ref[row, :, pl.ds(pl.multiple_of(block * LANES, LANES), LANES)]
                high = vals.astype(jnp.bfloat16)
                rest = vals - high.astype(jnp.float32)
                mid = rest.astype(jnp.bfloat16)
                low = (rest - mid.astype(jnp.float32)).astype(jnp.bfloat16)
                terms = jnp.concatenate([high, mid, low], 0)
                mats = []
                wins = []
                for v in range(views_n):
                    cos = trig_ref[v]
                    sin = trig_ref[views_n + v]
                    across = (lane8 + block * LANES).astype(jnp.float32) - 0.5 * cols_n + 0.5
                    coord = coordinate(across, along, cos, sin, bins_n)
                    lower = jnp.floor(coord)
                    frac = coord - lower
                    rel = lower - float(base)
                    bm = rel - LANES * jnp.floor(rel * (1.0 / LANES))
                    bn = jnp.where(bm == LANES - 1.0, 0.0, bm + 1.0)
                    fh = jnp.floor(frac * 128.0) * (1.0 / 128.0)
                    fl = frac - fh
                    here = sub == tall(bm)
                    next_ = sub == tall(bn)
                    wh = jnp.where(here, tall(1.0 - fh), jnp.where(next_, tall(fh), zero))
                    wl = jnp.where(here, tall(-fl), jnp.where(next_, tall(fl), zero))
                    mats.append(jnp.concatenate([wh, wl], 1))
                    wins.append(window_of(start, cos, sin, along, cols_n, bins_n, base))
                weights = jnp.concatenate(mats, 0)
                both = jnp.concatenate([terms, terms], 1)
                prod = lax.dot_general(both, weights, (((1,), (1,)), ((), ())), preferred_element_type=jnp.float32)
                outs.append((prod[0:16] + prod[16:32] + prod[32:48], wins))
            for summed, wins in outs:
                for v in range(views_n):
                    first = wins[v]
                    k = first >> 7
                    own = lane >= (first & (LANES - 1))
                    part = summed[:, v * LANES:(v + 1) * LANES]
                    acc_ref[v, k] += jnp.where(own, part, 0.0)
                    acc_ref[v, k + 1] += jnp.where(own, 0.0, part)
            return 0

        lax.fori_loop(0, cols_n // LANES // GROUP, step, 0)
    out_ref[...] = acc_ref[:, :blocks_n]


def project(trig, volume, bins_n, base, blocks_n, views_n):
    slices_n, rows_n, cols_n = volume.shape
    body = lambda *refs: project_kernel(cols_n, rows_n, bins_n, base, blocks_n, views_n, *refs)
    return pl.pallas_call(
        body,
        out_shape=jax.ShapeDtypeStruct((views_n, blocks_n, slices_n, LANES), jnp.float32),
        in_specs=[pl.BlockSpec(memory_space=pltpu.SMEM), pl.BlockSpec(memory_space=pl.ANY)],
        out_specs=pl.BlockSpec(memory_space=pltpu.VMEM),
        scratch_shapes=[
            pltpu.VMEM((rows_n, slices_n, cols_n), jnp.float32),
            pltpu.VMEM((views_n, blocks_n + 1, slices_n, LANES), jnp.float32),
            pltpu.SemaphoreType.DMA((rows_n,)),
        ],
        name="project",
    )(trig, volume)


def backproject_kernel(cols_n, rows_n, bins_n, base, views_n, width, per_n, trig_ref, starts_ref, res_ref, out_ref):
    lane16 = lax.broadcasted_iota(jnp.int32, (16, LANES), 1)
    pixel0 = starts_ref[views_n]

    def row_step(row, _):
        along = row.astype(jnp.float32) - 0.5 * rows_n + 0.5

        def step(u, _):
            column = pixel0 + u * LANES
            start = column.astype(jnp.float32)
            across = (lane16 + column).astype(jnp.float32) - 0.5 * cols_n + 0.5
            total = jnp.zeros((16, LANES), jnp.float32)
            for v in range(views_n):
                cos = trig_ref[v]
                sin = trig_ref[views_n + v]
                coord = coordinate(across, along, cos, sin, bins_n)
                lower = jnp.floor(coord)
                frac = coord - lower
                offset = starts_ref[v]
                rel = lower.astype(jnp.int32) - (base + offset)
                here = rel & (LANES - 1)
                next_ = (rel + 1) & (LANES - 1)
                first = window_of(start, cos, sin, along, cols_n, bins_n, base) - offset
                k = first >> 7
                left = res_ref[v, k]
                right = res_ref[v, jnp.minimum(k + 1, width - 1)]
                band = jnp.where(lane16 >= (first & (LANES - 1)), left, right)
                a = jnp.take_along_axis(band, here, axis=1, mode="promise_in_bounds")
                b = jnp.take_along_axis(band, next_, axis=1, mode="promise_in_bounds")
                total = total + (a * (1.0 - frac) + b * frac)
            out_ref[row, :, pl.ds(pl.multiple_of(u * LANES, LANES), LANES)] = total
            return 0

        lax.fori_loop(0, per_n // LANES, step, 0)
        return 0

    lax.fori_loop(0, rows_n, row_step, 0)


def backproject(trig, starts, res, rows_n, cols_n, bins_n, base, per_n):
    views_n, width, slices_n, _ = res.shape
    body = lambda *refs: backproject_kernel(cols_n, rows_n, bins_n, base, views_n, width, per_n, *refs)
    return pl.pallas_call(
        body,
        out_shape=jax.ShapeDtypeStruct((rows_n, slices_n, per_n), jnp.float32),
        in_specs=[pl.BlockSpec(memory_space=pltpu.SMEM), pl.BlockSpec(memory_space=pltpu.SMEM), pl.BlockSpec(memory_space=pltpu.VMEM)],
        out_specs=pl.BlockSpec(memory_space=pltpu.VMEM),
        name="backproject",
    )(trig, starts, res)


def padded_2(cells, sides, width):
    for axis, dim in sides:
        count = lax.axis_size(axis)
        ends = count - 1
        head = lax.slice_in_dim(cells, 0, width, axis=dim)
        tail = lax.slice_in_dim(cells, cells.shape[dim] - width, cells.shape[dim], axis=dim)
        cells = jnp.concatenate(
            [
                lax.ppermute(tail, axis, [(i, (i + 1) % count) for i in range(ends)]),
                cells,
                lax.ppermute(head, axis, [((i + 1) % count, i) for i in range(ends)]),
            ],
            axis=dim,
        )
    return cells


def slope(diff):
    return jnp.clip(diff / huber_delta, -1.0, 1.0)


def tv_padded(padded):
    centre = padded[1:-1, 1:-1, 1:-1]
    result = slope(centre - padded[:-2, 1:-1, 1:-1]) - slope(padded[2:, 1:-1, 1:-1] - centre)
    result = (
        result + slope(centre - padded[1:-1, :-2, 1:-1]) - slope(padded[1:-1, 2:, 1:-1] - centre)
    )
    result = (
        result + slope(centre - padded[1:-1, 1:-1, :-2]) - slope(padded[1:-1, 1:-1, 2:] - centre)
    )
    return result


def extent(rows_n, cols_n, bins_n):
    reach = scale * math.hypot(0.5 * (cols_n - 1), 0.5 * (rows_n - 1))
    centre = 0.5 * bins_n - 0.5
    base = (int(centre - reach) - 3) // 8 * 8
    blocks = -(-(int(centre + reach) + 3 - base) // LANES)
    return base, blocks


def local_any(volume, sinogram, curvature, angles, offsets):
    slices_n, rows_n, cols_n = volume.shape
    views_n = angles.shape[0]
    bins_n = sinogram.shape[2]
    base, blocks = extent(rows_n, cols_n, bins_n)
    pixels_n = rows_n * cols_n
    slab_count = lax.axis_size("slab")
    all_rows = sinogram.shape[1] * slab_count
    slab_pos = lax.axis_index("slab")
    angle_rad = angles.astype(jnp.float32) * (2.0 * math.pi / ROTATION_VIEWS)
    trig = jnp.concatenate([jnp.cos(angle_rad), jnp.sin(angle_rad)])
    proj = project(trig, volume, bins_n, base, blocks, views_n)
    stacked = []
    bands = []
    for v in range(views_n):
        start = lax.dynamic_index_in_dim(offsets[v], slab_pos, 0, keepdims=False)
        flat = proj[v].transpose(1, 0, 2).reshape(slices_n, blocks * LANES)
        stacked.append(
            lax.dynamic_update_slice(
                jnp.zeros((all_rows, blocks * LANES), jnp.float32), flat, (start, jnp.int32(0))
            )
        )
        bands.append(start)
    own = lax.psum_scatter(jnp.stack(stacked), "slab", scatter_dimension=1, tiled=True)
    measured = sinogram[:, :, base : base + blocks * LANES]
    residual = lax.all_gather(own - measured, "slab", axis=1, tiled=True)
    windows = jnp.stack(
        [
            lax.dynamic_slice(
                residual[v], (bands[v], jnp.int32(0)), (slices_n, blocks * LANES)
            )
            .reshape(slices_n, blocks, LANES)
            .transpose(1, 0, 2)
            for v in range(views_n)
        ]
    )
    starts = jnp.zeros((views_n + 1,), jnp.int32)
    data_local = backproject(trig, starts, windows, rows_n, cols_n, bins_n, base, cols_n)
    extended = padded_2(volume, (("slab", 0),), 1)
    padded = jnp.pad(extended, ((0, 0), (1, 1), (1, 1)))
    tv_grad = tv_padded(padded)
    data_grad = lax.psum(data_local, "view").transpose(1, 0, 2)
    direction = (data_grad + tv_weight * tv_grad) / curvature
    squares = lax.psum(jnp.sum(direction * direction), "slab")
    voxel_count = slices_n * slab_count * pixels_n
    factor = jnp.minimum(1.0, step_limit / jnp.sqrt(squares / voxel_count + epsilon))
    return volume - factor * direction


WINDOW = 3
SLOTS = (0, 2, 4, 6, 1, 3, 5, 7)
COS_LANE = LANES - 2
SIN_LANE = LANES - 1


def window_start(part, per_n, cos, sin, rows_n, cols_n, bins_n, base, blocks):
    low = None
    for row in (0, rows_n - 1):
        along = row - 0.5 * rows_n + 0.5
        for edge in (0.0, per_n - 1.0):
            across = (part * per_n).astype(jnp.float32) + edge - 0.5 * cols_n + 0.5
            t = coordinate(across, along, cos, sin, bins_n)
            low = t if low is None else jnp.minimum(low, t)
    first = low.astype(jnp.int32) - (base + 1)
    return jnp.clip(first, 0, (blocks - WINDOW) * LANES)


def residual_kernel(dims, parts_n, ints_ref, trig_ref, *rest):
    rows_n, cols_n, bins_n, base, blocks = dims
    projs, sinos, outs = rest[:4], rest[4:8], rest[8 : 8 + parts_n]
    pads = rest[8 + parts_n : 11 + parts_n]
    sino, res = rest[11 + parts_n :]
    views_n, _, band, _ = projs[0].shape
    slab, part = ints_ref[0], ints_ref[1]
    for other in range(1, 4):
        pad = pads[other - 1]
        pad[:, :, 0:band] = jnp.zeros((views_n, blocks, band, LANES), jnp.float32)
        pad[:, :, 2 * band :] = jnp.zeros((views_n, blocks, band, LANES), jnp.float32)
        pad[:, :, band : 2 * band] = projs[other][...]
    for other in range(4):
        rows = pl.ds(pl.multiple_of((slab ^ other) * band, band), band)
        sino[:, :, rows] = sinos[other][:, 0:blocks]
    for v in range(views_n):
        value = projs[0][v]
        for other in range(1, 4):
            value = value + pads[other - 1][v, :, pl.ds(ints_ref[2 + 4 * v + other], band), :]
        res[v, 0:blocks] = value - sino[v, :, pl.ds(ints_ref[2 + 4 * v], band), :]
        res[v, blocks] = jnp.zeros((band, LANES), jnp.float32)
    lane = lax.broadcasted_iota(jnp.int32, (band, LANES), 1)
    per_n = cols_n // parts_n
    for r in range(parts_n):
        for v in range(views_n):
            cos, sin = trig_ref[v], trig_ref[views_n + v]
            first = window_start(part ^ r, per_n, cos, sin, rows_n, cols_n, bins_n, base, blocks)
            k = first >> 7
            shift = first & (LANES - 1)
            turned = [pltpu.roll(res[v, k + m], (LANES - shift) & (LANES - 1), 1) for m in range(WINDOW + 1)]
            for m in range(WINDOW):
                value = jnp.where(lane < LANES - shift, turned[m], turned[m + 1])
                if m == WINDOW - 1:
                    value = jnp.where(lane == COS_LANE, cos, jnp.where(lane == SIN_LANE, sin, value))
                outs[r][v, m] = value


def residual_windows(dims, parts_n, ints, trig, arrays):
    views_n, blocks, band, _ = arrays[0].shape
    body = lambda *refs: residual_kernel(dims, parts_n, *refs)
    vmem = pl.BlockSpec(memory_space=pltpu.VMEM)
    smem = pl.BlockSpec(memory_space=pltpu.SMEM)
    return pl.pallas_call(
        body,
        out_shape=[jax.ShapeDtypeStruct((views_n, WINDOW, band, LANES), jnp.float32)] * parts_n,
        in_specs=[smem, smem] + [vmem] * len(arrays),
        out_specs=[vmem] * parts_n,
        scratch_shapes=[
            pltpu.VMEM((views_n, blocks, 3 * band, LANES), jnp.float32),
            pltpu.VMEM((views_n, blocks, 3 * band, LANES), jnp.float32),
            pltpu.VMEM((views_n, blocks, 3 * band, LANES), jnp.float32),
            pltpu.VMEM((views_n, blocks, 4 * band, LANES), jnp.float32),
            pltpu.VMEM((views_n, blocks + 1, band, LANES), jnp.float32),
        ],
        name="residual_windows",
    )(ints, trig, *arrays)


def gather_kernel(dims, parts_n, pieces_n, views_n, last, ints_ref, *rest):
    rows_n, cols_n, bins_n, base, blocks = dims
    if last:
        tv_ref, curv_ref, near_ref, *rest = rest
    pieces = rest[:pieces_n]
    if last:
        out_ref, rows_ref, trig_ref, starts_ref = rest[pieces_n:]
    else:
        rows_ref, trig_ref, starts_ref = rest[pieces_n:]
    per_n = cols_n // parts_n
    part = ints_ref[1]
    lane8 = lax.broadcasted_iota(jnp.int32, (8, LANES), 1)
    lane = lax.broadcasted_iota(jnp.int32, (16, LANES), 1)
    total_n = pieces_n * views_n
    for n in range(total_n):
        tagged = pieces[n // views_n][n % views_n, WINDOW - 1, 0:8, :]
        cos = jnp.max(jnp.where(lane8 == COS_LANE, tagged, -2.0))
        sin = jnp.max(jnp.where(lane8 == SIN_LANE, tagged, -2.0))
        trig_ref[n] = cos
        trig_ref[total_n + n] = sin
        starts_ref[n] = window_start(part, per_n, cos, sin, rows_n, cols_n, bins_n, base, blocks)

    def step(index, squares):
        row = index // (per_n // LANES)
        u = index - row * (per_n // LANES)
        along = row.astype(jnp.float32) - 0.5 * rows_n + 0.5
        column = part * per_n + u * LANES
        start = column.astype(jnp.float32)
        across = (lane + column).astype(jnp.float32) - 0.5 * cols_n + 0.5
        cols = pl.ds(pl.multiple_of(u * LANES, LANES), LANES)
        total = near_ref[row, :, cols] if last else jnp.zeros((16, LANES), jnp.float32)
        for n in range(total_n):
            cos = trig_ref[n]
            sin = trig_ref[total_n + n]
            offset = starts_ref[n]
            coord = coordinate(across, along, cos, sin, bins_n)
            lower = jnp.floor(coord)
            frac = coord - lower
            rel = lower.astype(jnp.int32) - (base + offset)
            here = rel & (LANES - 1)
            next_ = (rel + 1) & (LANES - 1)
            first = jnp.maximum(window_of(start, cos, sin, along, cols_n, bins_n, base) - offset, 0)
            k = jnp.minimum(first >> 7, WINDOW - 1)
            windows = pieces[n // views_n]
            left = windows[n % views_n, k]
            right = windows[n % views_n, jnp.minimum(k + 1, WINDOW - 1)]
            held = jnp.where(lane >= (first & (LANES - 1)), left, right)
            a = jnp.take_along_axis(held, here, axis=1, mode="promise_in_bounds")
            b = jnp.take_along_axis(held, next_, axis=1, mode="promise_in_bounds")
            total = total + (a * (1.0 - frac) + b * frac)
        if last:
            total = (total + tv_ref[row, :, cols]) / curv_ref[row, :, cols]
        rows_ref[row, :, cols] = total
        return squares + total * total if last else squares

    steps = rows_n * (per_n // LANES)
    squares = lax.fori_loop(0, steps, step, jnp.zeros((16, LANES), jnp.float32), unroll=4)
    if last:
        for row in range(rows_n):
            out_ref[0:16, row, :] = rows_ref[row]
        out_ref[16] = jnp.full((rows_n, per_n), jnp.sum(squares), jnp.float32)


def gather_views(dims, parts_n, ints, pieces, extra=()):
    views_n, _, slices_n, _ = pieces[0].shape
    rows_n, cols_n = dims[:2]
    per_n = cols_n // parts_n
    pieces_n = len(pieces)
    last = len(extra) > 0
    rows = (rows_n, slices_n, per_n)
    shape = (slices_n + 1, rows_n, per_n) if last else rows
    vmem = pl.BlockSpec(memory_space=pltpu.VMEM)
    scratch = [
        pltpu.SMEM((2 * pieces_n * views_n,), jnp.float32),
        pltpu.SMEM((pieces_n * views_n,), jnp.int32),
    ]
    return pl.pallas_call(
        lambda *refs: gather_kernel(dims, parts_n, pieces_n, views_n, last, *refs),
        out_shape=jax.ShapeDtypeStruct(shape, jnp.float32),
        in_specs=[pl.BlockSpec(memory_space=pltpu.SMEM)] + [vmem] * (pieces_n + len(extra)),
        out_specs=vmem,
        scratch_shapes=([pltpu.VMEM(rows, jnp.float32)] if last else []) + scratch,
        name="gather_views",
    )(ints, *extra, *pieces)


def total_kernel(*refs):
    sums = [ref[0, 0:1, :] for ref in refs[:-1]]
    while len(sums) > 1:
        sums = [a + b for a, b in zip(sums[0::2], sums[1::2])]
    refs[-1][...] = sums[0]


def total(pieces):
    slices_n, rows_n, _ = pieces[0].shape
    last = pl.BlockSpec((1, rows_n, LANES), lambda i: (slices_n - 1, 0, 0))
    return pl.pallas_call(
        total_kernel,
        grid=(1,),
        out_shape=jax.ShapeDtypeStruct((1, LANES), jnp.float32),
        in_specs=[last] * len(pieces),
        out_specs=pl.BlockSpec((1, LANES), lambda i: (0, 0)),
        name="total",
    )(*pieces)


def finish_kernel(parts_n, voxel_count, ints_ref, *rest):
    sums, vol_ref, pieces = rest[:4], rest[4], rest[5 : 5 + parts_n]
    out_ref = rest[5 + parts_n]
    squares = sums[0][...] + sums[1][...] + (sums[2][...] + sums[3][...])
    rms = jnp.sqrt(squares / float(voxel_count) + epsilon)
    factor = jnp.max(jnp.minimum(1.0, step_limit / rms))
    slices_n, _, per_n = pieces[0].shape
    part = ints_ref[1]
    for r in range(parts_n):
        cols = pl.ds(pl.multiple_of((part ^ SLOTS[r]) * per_n, per_n), per_n)
        out_ref[:, :, cols] = vol_ref[:, :, cols] - factor * pieces[r][0 : slices_n - 1]


def finish(voxel_count, ints, sums, volume, pieces):
    parts_n = len(pieces)
    vmem = pl.BlockSpec(memory_space=pltpu.VMEM)
    smem = pl.BlockSpec(memory_space=pltpu.SMEM)
    return pl.pallas_call(
        lambda *refs: finish_kernel(parts_n, voxel_count, *refs),
        out_shape=jax.ShapeDtypeStruct(volume.shape, volume.dtype),
        in_specs=[smem] + [vmem] * (parts_n + 5),
        out_specs=vmem,
        name="finish",
    )(ints, *sums, volume, *pieces)


def swapped(x, axis, bit):
    return lax.ppermute(x, axis, [(i, i ^ bit) for i in range(lax.axis_size(axis))])


def gathered(piece):
    near = swapped(piece, "view", 2)
    far = [swapped(piece, "view", 4), swapped(piece, "view", 6)]
    side = [swapped(piece, "view", 1), swapped(piece, "view", 3)]
    return [piece, near] + far + side + [swapped(x, "view", 1) for x in far]


def local_split(volume, sinogram, curvature, angles, offsets):
    slices_n, rows_n, cols_n = volume.shape
    views_n = angles.shape[0]
    bins_n = sinogram.shape[2]
    base, blocks = extent(rows_n, cols_n, bins_n)
    dims = (rows_n, cols_n, bins_n, base, blocks)
    slab_count = lax.axis_size("slab")
    parts_n = lax.axis_size("view")
    slab = lax.axis_index("slab")
    part = lax.axis_index("view")
    per_n = cols_n // parts_n

    angle_rad = angles.astype(jnp.float32) * (2.0 * math.pi / ROTATION_VIEWS)
    trig = jnp.concatenate([jnp.cos(angle_rad), jnp.sin(angle_rad)])

    def outer(at):
        face = lax.dynamic_slice(volume, (at, 0, part * per_n), (1, rows_n, per_n))
        return face.reshape(1, 1, slices_n, LANES)

    measured = sinogram[:, :, base : base + blocks * LANES]
    measured = measured.reshape(views_n, slices_n, blocks, LANES).transpose(0, 2, 1, 3)
    faces = jnp.concatenate([outer(0), outer(slices_n - 1)], axis=0)
    measured = jnp.concatenate([measured, faces], axis=1)
    cross_rows = swapped(measured, "slab", 2)
    pair_rows = swapped(measured, "slab", 1)
    trig, measured = lax.optimization_barrier((trig, measured))
    proj = project(trig, volume, bins_n, base, blocks, views_n)
    cross_pair_rows = swapped(cross_rows, "slab", 1)
    cross = swapped(proj, "slab", 2)
    near = swapped(proj, "slab", 1)
    cross_pair = swapped(cross, "slab", 1)

    def of(k):
        return lax.dynamic_index_in_dim(offsets, k, 1, keepdims=False)

    start = of(slab)
    shifts = [slices_n + jnp.clip(start - of(slab ^ k), -slices_n, slices_n) for k in (1, 2, 3)]
    table = jnp.stack([start] + shifts, axis=1).reshape(-1)
    ints = jnp.concatenate([jnp.stack([slab, part]).astype(jnp.int32), table])
    windows = residual_windows(
        dims,
        parts_n,
        ints,
        trig,
        [proj, near, cross, cross_pair, measured, pair_rows, cross_rows, cross_pair_rows],
    )
    pieces = [windows[0]] + [swapped(windows[r], "view", r) for r in range(1, parts_n)]
    def face_of(rows, which):
        return rows[which, blocks].reshape(1, rows_n, per_n)

    odd = slab % 2 == 1
    below = jnp.where(odd, face_of(pair_rows, 1), jnp.where(slab == 0, 0.0, face_of(cross_pair_rows, 1)))
    above = jnp.where(odd, jnp.where(slab == slab_count - 1, 0.0, face_of(cross_pair_rows, 0)), face_of(pair_rows, 0))
    wide = jnp.pad(volume, ((0, 0), (0, 0), (1, 1)))
    block = lax.dynamic_slice_in_dim(wide, part * per_n, per_n + 2, axis=2)
    sides = ((0, 0), (0, 0), (1, 1))
    block = jnp.concatenate([jnp.pad(below, sides), block, jnp.pad(above, sides)], axis=0)
    tv_grad = tv_padded(jnp.pad(block, ((0, 0), (1, 1), (0, 0))))
    curv = lax.dynamic_slice_in_dim(curvature, part * per_n, per_n, axis=2)
    tv = (tv_weight * tv_grad).transpose(1, 0, 2)
    near_grad = gather_views(dims, parts_n, ints, pieces[: parts_n // 2])
    extra = (tv, curv.transpose(1, 0, 2), near_grad)
    parts = gathered(gather_views(dims, parts_n, ints, pieces[parts_n // 2 :], extra))
    squares = total(parts)
    sums = [squares] + [swapped(squares, "slab", k) for k in (1, 2, 3)]
    voxel_count = slices_n * slab_count * rows_n * cols_n
    return finish(voxel_count, ints, sums, volume, parts)


def local(volume, sinogram, curvature, angles, offsets):
    shape = (lax.axis_size("slab"), lax.axis_size("view"), angles.shape[0])
    if shape == (4, 8, 2):
        return local_split(volume, sinogram, curvature, angles, offsets)
    return local_any(volume, sinogram, curvature, angles, offsets)


def solution(mesh):
    in_specs = (
        P("slab", None, None),
        P("view", "slab", None),
        P("slab", None, None),
        P("view"),
        P("view", None),
    )
    out_specs = P("slab", None, None)
    return jax.shard_map(local, mesh=mesh, in_specs=in_specs, out_specs=out_specs, check_vma=False)
```

```python
import math
import jax
import jax.numpy as jnp
from jax import lax
from jax.experimental import pallas as pl
from jax.experimental.pallas import tpu as pltpu
from jax.sharding import PartitionSpec as P

ROTATION_VIEWS = 1152


huber_delta = 0.5
tv_weight = 4.0
step_limit = 1.0
epsilon = 1e-06
scale = 0.7
LANES = 128
GROUP = 32


def coordinate(across, along, cos, sin, bins_n):
    return scale * (across * cos + along * sin) + 0.5 * bins_n - 0.5


def window_of(start, cos, sin, along, cols_n, bins_n, base):
    first = coordinate(start - 0.5 * cols_n + 0.5, along, cos, sin, bins_n)
    last = coordinate(start + (LANES - 1.0) - 0.5 * cols_n + 0.5, along, cos, sin, bins_n)
    return jnp.minimum(first, last).astype(jnp.int32) - (base + 1)


def project_kernel(cols_n, rows_n, bins_n, base, blocks_n, views_n, trig_ref, vol_ref, out_ref, rows_ref, acc_ref, sem):
    copies = [pltpu.make_async_copy(vol_ref.at[:, i, :], rows_ref.at[i], sem.at[i]) for i in range(rows_n)]
    for c in copies:
        c.start()
    acc_ref[...] = jnp.zeros_like(acc_ref)
    lane8 = lax.broadcasted_iota(jnp.int32, (8, LANES), 1)
    lane = lax.broadcasted_iota(jnp.int32, (16, LANES), 1)
    sub = lax.broadcasted_iota(jnp.int32, (LANES, LANES), 0).astype(jnp.float32).astype(jnp.bfloat16)
    zero = jnp.zeros((LANES, LANES), jnp.bfloat16)

    def tall(x):
        return jnp.concatenate([jnp.concatenate([x, x], 0).astype(jnp.bfloat16)] * (LANES // 16), 0)

    for row in range(rows_n):
        copies[row].wait()
        along = row - 0.5 * rows_n + 0.5

        def step(g, _):
            outs = []
            for u in range(GROUP):
                block = g * GROUP + u
                start = (block * LANES).astype(jnp.float32)
                vals = rows_ref[row, :, pl.ds(pl.multiple_of(block * LANES, LANES), LANES)]
                high = vals.astype(jnp.bfloat16)
                rest = vals - high.astype(jnp.float32)
                mid = rest.astype(jnp.bfloat16)
                low = (rest - mid.astype(jnp.float32)).astype(jnp.bfloat16)
                terms = jnp.concatenate([high, mid, low], 0)
                mats = []
                wins = []
                for v in range(views_n):
                    cos = trig_ref[v]
                    sin = trig_ref[views_n + v]
                    across = (lane8 + block * LANES).astype(jnp.float32) - 0.5 * cols_n + 0.5
                    coord = coordinate(across, along, cos, sin, bins_n)
                    lower = jnp.floor(coord)
                    frac = coord - lower
                    rel = lower - float(base)
                    bm = rel - LANES * jnp.floor(rel * (1.0 / LANES))
                    bn = jnp.where(bm == LANES - 1.0, 0.0, bm + 1.0)
                    fh = jnp.floor(frac * 128.0) * (1.0 / 128.0)
                    fl = frac - fh
                    here = sub == tall(bm)
                    next_ = sub == tall(bn)
                    wh = jnp.where(here, tall(1.0 - fh), jnp.where(next_, tall(fh), zero))
                    wl = jnp.where(here, tall(-fl), jnp.where(next_, tall(fl), zero))
                    mats.append(jnp.concatenate([wh, wl], 1))
                    wins.append(window_of(start, cos, sin, along, cols_n, bins_n, base))
                weights = jnp.concatenate(mats, 0)
                both = jnp.concatenate([terms, terms], 1)
                prod = lax.dot_general(both, weights, (((1,), (1,)), ((), ())), preferred_element_type=jnp.float32)
                outs.append((prod[0:16] + prod[16:32] + prod[32:48], wins))
            for summed, wins in outs:
                for v in range(views_n):
                    first = wins[v]
                    k = first >> 7
                    own = lane >= (first & (LANES - 1))
                    part = summed[:, v * LANES:(v + 1) * LANES]
                    acc_ref[v, k] += jnp.where(own, part, 0.0)
                    acc_ref[v, k + 1] += jnp.where(own, 0.0, part)
            return 0

        lax.fori_loop(0, cols_n // LANES // GROUP, step, 0)
    out_ref[...] = acc_ref[:, :blocks_n]


def project(trig, volume, bins_n, base, blocks_n, views_n):
    slices_n, rows_n, cols_n = volume.shape
    body = lambda *refs: project_kernel(cols_n, rows_n, bins_n, base, blocks_n, views_n, *refs)
    return pl.pallas_call(
        body,
        out_shape=jax.ShapeDtypeStruct((views_n, blocks_n, slices_n, LANES), jnp.float32),
        in_specs=[pl.BlockSpec(memory_space=pltpu.SMEM), pl.BlockSpec(memory_space=pl.ANY)],
        out_specs=pl.BlockSpec(memory_space=pltpu.VMEM),
        scratch_shapes=[
            pltpu.VMEM((rows_n, slices_n, cols_n), jnp.float32),
            pltpu.VMEM((views_n, blocks_n + 1, slices_n, LANES), jnp.float32),
            pltpu.SemaphoreType.DMA((rows_n,)),
        ],
        name="project",
    )(trig, volume)


def backproject_kernel(cols_n, rows_n, bins_n, base, views_n, width, per_n, trig_ref, starts_ref, res_ref, out_ref):
    lane16 = lax.broadcasted_iota(jnp.int32, (16, LANES), 1)
    pixel0 = starts_ref[views_n]

    def row_step(row, _):
        along = row.astype(jnp.float32) - 0.5 * rows_n + 0.5

        def step(u, _):
            column = pixel0 + u * LANES
            start = column.astype(jnp.float32)
            across = (lane16 + column).astype(jnp.float32) - 0.5 * cols_n + 0.5
            total = jnp.zeros((16, LANES), jnp.float32)
            for v in range(views_n):
                cos = trig_ref[v]
                sin = trig_ref[views_n + v]
                coord = coordinate(across, along, cos, sin, bins_n)
                lower = jnp.floor(coord)
                frac = coord - lower
                offset = starts_ref[v]
                rel = lower.astype(jnp.int32) - (base + offset)
                here = rel & (LANES - 1)
                next_ = (rel + 1) & (LANES - 1)
                first = window_of(start, cos, sin, along, cols_n, bins_n, base) - offset
                k = first >> 7
                left = res_ref[v, k]
                right = res_ref[v, jnp.minimum(k + 1, width - 1)]
                band = jnp.where(lane16 >= (first & (LANES - 1)), left, right)
                a = jnp.take_along_axis(band, here, axis=1, mode="promise_in_bounds")
                b = jnp.take_along_axis(band, next_, axis=1, mode="promise_in_bounds")
                total = total + (a * (1.0 - frac) + b * frac)
            out_ref[row, :, pl.ds(pl.multiple_of(u * LANES, LANES), LANES)] = total
            return 0

        lax.fori_loop(0, per_n // LANES, step, 0)
        return 0

    lax.fori_loop(0, rows_n, row_step, 0)


def backproject(trig, starts, res, rows_n, cols_n, bins_n, base, per_n):
    views_n, width, slices_n, _ = res.shape
    body = lambda *refs: backproject_kernel(cols_n, rows_n, bins_n, base, views_n, width, per_n, *refs)
    return pl.pallas_call(
        body,
        out_shape=jax.ShapeDtypeStruct((rows_n, slices_n, per_n), jnp.float32),
        in_specs=[pl.BlockSpec(memory_space=pltpu.SMEM), pl.BlockSpec(memory_space=pltpu.SMEM), pl.BlockSpec(memory_space=pltpu.VMEM)],
        out_specs=pl.BlockSpec(memory_space=pltpu.VMEM),
        name="backproject",
    )(trig, starts, res)


def padded_2(cells, sides, width):
    for axis, dim in sides:
        count = lax.axis_size(axis)
        ends = count - 1
        head = lax.slice_in_dim(cells, 0, width, axis=dim)
        tail = lax.slice_in_dim(cells, cells.shape[dim] - width, cells.shape[dim], axis=dim)
        cells = jnp.concatenate(
            [
                lax.ppermute(tail, axis, [(i, (i + 1) % count) for i in range(ends)]),
                cells,
                lax.ppermute(head, axis, [((i + 1) % count, i) for i in range(ends)]),
            ],
            axis=dim,
        )
    return cells


def slope(diff):
    return jnp.clip(diff / huber_delta, -1.0, 1.0)


def tv_padded(padded):
    centre = padded[1:-1, 1:-1, 1:-1]
    result = slope(centre - padded[:-2, 1:-1, 1:-1]) - slope(padded[2:, 1:-1, 1:-1] - centre)
    result = (
        result + slope(centre - padded[1:-1, :-2, 1:-1]) - slope(padded[1:-1, 2:, 1:-1] - centre)
    )
    result = (
        result + slope(centre - padded[1:-1, 1:-1, :-2]) - slope(padded[1:-1, 1:-1, 2:] - centre)
    )
    return result


def extent(rows_n, cols_n, bins_n):
    reach = scale * math.hypot(0.5 * (cols_n - 1), 0.5 * (rows_n - 1))
    centre = 0.5 * bins_n - 0.5
    base = (int(centre - reach) - 3) // 8 * 8
    blocks = -(-(int(centre + reach) + 3 - base) // LANES)
    return base, blocks


def local_any(volume, sinogram, curvature, angles, offsets):
    slices_n, rows_n, cols_n = volume.shape
    views_n = angles.shape[0]
    bins_n = sinogram.shape[2]
    base, blocks = extent(rows_n, cols_n, bins_n)
    pixels_n = rows_n * cols_n
    slab_count = lax.axis_size("slab")
    all_rows = sinogram.shape[1] * slab_count
    slab_pos = lax.axis_index("slab")
    angle_rad = angles.astype(jnp.float32) * (2.0 * math.pi / ROTATION_VIEWS)
    trig = jnp.concatenate([jnp.cos(angle_rad), jnp.sin(angle_rad)])
    proj = project(trig, volume, bins_n, base, blocks, views_n)
    stacked = []
    bands = []
    for v in range(views_n):
        start = lax.dynamic_index_in_dim(offsets[v], slab_pos, 0, keepdims=False)
        flat = proj[v].transpose(1, 0, 2).reshape(slices_n, blocks * LANES)
        stacked.append(
            lax.dynamic_update_slice(
                jnp.zeros((all_rows, blocks * LANES), jnp.float32), flat, (start, jnp.int32(0))
            )
        )
        bands.append(start)
    own = lax.psum_scatter(jnp.stack(stacked), "slab", scatter_dimension=1, tiled=True)
    measured = sinogram[:, :, base : base + blocks * LANES]
    residual = lax.all_gather(own - measured, "slab", axis=1, tiled=True)
    windows = jnp.stack(
        [
            lax.dynamic_slice(
                residual[v], (bands[v], jnp.int32(0)), (slices_n, blocks * LANES)
            )
            .reshape(slices_n, blocks, LANES)
            .transpose(1, 0, 2)
            for v in range(views_n)
        ]
    )
    starts = jnp.zeros((views_n + 1,), jnp.int32)
    data_local = backproject(trig, starts, windows, rows_n, cols_n, bins_n, base, cols_n)
    extended = padded_2(volume, (("slab", 0),), 1)
    padded = jnp.pad(extended, ((0, 0), (1, 1), (1, 1)))
    tv_grad = tv_padded(padded)
    data_grad = lax.psum(data_local, "view").transpose(1, 0, 2)
    direction = (data_grad + tv_weight * tv_grad) / curvature
    squares = lax.psum(jnp.sum(direction * direction), "slab")
    voxel_count = slices_n * slab_count * pixels_n
    factor = jnp.minimum(1.0, step_limit / jnp.sqrt(squares / voxel_count + epsilon))
    return volume - factor * direction


WINDOW = 3
SLOTS = (0, 2, 4, 6, 1, 3, 5, 7)
COS_LANE = LANES - 2
SIN_LANE = LANES - 1


def window_start(part, per_n, cos, sin, rows_n, cols_n, bins_n, base, blocks):
    low = None
    for row in (0, rows_n - 1):
        along = row - 0.5 * rows_n + 0.5
        for edge in (0.0, per_n - 1.0):
            across = (part * per_n).astype(jnp.float32) + edge - 0.5 * cols_n + 0.5
            t = coordinate(across, along, cos, sin, bins_n)
            low = t if low is None else jnp.minimum(low, t)
    first = low.astype(jnp.int32) - (base + 1)
    return jnp.clip(first, 0, (blocks - WINDOW) * LANES)


def fill_pad(pad, value):
    views_n, blocks, band, _ = value.shape
    edge = jnp.zeros((views_n, blocks, band, LANES), jnp.float32)
    pad[:, :, 0:band] = edge
    pad[:, :, 2 * band :] = edge
    pad[:, :, band : 2 * band] = value[...]


def near_kernel(ints_ref, proj_ref, near_ref, *rest):
    sinos, out_ref, pad, sino = rest[:4], rest[4], rest[5], rest[6]
    views_n, blocks, band, _ = proj_ref.shape
    slab = ints_ref[0]
    fill_pad(pad, near_ref)
    for other in range(4):
        rows = pl.ds(pl.multiple_of((slab ^ other) * band, band), band)
        sino[:, :, rows] = sinos[other][:, 0:blocks]
    for v in range(views_n):
        value = proj_ref[v] + pad[v, :, pl.ds(ints_ref[3 + 4 * v], band), :]
        out_ref[v] = value - sino[v, :, pl.ds(ints_ref[2 + 4 * v], band), :]


def near_residual(ints, arrays):
    views_n, blocks, band, _ = arrays[0].shape
    vmem = pl.BlockSpec(memory_space=pltpu.VMEM)
    return pl.pallas_call(
        near_kernel,
        out_shape=jax.ShapeDtypeStruct(arrays[0].shape, jnp.float32),
        in_specs=[pl.BlockSpec(memory_space=pltpu.SMEM)] + [vmem] * len(arrays),
        out_specs=vmem,
        scratch_shapes=[
            pltpu.VMEM((views_n, blocks, 3 * band, LANES), jnp.float32),
            pltpu.VMEM((views_n, blocks, 4 * band, LANES), jnp.float32),
        ],
        name="near_residual",
    )(ints, *arrays)


def residual_kernel(dims, parts_n, ints_ref, trig_ref, base_ref, cross_ref, cross_pair_ref, *rest):
    rows_n, cols_n, bins_n, base, blocks = dims
    outs = rest[:parts_n]
    cross_pad, cross_pair_pad, res = rest[parts_n:]
    views_n, _, band, _ = base_ref.shape
    part = ints_ref[1]
    fill_pad(cross_pad, cross_ref)
    fill_pad(cross_pair_pad, cross_pair_ref)
    for v in range(views_n):
        value = base_ref[v] + cross_pad[v, :, pl.ds(ints_ref[4 + 4 * v], band), :]
        res[v, 0:blocks] = value + cross_pair_pad[v, :, pl.ds(ints_ref[5 + 4 * v], band), :]
        res[v, blocks] = jnp.zeros((band, LANES), jnp.float32)
    lane = lax.broadcasted_iota(jnp.int32, (band, LANES), 1)
    per_n = cols_n // parts_n
    for r in range(parts_n):
        for v in range(views_n):
            cos, sin = trig_ref[v], trig_ref[views_n + v]
            first = window_start(part ^ r, per_n, cos, sin, rows_n, cols_n, bins_n, base, blocks)
            k = first >> 7
            shift = first & (LANES - 1)
            turned = [pltpu.roll(res[v, k + m], (LANES - shift) & (LANES - 1), 1) for m in range(WINDOW + 1)]
            for m in range(WINDOW):
                value = jnp.where(lane < LANES - shift, turned[m], turned[m + 1])
                if m == WINDOW - 1:
                    value = jnp.where(lane == COS_LANE, cos, jnp.where(lane == SIN_LANE, sin, value))
                outs[r][v, m] = value


def residual_windows(dims, parts_n, ints, trig, arrays):
    views_n, blocks, band, _ = arrays[0].shape
    body = lambda *refs: residual_kernel(dims, parts_n, *refs)
    vmem = pl.BlockSpec(memory_space=pltpu.VMEM)
    smem = pl.BlockSpec(memory_space=pltpu.SMEM)
    return pl.pallas_call(
        body,
        out_shape=[jax.ShapeDtypeStruct((views_n, WINDOW, band, LANES), jnp.float32)] * parts_n,
        in_specs=[smem, smem] + [vmem] * len(arrays),
        out_specs=[vmem] * parts_n,
        scratch_shapes=[
            pltpu.VMEM((views_n, blocks, 3 * band, LANES), jnp.float32),
            pltpu.VMEM((views_n, blocks, 3 * band, LANES), jnp.float32),
            pltpu.VMEM((views_n, blocks + 1, band, LANES), jnp.float32),
        ],
        name="residual_windows",
    )(ints, trig, *arrays)


def gather_kernel(dims, parts_n, pieces_n, views_n, last, ints_ref, *rest):
    rows_n, cols_n, bins_n, base, blocks = dims
    if last:
        tv_ref, curv_ref, near_ref, *rest = rest
    pieces = rest[:pieces_n]
    if last:
        out_ref, sum_ref, rows_ref, trig_ref, starts_ref = rest[pieces_n:]
    else:
        rows_ref, trig_ref, starts_ref = rest[pieces_n:]
    per_n = cols_n // parts_n
    part = ints_ref[1]
    lane8 = lax.broadcasted_iota(jnp.int32, (8, LANES), 1)
    lane = lax.broadcasted_iota(jnp.int32, (16, LANES), 1)
    total_n = pieces_n * views_n
    for n in range(total_n):
        tagged = pieces[n // views_n][n % views_n, WINDOW - 1, 0:8, :]
        cos = jnp.max(jnp.where(lane8 == COS_LANE, tagged, -2.0))
        sin = jnp.max(jnp.where(lane8 == SIN_LANE, tagged, -2.0))
        trig_ref[n] = cos
        trig_ref[total_n + n] = sin
        starts_ref[n] = window_start(part, per_n, cos, sin, rows_n, cols_n, bins_n, base, blocks)

    def step(index, squares):
        row = index // (per_n // LANES)
        u = index - row * (per_n // LANES)
        along = row.astype(jnp.float32) - 0.5 * rows_n + 0.5
        column = part * per_n + u * LANES
        start = column.astype(jnp.float32)
        across = (lane + column).astype(jnp.float32) - 0.5 * cols_n + 0.5
        cols = pl.ds(pl.multiple_of(u * LANES, LANES), LANES)
        total = near_ref[row, :, cols] if last else jnp.zeros((16, LANES), jnp.float32)
        for n in range(total_n):
            cos = trig_ref[n]
            sin = trig_ref[total_n + n]
            offset = starts_ref[n]
            coord = coordinate(across, along, cos, sin, bins_n)
            lower = jnp.floor(coord)
            frac = coord - lower
            rel = lower.astype(jnp.int32) - (base + offset)
            here = rel & (LANES - 1)
            next_ = (rel + 1) & (LANES - 1)
            first = jnp.maximum(window_of(start, cos, sin, along, cols_n, bins_n, base) - offset, 0)
            k = jnp.minimum(first >> 7, WINDOW - 1)
            windows = pieces[n // views_n]
            left = windows[n % views_n, k]
            right = windows[n % views_n, jnp.minimum(k + 1, WINDOW - 1)]
            held = jnp.where(lane >= (first & (LANES - 1)), left, right)
            a = jnp.take_along_axis(held, here, axis=1, mode="promise_in_bounds")
            b = jnp.take_along_axis(held, next_, axis=1, mode="promise_in_bounds")
            total = total + (a * (1.0 - frac) + b * frac)
        if last:
            total = (total + tv_ref[row, :, cols]) / curv_ref[row, :, cols]
        rows_ref[row, :, cols] = total
        return squares + total * total if last else squares

    steps = rows_n * (per_n // LANES)
    squares = lax.fori_loop(0, steps, step, jnp.zeros((16, LANES), jnp.float32), unroll=4)
    if last:
        for row in range(rows_n):
            out_ref[0:16, row, :] = rows_ref[row]
        summed = jnp.sum(squares)
        out_ref[16] = jnp.full((rows_n, per_n), summed, jnp.float32)
        sum_ref[...] = jnp.full((1, LANES), summed, jnp.float32)


def gather_views(dims, parts_n, ints, pieces, extra=()):
    views_n, _, slices_n, _ = pieces[0].shape
    rows_n, cols_n = dims[:2]
    per_n = cols_n // parts_n
    pieces_n = len(pieces)
    last = len(extra) > 0
    rows = (rows_n, slices_n, per_n)
    shapes = [(slices_n + 1, rows_n, per_n), (1, LANES)] if last else [rows]
    vmem = pl.BlockSpec(memory_space=pltpu.VMEM)
    scratch = [
        pltpu.SMEM((2 * pieces_n * views_n,), jnp.float32),
        pltpu.SMEM((pieces_n * views_n,), jnp.int32),
    ]
    return pl.pallas_call(
        lambda *refs: gather_kernel(dims, parts_n, pieces_n, views_n, last, *refs),
        out_shape=[jax.ShapeDtypeStruct(x, jnp.float32) for x in shapes],
        in_specs=[pl.BlockSpec(memory_space=pltpu.SMEM)] + [vmem] * (pieces_n + len(extra)),
        out_specs=[vmem] * len(shapes),
        scratch_shapes=([pltpu.VMEM(rows, jnp.float32)] if last else []) + scratch,
        name="gather_views",
    )(ints, *extra, *pieces)


def total_kernel(pieces_n, *refs):
    sums = [ref[0, 0:1, :] for ref in refs[:pieces_n]] + [ref[...] for ref in refs[pieces_n:-1]]
    while len(sums) > 1:
        sums = [a + b for a, b in zip(sums[0::2], sums[1::2])]
    refs[-1][...] = sums[0]


def total(pieces, distant):
    slices_n, rows_n, _ = pieces[0].shape
    last = pl.BlockSpec((1, rows_n, LANES), lambda i: (slices_n - 1, 0, 0))
    line = pl.BlockSpec((1, LANES), lambda i: (0, 0))
    return pl.pallas_call(
        lambda *refs: total_kernel(len(pieces), *refs),
        grid=(1,),
        out_shape=jax.ShapeDtypeStruct((1, LANES), jnp.float32),
        in_specs=[last] * len(pieces) + [line] * len(distant),
        out_specs=line,
        name="total",
    )(*pieces, *distant)


def finish_kernel(parts_n, voxel_count, ints_ref, *rest):
    sums, vol_ref, pieces = rest[:4], rest[4], rest[5 : 5 + parts_n]
    out_ref = rest[5 + parts_n]
    squares = sums[0][...] + sums[1][...] + (sums[2][...] + sums[3][...])
    rms = jnp.sqrt(squares / float(voxel_count) + epsilon)
    factor = jnp.max(jnp.minimum(1.0, step_limit / rms))
    slices_n, _, per_n = pieces[0].shape
    part = ints_ref[1]
    for r in range(parts_n):
        cols = pl.ds(pl.multiple_of((part ^ SLOTS[r]) * per_n, per_n), per_n)
        out_ref[:, :, cols] = vol_ref[:, :, cols] - factor * pieces[r][0 : slices_n - 1]


def finish(voxel_count, ints, sums, volume, pieces):
    parts_n = len(pieces)
    vmem = pl.BlockSpec(memory_space=pltpu.VMEM)
    smem = pl.BlockSpec(memory_space=pltpu.SMEM)
    return pl.pallas_call(
        lambda *refs: finish_kernel(parts_n, voxel_count, *refs),
        out_shape=jax.ShapeDtypeStruct(volume.shape, volume.dtype),
        in_specs=[smem] + [vmem] * (parts_n + 5),
        out_specs=vmem,
        name="finish",
    )(ints, *sums, volume, *pieces)


def swapped(x, axis, bit):
    return lax.ppermute(x, axis, [(i, i ^ bit) for i in range(lax.axis_size(axis))])


def gathered(piece):
    near = swapped(piece, "view", 2)
    far = [swapped(piece, "view", 4), swapped(piece, "view", 6)]
    side = [swapped(piece, "view", 1), swapped(piece, "view", 3)]
    return [piece, near] + far + side + [swapped(x, "view", 1) for x in far]


def local_split(volume, sinogram, curvature, angles, offsets):
    slices_n, rows_n, cols_n = volume.shape
    views_n = angles.shape[0]
    bins_n = sinogram.shape[2]
    base, blocks = extent(rows_n, cols_n, bins_n)
    dims = (rows_n, cols_n, bins_n, base, blocks)
    slab_count = lax.axis_size("slab")
    parts_n = lax.axis_size("view")
    slab = lax.axis_index("slab")
    part = lax.axis_index("view")
    per_n = cols_n // parts_n

    angle_rad = angles.astype(jnp.float32) * (2.0 * math.pi / ROTATION_VIEWS)
    trig = jnp.concatenate([jnp.cos(angle_rad), jnp.sin(angle_rad)])

    def outer(at):
        face = lax.dynamic_slice(volume, (at, 0, part * per_n), (1, rows_n, per_n))
        return face.reshape(1, 1, slices_n, LANES)

    measured = sinogram[:, :, base : base + blocks * LANES]
    measured = measured.reshape(views_n, slices_n, blocks, LANES).transpose(0, 2, 1, 3)
    faces = jnp.concatenate([outer(0), outer(slices_n - 1)], axis=0)
    measured = jnp.concatenate([measured, faces], axis=1)
    cross_rows = swapped(measured, "slab", 2)
    pair_rows = swapped(measured, "slab", 1)
    trig, measured = lax.optimization_barrier((trig, measured))
    proj = project(trig, volume, bins_n, base, blocks, views_n)
    cross_pair_rows = swapped(cross_rows, "slab", 1)
    cross = swapped(proj, "slab", 2)
    near = swapped(proj, "slab", 1)

    def of(k):
        return lax.dynamic_index_in_dim(offsets, k, 1, keepdims=False)

    start = of(slab)
    shifts = [slices_n + jnp.clip(start - of(slab ^ k), -slices_n, slices_n) for k in (1, 2, 3)]
    table = jnp.stack([start] + shifts, axis=1).reshape(-1)
    ints = jnp.concatenate([jnp.stack([slab, part]).astype(jnp.int32), table])
    rows = [measured, pair_rows, cross_rows, cross_pair_rows]
    local_part = near_residual(ints, [proj, near] + rows)
    local_part, cross = lax.optimization_barrier((local_part, cross))
    cross_pair = swapped(cross, "slab", 1)
    windows = residual_windows(dims, parts_n, ints, trig, [local_part, cross, cross_pair])
    pieces = [windows[0]] + [swapped(windows[r], "view", r) for r in range(1, parts_n)]
    def face_of(rows, which):
        return rows[which, blocks].reshape(1, rows_n, per_n)

    odd = slab % 2 == 1
    below = jnp.where(odd, face_of(pair_rows, 1), jnp.where(slab == 0, 0.0, face_of(cross_pair_rows, 1)))
    above = jnp.where(odd, jnp.where(slab == slab_count - 1, 0.0, face_of(cross_pair_rows, 0)), face_of(pair_rows, 0))
    wide = jnp.pad(volume, ((0, 0), (0, 0), (1, 1)))
    block = lax.dynamic_slice_in_dim(wide, part * per_n, per_n + 2, axis=2)
    sides = ((0, 0), (0, 0), (1, 1))
    block = jnp.concatenate([jnp.pad(below, sides), block, jnp.pad(above, sides)], axis=0)
    tv_grad = tv_padded(jnp.pad(block, ((0, 0), (1, 1), (0, 0))))
    curv = lax.dynamic_slice_in_dim(curvature, part * per_n, per_n, axis=2)
    tv = (tv_weight * tv_grad).transpose(1, 0, 2)
    (near_grad,) = gather_views(dims, parts_n, ints, pieces[: parts_n // 2])
    extra = (tv, curv.transpose(1, 0, 2), near_grad)
    piece, squares = gather_views(dims, parts_n, ints, pieces[parts_n // 2 :], extra)
    distant = [swapped(squares, "view", k) for k in SLOTS[6:]]
    parts = gathered(piece)
    squares = total(parts[:6], distant)
    sums = [squares] + [swapped(squares, "slab", k) for k in (1, 2, 3)]
    voxel_count = slices_n * slab_count * rows_n * cols_n
    return finish(voxel_count, ints, sums, volume, parts)


def local(volume, sinogram, curvature, angles, offsets):
    shape = (lax.axis_size("slab"), lax.axis_size("view"), angles.shape[0])
    if shape == (4, 8, 2):
        return local_split(volume, sinogram, curvature, angles, offsets)
    return local_any(volume, sinogram, curvature, angles, offsets)


def solution(mesh):
    in_specs = (
        P("slab", None, None),
        P("view", "slab", None),
        P("slab", None, None),
        P("view"),
        P("view", None),
    )
    out_specs = P("slab", None, None)
    return jax.shard_map(local, mesh=mesh, in_specs=in_specs, out_specs=out_specs, check_vma=False)
```

```python
import math
import jax
import jax.numpy as jnp
from jax import lax
from jax.experimental import pallas as pl
from jax.experimental.pallas import tpu as pltpu
from jax.sharding import PartitionSpec as P

ROTATION_VIEWS = 1152


huber_delta = 0.5
tv_weight = 4.0
step_limit = 1.0
epsilon = 1e-06
scale = 0.7
LANES = 128
GROUP = 32


def coordinate(across, along, cos, sin, bins_n):
    return scale * (across * cos + along * sin) + 0.5 * bins_n - 0.5


def window_of(start, cos, sin, along, cols_n, bins_n, base):
    first = coordinate(start - 0.5 * cols_n + 0.5, along, cos, sin, bins_n)
    last = coordinate(start + (LANES - 1.0) - 0.5 * cols_n + 0.5, along, cos, sin, bins_n)
    return jnp.minimum(first, last).astype(jnp.int32) - (base + 1)


def project_kernel(cols_n, rows_n, bins_n, base, blocks_n, views_n, trig_ref, vol_ref, out_ref, rows_ref, acc_ref, sem):
    copies = [pltpu.make_async_copy(vol_ref.at[:, i, :], rows_ref.at[i], sem.at[i]) for i in range(rows_n)]
    for c in copies:
        c.start()
    acc_ref[...] = jnp.zeros_like(acc_ref)
    lane8 = lax.broadcasted_iota(jnp.int32, (8, LANES), 1)
    lane = lax.broadcasted_iota(jnp.int32, (16, LANES), 1)
    sub = lax.broadcasted_iota(jnp.int32, (LANES, LANES), 0).astype(jnp.float32).astype(jnp.bfloat16)
    zero = jnp.zeros((LANES, LANES), jnp.bfloat16)

    def tall(x):
        return jnp.concatenate([jnp.concatenate([x, x], 0).astype(jnp.bfloat16)] * (LANES // 16), 0)

    for row in range(rows_n):
        copies[row].wait()
        along = row - 0.5 * rows_n + 0.5

        def step(g, _):
            outs = []
            for u in range(GROUP):
                block = g * GROUP + u
                start = (block * LANES).astype(jnp.float32)
                vals = rows_ref[row, :, pl.ds(pl.multiple_of(block * LANES, LANES), LANES)]
                high = vals.astype(jnp.bfloat16)
                rest = vals - high.astype(jnp.float32)
                mid = rest.astype(jnp.bfloat16)
                low = (rest - mid.astype(jnp.float32)).astype(jnp.bfloat16)
                terms = jnp.concatenate([high, mid, low], 0)
                mats = []
                wins = []
                for v in range(views_n):
                    cos = trig_ref[v]
                    sin = trig_ref[views_n + v]
                    across = (lane8 + block * LANES).astype(jnp.float32) - 0.5 * cols_n + 0.5
                    coord = coordinate(across, along, cos, sin, bins_n)
                    lower = jnp.floor(coord)
                    frac = coord - lower
                    rel = lower - float(base)
                    bm = rel - LANES * jnp.floor(rel * (1.0 / LANES))
                    bn = jnp.where(bm == LANES - 1.0, 0.0, bm + 1.0)
                    fh = jnp.floor(frac * 128.0) * (1.0 / 128.0)
                    fl = frac - fh
                    here = sub == tall(bm)
                    next_ = sub == tall(bn)
                    wh = jnp.where(here, tall(1.0 - fh), jnp.where(next_, tall(fh), zero))
                    wl = jnp.where(here, tall(-fl), jnp.where(next_, tall(fl), zero))
                    mats.append(jnp.concatenate([wh, wl], 1))
                    wins.append(window_of(start, cos, sin, along, cols_n, bins_n, base))
                weights = jnp.concatenate(mats, 0)
                both = jnp.concatenate([terms, terms], 1)
                prod = lax.dot_general(both, weights, (((1,), (1,)), ((), ())), preferred_element_type=jnp.float32)
                outs.append((prod[0:16] + prod[16:32] + prod[32:48], wins))
            for summed, wins in outs:
                for v in range(views_n):
                    first = wins[v]
                    k = first >> 7
                    own = lane >= (first & (LANES - 1))
                    part = summed[:, v * LANES:(v + 1) * LANES]
                    acc_ref[v, k] += jnp.where(own, part, 0.0)
                    acc_ref[v, k + 1] += jnp.where(own, 0.0, part)
            return 0

        lax.fori_loop(0, cols_n // LANES // GROUP, step, 0)
    out_ref[...] = acc_ref[:, :blocks_n]


def project(trig, volume, bins_n, base, blocks_n, views_n):
    slices_n, rows_n, cols_n = volume.shape
    body = lambda *refs: project_kernel(cols_n, rows_n, bins_n, base, blocks_n, views_n, *refs)
    return pl.pallas_call(
        body,
        out_shape=jax.ShapeDtypeStruct((views_n, blocks_n, slices_n, LANES), jnp.float32),
        in_specs=[pl.BlockSpec(memory_space=pltpu.SMEM), pl.BlockSpec(memory_space=pl.ANY)],
        out_specs=pl.BlockSpec(memory_space=pltpu.VMEM),
        scratch_shapes=[
            pltpu.VMEM((rows_n, slices_n, cols_n), jnp.float32),
            pltpu.VMEM((views_n, blocks_n + 1, slices_n, LANES), jnp.float32),
            pltpu.SemaphoreType.DMA((rows_n,)),
        ],
        name="project",
    )(trig, volume)


def backproject_kernel(cols_n, rows_n, bins_n, base, views_n, width, per_n, trig_ref, starts_ref, res_ref, out_ref):
    lane16 = lax.broadcasted_iota(jnp.int32, (16, LANES), 1)
    pixel0 = starts_ref[views_n]

    def row_step(row, _):
        along = row.astype(jnp.float32) - 0.5 * rows_n + 0.5

        def step(u, _):
            column = pixel0 + u * LANES
            start = column.astype(jnp.float32)
            across = (lane16 + column).astype(jnp.float32) - 0.5 * cols_n + 0.5
            total = jnp.zeros((16, LANES), jnp.float32)
            for v in range(views_n):
                cos = trig_ref[v]
                sin = trig_ref[views_n + v]
                coord = coordinate(across, along, cos, sin, bins_n)
                lower = jnp.floor(coord)
                frac = coord - lower
                offset = starts_ref[v]
                rel = lower.astype(jnp.int32) - (base + offset)
                here = rel & (LANES - 1)
                next_ = (rel + 1) & (LANES - 1)
                first = window_of(start, cos, sin, along, cols_n, bins_n, base) - offset
                k = first >> 7
                left = res_ref[v, k]
                right = res_ref[v, jnp.minimum(k + 1, width - 1)]
                band = jnp.where(lane16 >= (first & (LANES - 1)), left, right)
                a = jnp.take_along_axis(band, here, axis=1, mode="promise_in_bounds")
                b = jnp.take_along_axis(band, next_, axis=1, mode="promise_in_bounds")
                total = total + (a * (1.0 - frac) + b * frac)
            out_ref[row, :, pl.ds(pl.multiple_of(u * LANES, LANES), LANES)] = total
            return 0

        lax.fori_loop(0, per_n // LANES, step, 0)
        return 0

    lax.fori_loop(0, rows_n, row_step, 0)


def backproject(trig, starts, res, rows_n, cols_n, bins_n, base, per_n):
    views_n, width, slices_n, _ = res.shape
    body = lambda *refs: backproject_kernel(cols_n, rows_n, bins_n, base, views_n, width, per_n, *refs)
    return pl.pallas_call(
        body,
        out_shape=jax.ShapeDtypeStruct((rows_n, slices_n, per_n), jnp.float32),
        in_specs=[pl.BlockSpec(memory_space=pltpu.SMEM), pl.BlockSpec(memory_space=pltpu.SMEM), pl.BlockSpec(memory_space=pltpu.VMEM)],
        out_specs=pl.BlockSpec(memory_space=pltpu.VMEM),
        name="backproject",
    )(trig, starts, res)


def padded_2(cells, sides, width):
    for axis, dim in sides:
        count = lax.axis_size(axis)
        ends = count - 1
        head = lax.slice_in_dim(cells, 0, width, axis=dim)
        tail = lax.slice_in_dim(cells, cells.shape[dim] - width, cells.shape[dim], axis=dim)
        cells = jnp.concatenate(
            [
                lax.ppermute(tail, axis, [(i, (i + 1) % count) for i in range(ends)]),
                cells,
                lax.ppermute(head, axis, [((i + 1) % count, i) for i in range(ends)]),
            ],
            axis=dim,
        )
    return cells


def slope(diff):
    return jnp.clip(diff / huber_delta, -1.0, 1.0)


def tv_padded(padded):
    centre = padded[1:-1, 1:-1, 1:-1]
    result = slope(centre - padded[:-2, 1:-1, 1:-1]) - slope(padded[2:, 1:-1, 1:-1] - centre)
    result = (
        result + slope(centre - padded[1:-1, :-2, 1:-1]) - slope(padded[1:-1, 2:, 1:-1] - centre)
    )
    result = (
        result + slope(centre - padded[1:-1, 1:-1, :-2]) - slope(padded[1:-1, 1:-1, 2:] - centre)
    )
    return result


def extent(rows_n, cols_n, bins_n):
    reach = scale * math.hypot(0.5 * (cols_n - 1), 0.5 * (rows_n - 1))
    centre = 0.5 * bins_n - 0.5
    base = (int(centre - reach) - 3) // 8 * 8
    blocks = -(-(int(centre + reach) + 3 - base) // LANES)
    return base, blocks


def local_any(volume, sinogram, curvature, angles, offsets):
    slices_n, rows_n, cols_n = volume.shape
    views_n = angles.shape[0]
    bins_n = sinogram.shape[2]
    base, blocks = extent(rows_n, cols_n, bins_n)
    pixels_n = rows_n * cols_n
    slab_count = lax.axis_size("slab")
    all_rows = sinogram.shape[1] * slab_count
    slab_pos = lax.axis_index("slab")
    angle_rad = angles.astype(jnp.float32) * (2.0 * math.pi / ROTATION_VIEWS)
    trig = jnp.concatenate([jnp.cos(angle_rad), jnp.sin(angle_rad)])
    proj = project(trig, volume, bins_n, base, blocks, views_n)
    stacked = []
    bands = []
    for v in range(views_n):
        start = lax.dynamic_index_in_dim(offsets[v], slab_pos, 0, keepdims=False)
        flat = proj[v].transpose(1, 0, 2).reshape(slices_n, blocks * LANES)
        stacked.append(
            lax.dynamic_update_slice(
                jnp.zeros((all_rows, blocks * LANES), jnp.float32), flat, (start, jnp.int32(0))
            )
        )
        bands.append(start)
    own = lax.psum_scatter(jnp.stack(stacked), "slab", scatter_dimension=1, tiled=True)
    measured = sinogram[:, :, base : base + blocks * LANES]
    residual = lax.all_gather(own - measured, "slab", axis=1, tiled=True)
    windows = jnp.stack(
        [
            lax.dynamic_slice(
                residual[v], (bands[v], jnp.int32(0)), (slices_n, blocks * LANES)
            )
            .reshape(slices_n, blocks, LANES)
            .transpose(1, 0, 2)
            for v in range(views_n)
        ]
    )
    starts = jnp.zeros((views_n + 1,), jnp.int32)
    data_local = backproject(trig, starts, windows, rows_n, cols_n, bins_n, base, cols_n)
    extended = padded_2(volume, (("slab", 0),), 1)
    padded = jnp.pad(extended, ((0, 0), (1, 1), (1, 1)))
    tv_grad = tv_padded(padded)
    data_grad = lax.psum(data_local, "view").transpose(1, 0, 2)
    direction = (data_grad + tv_weight * tv_grad) / curvature
    squares = lax.psum(jnp.sum(direction * direction), "slab")
    voxel_count = slices_n * slab_count * pixels_n
    factor = jnp.minimum(1.0, step_limit / jnp.sqrt(squares / voxel_count + epsilon))
    return volume - factor * direction


WINDOW = 3
SLOTS = (0, 2, 4, 6, 1, 3, 5, 7)
COS_LANE = LANES - 2
SIN_LANE = LANES - 1


def window_start(part, per_n, cos, sin, rows_n, cols_n, bins_n, base, blocks):
    low = None
    for row in (0, rows_n - 1):
        along = row - 0.5 * rows_n + 0.5
        for edge in (0.0, per_n - 1.0):
            across = (part * per_n).astype(jnp.float32) + edge - 0.5 * cols_n + 0.5
            t = coordinate(across, along, cos, sin, bins_n)
            low = t if low is None else jnp.minimum(low, t)
    first = low.astype(jnp.int32) - (base + 1)
    return jnp.clip(first, 0, (blocks - WINDOW) * LANES)


def fill_pad(pad, value):
    views_n, blocks, band, _ = value.shape
    edge = jnp.zeros((views_n, blocks, band, LANES), jnp.float32)
    pad[:, :, 0:band] = edge
    pad[:, :, 2 * band :] = edge
    pad[:, :, band : 2 * band] = value[...]


def near_kernel(ints_ref, proj_ref, near_ref, *rest):
    sinos, out_ref, pad, sino = rest[:4], rest[4], rest[5], rest[6]
    views_n, blocks, band, _ = proj_ref.shape
    slab = ints_ref[0]
    fill_pad(pad, near_ref)
    for other in range(4):
        rows = pl.ds(pl.multiple_of((slab ^ other) * band, band), band)
        sino[:, :, rows] = sinos[other][:, 0:blocks]
    for v in range(views_n):
        value = proj_ref[v] + pad[v, :, pl.ds(ints_ref[3 + 4 * v], band), :]
        out_ref[v] = value - sino[v, :, pl.ds(ints_ref[2 + 4 * v], band), :]


def near_residual(ints, arrays):
    views_n, blocks, band, _ = arrays[0].shape
    vmem = pl.BlockSpec(memory_space=pltpu.VMEM)
    return pl.pallas_call(
        near_kernel,
        out_shape=jax.ShapeDtypeStruct(arrays[0].shape, jnp.float32),
        in_specs=[pl.BlockSpec(memory_space=pltpu.SMEM)] + [vmem] * len(arrays),
        out_specs=vmem,
        scratch_shapes=[
            pltpu.VMEM((views_n, blocks, 3 * band, LANES), jnp.float32),
            pltpu.VMEM((views_n, blocks, 4 * band, LANES), jnp.float32),
        ],
        name="near_residual",
    )(ints, *arrays)


def residual_kernel(dims, parts_n, ints_ref, trig_ref, base_ref, cross_ref, cross_pair_ref, *rest):
    rows_n, cols_n, bins_n, base, blocks = dims
    outs = rest[:parts_n]
    cross_pad, cross_pair_pad, res = rest[parts_n:]
    views_n, _, band, _ = base_ref.shape
    part = ints_ref[1]
    fill_pad(cross_pad, cross_ref)
    fill_pad(cross_pair_pad, cross_pair_ref)
    for v in range(views_n):
        value = base_ref[v] + cross_pad[v, :, pl.ds(ints_ref[4 + 4 * v], band), :]
        res[v, 0:blocks] = value + cross_pair_pad[v, :, pl.ds(ints_ref[5 + 4 * v], band), :]
        res[v, blocks] = jnp.zeros((band, LANES), jnp.float32)
    lane = lax.broadcasted_iota(jnp.int32, (band, LANES), 1)
    per_n = cols_n // parts_n
    for r in range(parts_n):
        for v in range(views_n):
            cos, sin = trig_ref[v], trig_ref[views_n + v]
            first = window_start(part ^ r, per_n, cos, sin, rows_n, cols_n, bins_n, base, blocks)
            k = first >> 7
            shift = first & (LANES - 1)
            turned = [pltpu.roll(res[v, k + m], (LANES - shift) & (LANES - 1), 1) for m in range(WINDOW + 1)]
            for m in range(WINDOW):
                value = jnp.where(lane < LANES - shift, turned[m], turned[m + 1])
                if m == WINDOW - 1:
                    value = jnp.where(lane == COS_LANE, cos, jnp.where(lane == SIN_LANE, sin, value))
                outs[r][v, m] = value


def residual_windows(dims, parts_n, ints, trig, arrays):
    views_n, blocks, band, _ = arrays[0].shape
    body = lambda *refs: residual_kernel(dims, parts_n, *refs)
    vmem = pl.BlockSpec(memory_space=pltpu.VMEM)
    smem = pl.BlockSpec(memory_space=pltpu.SMEM)
    return pl.pallas_call(
        body,
        out_shape=[jax.ShapeDtypeStruct((views_n, WINDOW, band, LANES), jnp.float32)] * parts_n,
        in_specs=[smem, smem] + [vmem] * len(arrays),
        out_specs=[vmem] * parts_n,
        scratch_shapes=[
            pltpu.VMEM((views_n, blocks, 3 * band, LANES), jnp.float32),
            pltpu.VMEM((views_n, blocks, 3 * band, LANES), jnp.float32),
            pltpu.VMEM((views_n, blocks + 1, band, LANES), jnp.float32),
        ],
        name="residual_windows",
    )(ints, trig, *arrays)


def gather_kernel(dims, parts_n, pieces_n, views_n, last, ints_ref, *rest):
    rows_n, cols_n, bins_n, base, blocks = dims
    if last:
        tv_ref, curv_ref, near_ref, *rest = rest
    pieces = rest[:pieces_n]
    if last:
        out_ref, rows_ref, trig_ref, starts_ref = rest[pieces_n:]
    else:
        rows_ref, trig_ref, starts_ref = rest[pieces_n:]
    per_n = cols_n // parts_n
    part = ints_ref[1]
    lane8 = lax.broadcasted_iota(jnp.int32, (8, LANES), 1)
    lane = lax.broadcasted_iota(jnp.int32, (16, LANES), 1)
    total_n = pieces_n * views_n
    for n in range(total_n):
        tagged = pieces[n // views_n][n % views_n, WINDOW - 1, 0:8, :]
        cos = jnp.max(jnp.where(lane8 == COS_LANE, tagged, -2.0))
        sin = jnp.max(jnp.where(lane8 == SIN_LANE, tagged, -2.0))
        trig_ref[n] = cos
        trig_ref[total_n + n] = sin
        starts_ref[n] = window_start(part, per_n, cos, sin, rows_n, cols_n, bins_n, base, blocks)

    def step(index, squares):
        row = index // (per_n // LANES)
        u = index - row * (per_n // LANES)
        along = row.astype(jnp.float32) - 0.5 * rows_n + 0.5
        column = part * per_n + u * LANES
        start = column.astype(jnp.float32)
        across = (lane + column).astype(jnp.float32) - 0.5 * cols_n + 0.5
        cols = pl.ds(pl.multiple_of(u * LANES, LANES), LANES)
        total = near_ref[row, :, cols] if last else jnp.zeros((16, LANES), jnp.float32)
        for n in range(total_n):
            cos = trig_ref[n]
            sin = trig_ref[total_n + n]
            offset = starts_ref[n]
            coord = coordinate(across, along, cos, sin, bins_n)
            lower = jnp.floor(coord)
            frac = coord - lower
            rel = lower.astype(jnp.int32) - (base + offset)
            here = rel & (LANES - 1)
            next_ = (rel + 1) & (LANES - 1)
            first = jnp.maximum(window_of(start, cos, sin, along, cols_n, bins_n, base) - offset, 0)
            k = jnp.minimum(first >> 7, WINDOW - 1)
            windows = pieces[n // views_n]
            left = windows[n % views_n, k]
            right = windows[n % views_n, jnp.minimum(k + 1, WINDOW - 1)]
            held = jnp.where(lane >= (first & (LANES - 1)), left, right)
            a = jnp.take_along_axis(held, here, axis=1, mode="promise_in_bounds")
            b = jnp.take_along_axis(held, next_, axis=1, mode="promise_in_bounds")
            total = total + (a * (1.0 - frac) + b * frac)
        if last:
            total = (total + tv_ref[row, :, cols]) / curv_ref[row, :, cols]
        rows_ref[row, :, cols] = total
        return squares + total * total if last else squares

    steps = rows_n * (per_n // LANES)
    squares = lax.fori_loop(0, steps, step, jnp.zeros((16, LANES), jnp.float32), unroll=4)
    if last:
        for row in range(rows_n):
            out_ref[0:16, row, :] = rows_ref[row]
        out_ref[16] = jnp.full((rows_n, per_n), jnp.sum(squares), jnp.float32)


def gather_views(dims, parts_n, ints, pieces, extra=()):
    views_n, _, slices_n, _ = pieces[0].shape
    rows_n, cols_n = dims[:2]
    per_n = cols_n // parts_n
    pieces_n = len(pieces)
    last = len(extra) > 0
    rows = (rows_n, slices_n, per_n)
    shape = (slices_n + 1, rows_n, per_n) if last else rows
    vmem = pl.BlockSpec(memory_space=pltpu.VMEM)
    scratch = [
        pltpu.SMEM((2 * pieces_n * views_n,), jnp.float32),
        pltpu.SMEM((pieces_n * views_n,), jnp.int32),
    ]
    return pl.pallas_call(
        lambda *refs: gather_kernel(dims, parts_n, pieces_n, views_n, last, *refs),
        out_shape=jax.ShapeDtypeStruct(shape, jnp.float32),
        in_specs=[pl.BlockSpec(memory_space=pltpu.SMEM)] + [vmem] * (pieces_n + len(extra)),
        out_specs=vmem,
        scratch_shapes=([pltpu.VMEM(rows, jnp.float32)] if last else []) + scratch,
        name="gather_views",
    )(ints, *extra, *pieces)


def total_kernel(*refs):
    sums = [ref[0, 0:1, :] for ref in refs[:-1]]
    while len(sums) > 1:
        sums = [a + b for a, b in zip(sums[0::2], sums[1::2])]
    refs[-1][...] = sums[0]


def total(pieces):
    slices_n, rows_n, _ = pieces[0].shape
    last = pl.BlockSpec((1, rows_n, LANES), lambda i: (slices_n - 1, 0, 0))
    return pl.pallas_call(
        total_kernel,
        grid=(1,),
        out_shape=jax.ShapeDtypeStruct((1, LANES), jnp.float32),
        in_specs=[last] * len(pieces),
        out_specs=pl.BlockSpec((1, LANES), lambda i: (0, 0)),
        name="total",
    )(*pieces)


def finish_kernel(parts_n, voxel_count, ints_ref, *rest):
    sums, vol_ref, pieces = rest[:4], rest[4], rest[5 : 5 + parts_n]
    out_ref = rest[5 + parts_n]
    squares = sums[0][...] + sums[1][...] + (sums[2][...] + sums[3][...])
    rms = jnp.sqrt(squares / float(voxel_count) + epsilon)
    factor = jnp.max(jnp.minimum(1.0, step_limit / rms))
    slices_n, _, per_n = pieces[0].shape
    part = ints_ref[1]
    for r in range(parts_n):
        cols = pl.ds(pl.multiple_of((part ^ SLOTS[r]) * per_n, per_n), per_n)
        out_ref[:, :, cols] = vol_ref[:, :, cols] - factor * pieces[r][0 : slices_n - 1]


def finish(voxel_count, ints, sums, volume, pieces):
    parts_n = len(pieces)
    vmem = pl.BlockSpec(memory_space=pltpu.VMEM)
    smem = pl.BlockSpec(memory_space=pltpu.SMEM)
    return pl.pallas_call(
        lambda *refs: finish_kernel(parts_n, voxel_count, *refs),
        out_shape=jax.ShapeDtypeStruct(volume.shape, volume.dtype),
        in_specs=[smem] + [vmem] * (parts_n + 5),
        out_specs=vmem,
        name="finish",
    )(ints, *sums, volume, *pieces)


def swapped(x, axis, bit):
    return lax.ppermute(x, axis, [(i, i ^ bit) for i in range(lax.axis_size(axis))])


def gathered(piece):
    near = swapped(piece, "view", 2)
    far = [swapped(piece, "view", 4), swapped(piece, "view", 6)]
    side = [swapped(piece, "view", 1), swapped(piece, "view", 3)]
    return [piece, near] + far + side + [swapped(x, "view", 1) for x in far]


def local_split(volume, sinogram, curvature, angles, offsets):
    slices_n, rows_n, cols_n = volume.shape
    views_n = angles.shape[0]
    bins_n = sinogram.shape[2]
    base, blocks = extent(rows_n, cols_n, bins_n)
    dims = (rows_n, cols_n, bins_n, base, blocks)
    slab_count = lax.axis_size("slab")
    parts_n = lax.axis_size("view")
    slab = lax.axis_index("slab")
    part = lax.axis_index("view")
    per_n = cols_n // parts_n

    angle_rad = angles.astype(jnp.float32) * (2.0 * math.pi / ROTATION_VIEWS)
    trig = jnp.concatenate([jnp.cos(angle_rad), jnp.sin(angle_rad)])

    def outer(at):
        face = lax.dynamic_slice(volume, (at, 0, part * per_n), (1, rows_n, per_n))
        return face.reshape(1, 1, slices_n, LANES)

    measured = sinogram[:, :, base : base + blocks * LANES]
    measured = measured.reshape(views_n, slices_n, blocks, LANES).transpose(0, 2, 1, 3)
    faces = jnp.concatenate([outer(0), outer(slices_n - 1)], axis=0)
    measured = jnp.concatenate([measured, faces], axis=1)
    cross_rows = swapped(measured, "slab", 2)
    pair_rows = swapped(measured, "slab", 1)
    trig, measured = lax.optimization_barrier((trig, measured))
    proj = project(trig, volume, bins_n, base, blocks, views_n)
    cross_pair_rows = swapped(cross_rows, "slab", 1)
    cross = swapped(proj, "slab", 2)
    near = swapped(proj, "slab", 1)

    def of(k):
        return lax.dynamic_index_in_dim(offsets, k, 1, keepdims=False)

    start = of(slab)
    shifts = [slices_n + jnp.clip(start - of(slab ^ k), -slices_n, slices_n) for k in (1, 2, 3)]
    table = jnp.stack([start] + shifts, axis=1).reshape(-1)
    ints = jnp.concatenate([jnp.stack([slab, part]).astype(jnp.int32), table])
    def face_of(rows, which):
        return rows[which, blocks].reshape(1, rows_n, per_n)

    odd = slab % 2 == 1
    below = jnp.where(odd, face_of(pair_rows, 1), jnp.where(slab == 0, 0.0, face_of(cross_pair_rows, 1)))
    above = jnp.where(odd, jnp.where(slab == slab_count - 1, 0.0, face_of(cross_pair_rows, 0)), face_of(pair_rows, 0))
    wide = jnp.pad(volume, ((0, 0), (0, 0), (1, 1)))
    block = lax.dynamic_slice_in_dim(wide, part * per_n, per_n + 2, axis=2)
    sides = ((0, 0), (0, 0), (1, 1))
    block = jnp.concatenate([jnp.pad(below, sides), block, jnp.pad(above, sides)], axis=0)
    tv_grad = tv_padded(jnp.pad(block, ((0, 0), (1, 1), (0, 0))))
    curv = lax.dynamic_slice_in_dim(curvature, part * per_n, per_n, axis=2)
    tv = (tv_weight * tv_grad).transpose(1, 0, 2)
    curv = curv.transpose(1, 0, 2)
    rows = [measured, pair_rows, cross_rows, cross_pair_rows]
    local_part = near_residual(ints, [proj, near] + rows)
    local_part, cross, tv, curv = lax.optimization_barrier((local_part, cross, tv, curv))
    cross_pair = swapped(cross, "slab", 1)
    windows = residual_windows(dims, parts_n, ints, trig, [local_part, cross, cross_pair])
    pieces = [windows[0]] + [swapped(windows[r], "view", r) for r in range(1, parts_n)]
    near_grad = gather_views(dims, parts_n, ints, pieces[: parts_n // 2])
    extra = (tv, curv, near_grad)
    parts = gathered(gather_views(dims, parts_n, ints, pieces[parts_n // 2 :], extra))
    squares = total(parts)
    sums = [squares] + [swapped(squares, "slab", k) for k in (1, 2, 3)]
    voxel_count = slices_n * slab_count * rows_n * cols_n
    return finish(voxel_count, ints, sums, volume, parts)


def local(volume, sinogram, curvature, angles, offsets):
    shape = (lax.axis_size("slab"), lax.axis_size("view"), angles.shape[0])
    if shape == (4, 8, 2):
        return local_split(volume, sinogram, curvature, angles, offsets)
    return local_any(volume, sinogram, curvature, angles, offsets)


def solution(mesh):
    in_specs = (
        P("slab", None, None),
        P("view", "slab", None),
        P("slab", None, None),
        P("view"),
        P("view", None),
    )
    out_specs = P("slab", None, None)
    return jax.shard_map(local, mesh=mesh, in_specs=in_specs, out_specs=out_specs, check_vma=False)
```

```python
import math
import jax
import jax.numpy as jnp
from jax import lax
from jax.experimental import pallas as pl
from jax.experimental.pallas import tpu as pltpu
from jax.sharding import PartitionSpec as P

ROTATION_VIEWS = 1152


huber_delta = 0.5
tv_weight = 4.0
step_limit = 1.0
epsilon = 1e-06
scale = 0.7
LANES = 128
GROUP = 32


def coordinate(across, along, cos, sin, bins_n):
    return scale * (across * cos + along * sin) + 0.5 * bins_n - 0.5


def window_of(start, cos, sin, along, cols_n, bins_n, base):
    first = coordinate(start - 0.5 * cols_n + 0.5, along, cos, sin, bins_n)
    last = coordinate(start + (LANES - 1.0) - 0.5 * cols_n + 0.5, along, cos, sin, bins_n)
    return jnp.minimum(first, last).astype(jnp.int32) - (base + 1)


def project_kernel(cols_n, rows_n, bins_n, base, blocks_n, views_n, trig_ref, vol_ref, out_ref, rows_ref, acc_ref, sem):
    copies = [pltpu.make_async_copy(vol_ref.at[:, i, :], rows_ref.at[i], sem.at[i]) for i in range(rows_n)]
    for c in copies:
        c.start()
    acc_ref[...] = jnp.zeros_like(acc_ref)
    lane8 = lax.broadcasted_iota(jnp.int32, (8, LANES), 1)
    lane = lax.broadcasted_iota(jnp.int32, (16, LANES), 1)
    sub = lax.broadcasted_iota(jnp.int32, (LANES, LANES), 0).astype(jnp.float32).astype(jnp.bfloat16)
    zero = jnp.zeros((LANES, LANES), jnp.bfloat16)

    def tall(x):
        return jnp.concatenate([jnp.concatenate([x, x], 0).astype(jnp.bfloat16)] * (LANES // 16), 0)

    for row in range(rows_n):
        copies[row].wait()
        along = row - 0.5 * rows_n + 0.5

        def step(g, _):
            outs = []
            for u in range(GROUP):
                block = g * GROUP + u
                start = (block * LANES).astype(jnp.float32)
                vals = rows_ref[row, :, pl.ds(pl.multiple_of(block * LANES, LANES), LANES)]
                high = vals.astype(jnp.bfloat16)
                rest = vals - high.astype(jnp.float32)
                mid = rest.astype(jnp.bfloat16)
                low = (rest - mid.astype(jnp.float32)).astype(jnp.bfloat16)
                terms = jnp.concatenate([high, mid, low], 0)
                mats = []
                wins = []
                for v in range(views_n):
                    cos = trig_ref[v]
                    sin = trig_ref[views_n + v]
                    across = (lane8 + block * LANES).astype(jnp.float32) - 0.5 * cols_n + 0.5
                    coord = coordinate(across, along, cos, sin, bins_n)
                    lower = jnp.floor(coord)
                    frac = coord - lower
                    rel = lower - float(base)
                    bm = rel - LANES * jnp.floor(rel * (1.0 / LANES))
                    bn = jnp.where(bm == LANES - 1.0, 0.0, bm + 1.0)
                    fh = jnp.floor(frac * 128.0) * (1.0 / 128.0)
                    fl = frac - fh
                    here = sub == tall(bm)
                    next_ = sub == tall(bn)
                    wh = jnp.where(here, tall(1.0 - fh), jnp.where(next_, tall(fh), zero))
                    wl = jnp.where(here, tall(-fl), jnp.where(next_, tall(fl), zero))
                    mats.append(jnp.concatenate([wh, wl], 1))
                    wins.append(window_of(start, cos, sin, along, cols_n, bins_n, base))
                weights = jnp.concatenate(mats, 0)
                both = jnp.concatenate([terms, terms], 1)
                prod = lax.dot_general(both, weights, (((1,), (1,)), ((), ())), preferred_element_type=jnp.float32)
                outs.append((prod[0:16] + prod[16:32] + prod[32:48], wins))
            for summed, wins in outs:
                for v in range(views_n):
                    first = wins[v]
                    k = first >> 7
                    own = lane >= (first & (LANES - 1))
                    part = summed[:, v * LANES:(v + 1) * LANES]
                    acc_ref[v, k] += jnp.where(own, part, 0.0)
                    acc_ref[v, k + 1] += jnp.where(own, 0.0, part)
            return 0

        lax.fori_loop(0, cols_n // LANES // GROUP, step, 0)
    out_ref[...] = acc_ref[:, :blocks_n]


def project(trig, volume, bins_n, base, blocks_n, views_n):
    slices_n, rows_n, cols_n = volume.shape
    body = lambda *refs: project_kernel(cols_n, rows_n, bins_n, base, blocks_n, views_n, *refs)
    return pl.pallas_call(
        body,
        out_shape=jax.ShapeDtypeStruct((views_n, blocks_n, slices_n, LANES), jnp.float32),
        in_specs=[pl.BlockSpec(memory_space=pltpu.SMEM), pl.BlockSpec(memory_space=pl.ANY)],
        out_specs=pl.BlockSpec(memory_space=pltpu.VMEM),
        scratch_shapes=[
            pltpu.VMEM((rows_n, slices_n, cols_n), jnp.float32),
            pltpu.VMEM((views_n, blocks_n + 1, slices_n, LANES), jnp.float32),
            pltpu.SemaphoreType.DMA((rows_n,)),
        ],
        name="project",
    )(trig, volume)


def backproject_kernel(cols_n, rows_n, bins_n, base, views_n, width, per_n, trig_ref, starts_ref, res_ref, out_ref):
    lane16 = lax.broadcasted_iota(jnp.int32, (16, LANES), 1)
    pixel0 = starts_ref[views_n]

    def row_step(row, _):
        along = row.astype(jnp.float32) - 0.5 * rows_n + 0.5

        def step(u, _):
            column = pixel0 + u * LANES
            start = column.astype(jnp.float32)
            across = (lane16 + column).astype(jnp.float32) - 0.5 * cols_n + 0.5
            total = jnp.zeros((16, LANES), jnp.float32)
            for v in range(views_n):
                cos = trig_ref[v]
                sin = trig_ref[views_n + v]
                coord = coordinate(across, along, cos, sin, bins_n)
                lower = jnp.floor(coord)
                frac = coord - lower
                offset = starts_ref[v]
                rel = lower.astype(jnp.int32) - (base + offset)
                here = rel & (LANES - 1)
                next_ = (rel + 1) & (LANES - 1)
                first = window_of(start, cos, sin, along, cols_n, bins_n, base) - offset
                k = first >> 7
                left = res_ref[v, k]
                right = res_ref[v, jnp.minimum(k + 1, width - 1)]
                band = jnp.where(lane16 >= (first & (LANES - 1)), left, right)
                a = jnp.take_along_axis(band, here, axis=1, mode="promise_in_bounds")
                b = jnp.take_along_axis(band, next_, axis=1, mode="promise_in_bounds")
                total = total + (a * (1.0 - frac) + b * frac)
            out_ref[row, :, pl.ds(pl.multiple_of(u * LANES, LANES), LANES)] = total
            return 0

        lax.fori_loop(0, per_n // LANES, step, 0)
        return 0

    lax.fori_loop(0, rows_n, row_step, 0)


def backproject(trig, starts, res, rows_n, cols_n, bins_n, base, per_n):
    views_n, width, slices_n, _ = res.shape
    body = lambda *refs: backproject_kernel(cols_n, rows_n, bins_n, base, views_n, width, per_n, *refs)
    return pl.pallas_call(
        body,
        out_shape=jax.ShapeDtypeStruct((rows_n, slices_n, per_n), jnp.float32),
        in_specs=[pl.BlockSpec(memory_space=pltpu.SMEM), pl.BlockSpec(memory_space=pltpu.SMEM), pl.BlockSpec(memory_space=pltpu.VMEM)],
        out_specs=pl.BlockSpec(memory_space=pltpu.VMEM),
        name="backproject",
    )(trig, starts, res)


def padded_2(cells, sides, width):
    for axis, dim in sides:
        count = lax.axis_size(axis)
        ends = count - 1
        head = lax.slice_in_dim(cells, 0, width, axis=dim)
        tail = lax.slice_in_dim(cells, cells.shape[dim] - width, cells.shape[dim], axis=dim)
        cells = jnp.concatenate(
            [
                lax.ppermute(tail, axis, [(i, (i + 1) % count) for i in range(ends)]),
                cells,
                lax.ppermute(head, axis, [((i + 1) % count, i) for i in range(ends)]),
            ],
            axis=dim,
        )
    return cells


def slope(diff):
    return jnp.clip(diff / huber_delta, -1.0, 1.0)


def tv_padded(padded):
    centre = padded[1:-1, 1:-1, 1:-1]
    result = slope(centre - padded[:-2, 1:-1, 1:-1]) - slope(padded[2:, 1:-1, 1:-1] - centre)
    result = (
        result + slope(centre - padded[1:-1, :-2, 1:-1]) - slope(padded[1:-1, 2:, 1:-1] - centre)
    )
    result = (
        result + slope(centre - padded[1:-1, 1:-1, :-2]) - slope(padded[1:-1, 1:-1, 2:] - centre)
    )
    return result


def extent(rows_n, cols_n, bins_n):
    reach = scale * math.hypot(0.5 * (cols_n - 1), 0.5 * (rows_n - 1))
    centre = 0.5 * bins_n - 0.5
    base = (int(centre - reach) - 3) // 8 * 8
    blocks = -(-(int(centre + reach) + 3 - base) // LANES)
    return base, blocks


def local_any(volume, sinogram, curvature, angles, offsets):
    slices_n, rows_n, cols_n = volume.shape
    views_n = angles.shape[0]
    bins_n = sinogram.shape[2]
    base, blocks = extent(rows_n, cols_n, bins_n)
    pixels_n = rows_n * cols_n
    slab_count = lax.axis_size("slab")
    all_rows = sinogram.shape[1] * slab_count
    slab_pos = lax.axis_index("slab")
    angle_rad = angles.astype(jnp.float32) * (2.0 * math.pi / ROTATION_VIEWS)
    trig = jnp.concatenate([jnp.cos(angle_rad), jnp.sin(angle_rad)])
    proj = project(trig, volume, bins_n, base, blocks, views_n)
    stacked = []
    bands = []
    for v in range(views_n):
        start = lax.dynamic_index_in_dim(offsets[v], slab_pos, 0, keepdims=False)
        flat = proj[v].transpose(1, 0, 2).reshape(slices_n, blocks * LANES)
        stacked.append(
            lax.dynamic_update_slice(
                jnp.zeros((all_rows, blocks * LANES), jnp.float32), flat, (start, jnp.int32(0))
            )
        )
        bands.append(start)
    own = lax.psum_scatter(jnp.stack(stacked), "slab", scatter_dimension=1, tiled=True)
    measured = sinogram[:, :, base : base + blocks * LANES]
    residual = lax.all_gather(own - measured, "slab", axis=1, tiled=True)
    windows = jnp.stack(
        [
            lax.dynamic_slice(
                residual[v], (bands[v], jnp.int32(0)), (slices_n, blocks * LANES)
            )
            .reshape(slices_n, blocks, LANES)
            .transpose(1, 0, 2)
            for v in range(views_n)
        ]
    )
    starts = jnp.zeros((views_n + 1,), jnp.int32)
    data_local = backproject(trig, starts, windows, rows_n, cols_n, bins_n, base, cols_n)
    extended = padded_2(volume, (("slab", 0),), 1)
    padded = jnp.pad(extended, ((0, 0), (1, 1), (1, 1)))
    tv_grad = tv_padded(padded)
    data_grad = lax.psum(data_local, "view").transpose(1, 0, 2)
    direction = (data_grad + tv_weight * tv_grad) / curvature
    squares = lax.psum(jnp.sum(direction * direction), "slab")
    voxel_count = slices_n * slab_count * pixels_n
    factor = jnp.minimum(1.0, step_limit / jnp.sqrt(squares / voxel_count + epsilon))
    return volume - factor * direction


WINDOW = 3
SLOTS = (0, 2, 4, 6, 1, 3, 5, 7)
COS_LANE = LANES - 2
SIN_LANE = LANES - 1


def window_start(part, per_n, cos, sin, rows_n, cols_n, bins_n, base, blocks):
    low = None
    for row in (0, rows_n - 1):
        along = row - 0.5 * rows_n + 0.5
        for edge in (0.0, per_n - 1.0):
            across = (part * per_n).astype(jnp.float32) + edge - 0.5 * cols_n + 0.5
            t = coordinate(across, along, cos, sin, bins_n)
            low = t if low is None else jnp.minimum(low, t)
    first = low.astype(jnp.int32) - (base + 1)
    return jnp.clip(first, 0, (blocks - WINDOW) * LANES)


def fill_pad(pad, value):
    views_n, blocks, band, _ = value.shape
    edge = jnp.zeros((views_n, blocks, band, LANES), jnp.float32)
    pad[:, :, 0:band] = edge
    pad[:, :, 2 * band :] = edge
    pad[:, :, band : 2 * band] = value[...]


def near_kernel(ints_ref, proj_ref, near_ref, *rest):
    sinos, out_ref, pad, sino = rest[:4], rest[4], rest[5], rest[6]
    views_n, blocks, band, _ = proj_ref.shape
    slab = ints_ref[0]
    fill_pad(pad, near_ref)
    for other in range(4):
        rows = pl.ds(pl.multiple_of((slab ^ other) * band, band), band)
        sino[:, :, rows] = sinos[other][:, 0:blocks]
    for v in range(views_n):
        value = proj_ref[v] + pad[v, :, pl.ds(ints_ref[3 + 4 * v], band), :]
        out_ref[v] = value - sino[v, :, pl.ds(ints_ref[2 + 4 * v], band), :]


def near_residual(ints, arrays):
    views_n, blocks, band, _ = arrays[0].shape
    vmem = pl.BlockSpec(memory_space=pltpu.VMEM)
    return pl.pallas_call(
        near_kernel,
        out_shape=jax.ShapeDtypeStruct(arrays[0].shape, jnp.float32),
        in_specs=[pl.BlockSpec(memory_space=pltpu.SMEM)] + [vmem] * len(arrays),
        out_specs=vmem,
        scratch_shapes=[
            pltpu.VMEM((views_n, blocks, 3 * band, LANES), jnp.float32),
            pltpu.VMEM((views_n, blocks, 4 * band, LANES), jnp.float32),
        ],
        name="near_residual",
    )(ints, *arrays)


def residual_kernel(dims, parts_n, ints_ref, trig_ref, base_ref, cross_ref, cross_pair_ref, *rest):
    rows_n, cols_n, bins_n, base, blocks = dims
    outs = rest[:parts_n]
    cross_pad, cross_pair_pad, res = rest[parts_n:]
    views_n, _, band, _ = base_ref.shape
    part = ints_ref[1]
    fill_pad(cross_pad, cross_ref)
    fill_pad(cross_pair_pad, cross_pair_ref)
    for v in range(views_n):
        value = base_ref[v] + cross_pad[v, :, pl.ds(ints_ref[4 + 4 * v], band), :]
        res[v, 0:blocks] = value + cross_pair_pad[v, :, pl.ds(ints_ref[5 + 4 * v], band), :]
        res[v, blocks] = jnp.zeros((band, LANES), jnp.float32)
    lane = lax.broadcasted_iota(jnp.int32, (band, LANES), 1)
    per_n = cols_n // parts_n
    for r in range(parts_n):
        for v in range(views_n):
            cos, sin = trig_ref[v], trig_ref[views_n + v]
            first = window_start(part ^ r, per_n, cos, sin, rows_n, cols_n, bins_n, base, blocks)
            k = first >> 7
            shift = first & (LANES - 1)
            turned = [pltpu.roll(res[v, k + m], (LANES - shift) & (LANES - 1), 1) for m in range(WINDOW + 1)]
            for m in range(WINDOW):
                value = jnp.where(lane < LANES - shift, turned[m], turned[m + 1])
                if m == WINDOW - 1:
                    value = jnp.where(lane == COS_LANE, cos, jnp.where(lane == SIN_LANE, sin, value))
                outs[r][v, m] = value


def residual_windows(dims, parts_n, ints, trig, arrays):
    views_n, blocks, band, _ = arrays[0].shape
    body = lambda *refs: residual_kernel(dims, parts_n, *refs)
    vmem = pl.BlockSpec(memory_space=pltpu.VMEM)
    smem = pl.BlockSpec(memory_space=pltpu.SMEM)
    return pl.pallas_call(
        body,
        out_shape=[jax.ShapeDtypeStruct((views_n, WINDOW, band, LANES), jnp.float32)] * parts_n,
        in_specs=[smem, smem] + [vmem] * len(arrays),
        out_specs=[vmem] * parts_n,
        scratch_shapes=[
            pltpu.VMEM((views_n, blocks, 3 * band, LANES), jnp.float32),
            pltpu.VMEM((views_n, blocks, 3 * band, LANES), jnp.float32),
            pltpu.VMEM((views_n, blocks + 1, band, LANES), jnp.float32),
        ],
        name="residual_windows",
    )(ints, trig, *arrays)


def gather_kernel(dims, parts_n, pieces_n, views_n, last, ints_ref, *rest):
    rows_n, cols_n, bins_n, base, blocks = dims
    if last:
        tv_ref, curv_ref, near_ref, *rest = rest
    pieces = rest[:pieces_n]
    if last:
        out_ref, rows_ref, trig_ref, starts_ref = rest[pieces_n:]
    else:
        rows_ref, trig_ref, starts_ref = rest[pieces_n:]
    per_n = cols_n // parts_n
    part = ints_ref[1]
    lane8 = lax.broadcasted_iota(jnp.int32, (8, LANES), 1)
    lane = lax.broadcasted_iota(jnp.int32, (16, LANES), 1)
    total_n = pieces_n * views_n
    for n in range(total_n):
        tagged = pieces[n // views_n][n % views_n, WINDOW - 1, 0:8, :]
        cos = jnp.max(jnp.where(lane8 == COS_LANE, tagged, -2.0))
        sin = jnp.max(jnp.where(lane8 == SIN_LANE, tagged, -2.0))
        trig_ref[n] = cos
        trig_ref[total_n + n] = sin
        starts_ref[n] = window_start(part, per_n, cos, sin, rows_n, cols_n, bins_n, base, blocks)

    def step(index, squares):
        row = index // (per_n // LANES)
        u = index - row * (per_n // LANES)
        along = row.astype(jnp.float32) - 0.5 * rows_n + 0.5
        column = part * per_n + u * LANES
        start = column.astype(jnp.float32)
        across = (lane + column).astype(jnp.float32) - 0.5 * cols_n + 0.5
        cols = pl.ds(pl.multiple_of(u * LANES, LANES), LANES)
        total = near_ref[row, :, cols] if last else jnp.zeros((16, LANES), jnp.float32)
        for n in range(total_n):
            cos = trig_ref[n]
            sin = trig_ref[total_n + n]
            offset = starts_ref[n]
            coord = coordinate(across, along, cos, sin, bins_n)
            lower = jnp.floor(coord)
            frac = coord - lower
            rel = lower.astype(jnp.int32) - (base + offset)
            here = rel & (LANES - 1)
            next_ = (rel + 1) & (LANES - 1)
            first = jnp.maximum(window_of(start, cos, sin, along, cols_n, bins_n, base) - offset, 0)
            k = jnp.minimum(first >> 7, WINDOW - 1)
            windows = pieces[n // views_n]
            left = windows[n % views_n, k]
            right = windows[n % views_n, jnp.minimum(k + 1, WINDOW - 1)]
            held = jnp.where(lane >= (first & (LANES - 1)), left, right)
            a = jnp.take_along_axis(held, here, axis=1, mode="promise_in_bounds")
            b = jnp.take_along_axis(held, next_, axis=1, mode="promise_in_bounds")
            total = total + (a * (1.0 - frac) + b * frac)
        if last:
            total = (total + tv_ref[row, :, cols]) / curv_ref[row, :, cols]
        rows_ref[row, :, cols] = total
        return squares + total * total if last else squares

    steps = rows_n * (per_n // LANES)
    squares = lax.fori_loop(0, steps, step, jnp.zeros((16, LANES), jnp.float32), unroll=4)
    if last:
        for row in range(rows_n):
            out_ref[0:16, row, :] = rows_ref[row]
        out_ref[16] = jnp.full((rows_n, per_n), jnp.sum(squares), jnp.float32)


def gather_views(dims, parts_n, ints, pieces, extra=()):
    views_n, _, slices_n, _ = pieces[0].shape
    rows_n, cols_n = dims[:2]
    per_n = cols_n // parts_n
    pieces_n = len(pieces)
    last = len(extra) > 0
    rows = (rows_n, slices_n, per_n)
    shape = (slices_n + 1, rows_n, per_n) if last else rows
    vmem = pl.BlockSpec(memory_space=pltpu.VMEM)
    scratch = [
        pltpu.SMEM((2 * pieces_n * views_n,), jnp.float32),
        pltpu.SMEM((pieces_n * views_n,), jnp.int32),
    ]
    return pl.pallas_call(
        lambda *refs: gather_kernel(dims, parts_n, pieces_n, views_n, last, *refs),
        out_shape=jax.ShapeDtypeStruct(shape, jnp.float32),
        in_specs=[pl.BlockSpec(memory_space=pltpu.SMEM)] + [vmem] * (pieces_n + len(extra)),
        out_specs=vmem,
        scratch_shapes=([pltpu.VMEM(rows, jnp.float32)] if last else []) + scratch,
        name="gather_views",
    )(ints, *extra, *pieces)


def total_kernel(*refs):
    sums = [ref[0, 0:1, :] for ref in refs[:-1]]
    while len(sums) > 1:
        sums = [a + b for a, b in zip(sums[0::2], sums[1::2])]
    refs[-1][...] = sums[0]


def total(pieces):
    slices_n, rows_n, _ = pieces[0].shape
    last = pl.BlockSpec((1, rows_n, LANES), lambda i: (slices_n - 1, 0, 0))
    return pl.pallas_call(
        total_kernel,
        grid=(1,),
        out_shape=jax.ShapeDtypeStruct((1, LANES), jnp.float32),
        in_specs=[last] * len(pieces),
        out_specs=pl.BlockSpec((1, LANES), lambda i: (0, 0)),
        name="total",
    )(*pieces)


def finish_kernel(parts_n, voxel_count, ints_ref, *rest):
    sums, vol_ref, pieces = rest[:4], rest[4], rest[5 : 5 + parts_n]
    out_ref = rest[5 + parts_n]
    squares = sums[0][...] + sums[1][...] + (sums[2][...] + sums[3][...])
    rms = jnp.sqrt(squares / float(voxel_count) + epsilon)
    factor = jnp.max(jnp.minimum(1.0, step_limit / rms))
    per_n = pieces[0].shape[2]
    part = ints_ref[1]
    for r in range(parts_n):
        cols = pl.ds(pl.multiple_of((part ^ SLOTS[r]) * per_n, per_n), per_n)
        out_ref[:, :, cols] = vol_ref[:, :, cols] - factor * pieces[r][...]


def finish(voxel_count, ints, sums, volume, pieces):
    parts_n = len(pieces)
    slices_n, rows_n, cols_n = volume.shape
    step = slices_n // 4
    line = pl.BlockSpec((1, LANES), lambda i: (0, 0))
    wide = pl.BlockSpec((step, rows_n, cols_n), lambda i: (i, 0, 0))
    piece = pl.BlockSpec((step, rows_n, cols_n // parts_n), lambda i: (i, 0, 0))
    return pl.pallas_call(
        lambda *refs: finish_kernel(parts_n, voxel_count, *refs),
        grid=(slices_n // step,),
        out_shape=jax.ShapeDtypeStruct(volume.shape, volume.dtype),
        in_specs=[pl.BlockSpec(memory_space=pltpu.SMEM)] + [line] * 4 + [wide] + [piece] * parts_n,
        out_specs=wide,
        name="finish",
    )(ints, *sums, volume, *pieces)


def swapped(x, axis, bit):
    return lax.ppermute(x, axis, [(i, i ^ bit) for i in range(lax.axis_size(axis))])


def gathered(piece):
    near = swapped(piece, "view", 2)
    far = [swapped(piece, "view", 4), swapped(piece, "view", 6)]
    side = [swapped(piece, "view", 1), swapped(piece, "view", 3)]
    return [piece, near] + far + side + [swapped(x, "view", 1) for x in far]


def local_split(volume, sinogram, curvature, angles, offsets):
    slices_n, rows_n, cols_n = volume.shape
    views_n = angles.shape[0]
    bins_n = sinogram.shape[2]
    base, blocks = extent(rows_n, cols_n, bins_n)
    dims = (rows_n, cols_n, bins_n, base, blocks)
    slab_count = lax.axis_size("slab")
    parts_n = lax.axis_size("view")
    slab = lax.axis_index("slab")
    part = lax.axis_index("view")
    per_n = cols_n // parts_n

    angle_rad = angles.astype(jnp.float32) * (2.0 * math.pi / ROTATION_VIEWS)
    trig = jnp.concatenate([jnp.cos(angle_rad), jnp.sin(angle_rad)])

    def outer(at):
        face = lax.dynamic_slice(volume, (at, 0, part * per_n), (1, rows_n, per_n))
        return face.reshape(1, 1, slices_n, LANES)

    measured = sinogram[:, :, base : base + blocks * LANES]
    measured = measured.reshape(views_n, slices_n, blocks, LANES).transpose(0, 2, 1, 3)
    faces = jnp.concatenate([outer(0), outer(slices_n - 1)], axis=0)
    measured = jnp.concatenate([measured, faces], axis=1)
    cross_rows = swapped(measured, "slab", 2)
    pair_rows = swapped(measured, "slab", 1)
    trig, measured = lax.optimization_barrier((trig, measured))
    proj = project(trig, volume, bins_n, base, blocks, views_n)
    cross_pair_rows = swapped(cross_rows, "slab", 1)
    cross = swapped(proj, "slab", 2)
    near = swapped(proj, "slab", 1)

    def of(k):
        return lax.dynamic_index_in_dim(offsets, k, 1, keepdims=False)

    start = of(slab)
    shifts = [slices_n + jnp.clip(start - of(slab ^ k), -slices_n, slices_n) for k in (1, 2, 3)]
    table = jnp.stack([start] + shifts, axis=1).reshape(-1)
    ints = jnp.concatenate([jnp.stack([slab, part]).astype(jnp.int32), table])
    def face_of(rows, which):
        return rows[which, blocks].reshape(1, rows_n, per_n)

    odd = slab % 2 == 1
    below = jnp.where(odd, face_of(pair_rows, 1), jnp.where(slab == 0, 0.0, face_of(cross_pair_rows, 1)))
    above = jnp.where(odd, jnp.where(slab == slab_count - 1, 0.0, face_of(cross_pair_rows, 0)), face_of(pair_rows, 0))
    wide = jnp.pad(volume, ((0, 0), (0, 0), (1, 1)))
    block = lax.dynamic_slice_in_dim(wide, part * per_n, per_n + 2, axis=2)
    sides = ((0, 0), (0, 0), (1, 1))
    block = jnp.concatenate([jnp.pad(below, sides), block, jnp.pad(above, sides)], axis=0)
    tv_grad = tv_padded(jnp.pad(block, ((0, 0), (1, 1), (0, 0))))
    curv = lax.dynamic_slice_in_dim(curvature, part * per_n, per_n, axis=2)
    tv = (tv_weight * tv_grad).transpose(1, 0, 2)
    curv = curv.transpose(1, 0, 2)
    rows = [measured, pair_rows, cross_rows, cross_pair_rows]
    local_part = near_residual(ints, [proj, near] + rows)
    local_part, cross, tv, curv = lax.optimization_barrier((local_part, cross, tv, curv))
    cross_pair = swapped(cross, "slab", 1)
    windows = residual_windows(dims, parts_n, ints, trig, [local_part, cross, cross_pair])
    pieces = [windows[0]] + [swapped(windows[r], "view", r) for r in range(1, parts_n)]
    near_grad = gather_views(dims, parts_n, ints, pieces[: parts_n // 2])
    extra = (tv, curv, near_grad)
    parts = gathered(gather_views(dims, parts_n, ints, pieces[parts_n // 2 :], extra))
    squares = total(parts)
    sums = [squares] + [swapped(squares, "slab", k) for k in (1, 2, 3)]
    voxel_count = slices_n * slab_count * rows_n * cols_n
    return finish(voxel_count, ints, sums, volume, parts)


def local(volume, sinogram, curvature, angles, offsets):
    shape = (lax.axis_size("slab"), lax.axis_size("view"), angles.shape[0])
    if shape == (4, 8, 2):
        return local_split(volume, sinogram, curvature, angles, offsets)
    return local_any(volume, sinogram, curvature, angles, offsets)


def solution(mesh):
    in_specs = (
        P("slab", None, None),
        P("view", "slab", None),
        P("slab", None, None),
        P("view"),
        P("view", None),
    )
    out_specs = P("slab", None, None)
    return jax.shard_map(local, mesh=mesh, in_specs=in_specs, out_specs=out_specs, check_vma=False)
```
